32 devices in a mesh: groups: 2 (over x), node: 16 (over z, y, core).
Axes of the slice: x: 2, y: 2, z: 4, core: 2. Of those that a mesh axis runs over, the one named last changes fastest.
Arguments:
- unit_costs: bfloat16 [1024, 24, 2048], P(('groups', 'node')), parts along dimension 0, may hold values from -15 to 15
- hour_duals: bfloat16 [1024, 24, 2048], P(('groups', 'node')), parts along dimension 0, may hold values from -3 to 3
- inverse: bfloat16 [2048, 2048], replicated, may hold values from -0.5 to 1.5, as said below
- weights: int32 [1024], P(('groups', 'node')), parts along dimension 0, may hold values from 1 to 120
- section_three: int32 [1024], P(('groups', 'node')), parts along dimension 0, may hold values from 0 to 63, as said below
- prev_first: bfloat16 [16, 2048], P('groups'), parts along dimension 0, may hold values from -6 to 6
- prev_second: bfloat16 [32, 8, 512], P(('groups', 'node')), parts along dimension 0, may hold values from -6 to 6
- prev_third: bfloat16 [128, 8, 2048], P(('groups', 'node')), parts along dimension 0, may hold values from -6 to 6
- eta_mean: float32 [2], P('groups'), parts along dimension 0, may hold values from -2 to -1
- eta_duals: float32 [1024], P(('groups', 'node')), parts along dimension 0, may hold values from -1.2 to 1.2
Outputs:
- duals_new: bfloat16 [1024, 24, 2048], P(('groups', 'node')), parts along dimension 0
- first_avg: float32 [16, 2048], P('groups'), parts along dimension 0
- second_avg: float32 [32, 8, 512], P(('groups', 'node')), parts along dimension 0
- third_avg: float32 [128, 8, 2048], P(('groups', 'node')), parts along dimension 0
- eta_avg: float32 [2], P('groups'), parts along dimension 0
- eta_duals_new: float32 [1024], P(('groups', 'node')), parts along dimension 0
The draws below stay inside these ranges and needn't reach their ends.
There are 2 independent parts, one for each index of `groups`. The reference program is written for one: setup_inputs(seed, part) draws one part's arguments, and reference() takes and returns one part's arrays. A program takes and returns all parts, laid end to end along the dimension named above; an argument that names none is the same for every part. Nothing has to cross between parts.
Inputs may be any that keep to these rules, and one draw needn't show every extreme that they name: `inverse`: A fixed matrix of order 2048. `section_three`: scenario s lies below section-2 node n = s // 128: its section-3 node is n * 16 + b with b from 0 to 15; every section-3 node holds exactly 8 scenarios.
All inputs are finite; a program needn't handle non-finite values.
Results may differ from the reference program's by a relative error of at most 0.0082.
Values may be sent and summed in bfloat16 or wider, within the bound.
No kernel may reach another device: no remote copies, remote signals or barrier semaphores. Data moves between devices by JAX's collectives and lax.ppermute only.
A program may use at most 128 MiB of HBM per device.

```python
import math
import jax
import jax.numpy as jnp

GEN = 2048
HS = 8
BRANCH = 16
SC_DEV = 32
HOURS = 24
SCEN = 512
N2 = 4
N3 = 64


def draw_unit_costs(key, part):
    key_level, key_base, key_noise = jax.random.split(key, 3)
    node_level = jnp.exp(jax.random.uniform(key_level, (N2, 1, 1), jnp.float32, math.log(0.5), math.log(2.0)))
    scen_level = jnp.repeat(node_level, 4 * SC_DEV, axis=0)
    base_cost = 1.0 + 0.8 * jnp.clip(jax.random.normal(key_base, (1, HOURS, GEN), jnp.float32), -3.0, 3.0)
    noise = 0.7 * jnp.clip(jax.random.normal(key_noise, (SCEN, HOURS, GEN), jnp.float32), -3.0, 3.0)
    return (scen_level * (base_cost + noise)).astype(jnp.bfloat16)


def draw_inverse(key, part):
    key_diag, key_off = jax.random.split(key, 2)
    diag_vals = jnp.exp(jax.random.uniform(key_diag, (GEN,), jnp.float32, math.log(0.4), math.log(1.2)))
    raw_noise = jnp.clip(jax.random.normal(key_off, (GEN, GEN), jnp.float32), -6.0, 6.0)
    off_part = (raw_noise + raw_noise.T) * (0.18 / math.sqrt(2.0 * GEN))
    coupled = jnp.full((GEN, GEN), 0.25 / GEN, jnp.float32)
    return (off_part + coupled + jnp.diag(diag_vals)).astype(jnp.bfloat16)


def draw_weights(key, part):
    base_part = jax.random.randint(key, (SCEN,), 1, 41, dtype=jnp.int32)
    rise_part = jnp.arange(SCEN, dtype=jnp.int32) * 80 // SCEN
    return (base_part + rise_part).astype(jnp.int32)


def draw_section_three(key, part):
    key_list = jax.random.split(key, N2)
    shuffles = jax.vmap(lambda one_key: jax.random.permutation(one_key, 4 * SC_DEV))(key_list)
    node_base = jnp.arange(N2, dtype=jnp.int32)[:, None] * BRANCH
    return (node_base + shuffles.astype(jnp.int32) % BRANCH).reshape(SCEN).astype(jnp.int32)


def block_levels(own_key, extent, cuts, smallest, high):
    def one(dim, parts):
        steps = jax.random.uniform(jax.random.fold_in(jax.random.fold_in(own_key, 6), dim), (parts,), jnp.float32, smallest / len(cuts), high / len(cuts))
        return jnp.repeat(jnp.exp(steps), extent[dim] // parts).reshape((-1,) + (1,) * (len(extent) - dim - 1))

    gain = one(*cuts[0])
    for cut in cuts[1:]:
        gain = gain * one(*cut)
    return gain


def normal_values(stream_key, dims, scale, most, cuts=(), kind=jnp.bfloat16):
    level = block_levels(stream_key, dims, cuts, -0.22, 0.18) if cuts else 1.0
    values = jax.random.normal(stream_key, dims, jnp.float32) * scale * level
    return jnp.minimum(jnp.maximum(values, -most), most).astype(kind)


def setup_inputs(seed: int = 0, part: int = 0) -> dict:
    keys = jax.random.split(jax.random.key(seed), 11)
    part_splits = jax.random.split(jax.random.fold_in(keys[10], part), 11)
    unit_costs = draw_unit_costs(jax.random.fold_in(jax.random.fold_in(keys[10], part), 71), part)
    hour_duals = normal_values(part_splits[1], (SCEN, HOURS, GEN), 0.5, 3.0, ((0, 16),))
    inverse = draw_inverse(jax.random.fold_in(keys[10], 71), part)
    weights = draw_weights(jax.random.fold_in(jax.random.fold_in(keys[10], part), 71), part)
    section_three = draw_section_three(jax.random.fold_in(jax.random.fold_in(keys[10], part), 71), part)
    prev_first = normal_values(part_splits[5], (HS, GEN), 1.0, 6.0)
    prev_second = normal_values(part_splits[6], (4 * N2, HS, GEN // 4), 1.0, 6.0, ((0, 16),))
    prev_third = normal_values(part_splits[7], (N3, HS, GEN), 1.0, 6.0, ((0, 16),))
    eta_mean = jnp.clip(jax.random.uniform(part_splits[8], (1,), jnp.float32, -2.0, -1.0), -2.0, -1.0)
    eta_duals = normal_values(part_splits[9], (SCEN,), 0.3, 1.2, ((0, 16),), jnp.float32)
    return dict(unit_costs=unit_costs, hour_duals=hour_duals, inverse=inverse, weights=weights, section_three=section_three, prev_first=prev_first, prev_second=prev_second, prev_third=prev_third, eta_mean=eta_mean, eta_duals=eta_duals)


PENALTY = 1.0
CVAR_WEIGHT = 0.25
CVAR_LEVEL = 0.75


def reference(unit_costs, hour_duals, inverse, weights, section_three, prev_first, prev_second, prev_third, eta_mean, eta_duals):
    scenarios = unit_costs.shape[0]
    block_len = 4 * SC_DEV
    section_two = jnp.arange(scenarios, dtype=jnp.int32) // block_len
    second_table = prev_second.reshape(N2, 4, HS, GEN // 4).transpose(0, 2, 1, 3).reshape(N2, HS, GEN)
    anchor = jnp.concatenate((
        jnp.broadcast_to(prev_first.astype(jnp.float32)[None], (scenarios, HS, GEN)),
        second_table.astype(jnp.float32)[section_two],
        prev_third.astype(jnp.float32)[section_three]), axis=1)
    target = (PENALTY * anchor - unit_costs.astype(jnp.float32) - hour_duals.astype(jnp.float32)).astype(jnp.bfloat16)
    solution = jnp.dot(target.reshape(scenarios * HOURS, GEN), inverse, preferred_element_type=jnp.float32).reshape(scenarios, HOURS, GEN)
    mass_vec = weights.astype(jnp.float32)
    mass_sum = jnp.sum(mass_vec)
    weighted = mass_vec[:, None, None] * solution
    first_avg = jnp.sum(weighted[:, :HS], axis=0) / mass_sum
    second_mass = jnp.sum(mass_vec.reshape(N2, block_len), axis=1)
    second_full = jnp.sum(weighted[:, HS:2 * HS].reshape(N2, block_len, HS, GEN), axis=1) / second_mass[:, None, None]
    third_mass = jax.ops.segment_sum(mass_vec, section_three, num_segments=N3)
    third_avg = jax.ops.segment_sum(weighted[:, 2 * HS:], section_three, num_segments=N3) / third_mass[:, None, None]
    new_anchor = jnp.concatenate((
        jnp.broadcast_to(first_avg[None], (scenarios, HS, GEN)),
        second_full[section_two],
        third_avg[section_three]), axis=1)
    duals_new = (hour_duals.astype(jnp.float32) + PENALTY * (solution - new_anchor)).astype(jnp.bfloat16)
    scen_cost = jnp.sum(unit_costs.astype(jnp.float32) * solution, axis=(1, 2)) / (HOURS * GEN)
    low_end = eta_mean[0] - (CVAR_WEIGHT + eta_duals) / PENALTY
    high_end = low_end + CVAR_WEIGHT / ((1.0 - CVAR_LEVEL) * PENALTY)
    eta_value = jnp.minimum(jnp.maximum(scen_cost, low_end), high_end)
    eta_level = jnp.sum(mass_vec * eta_value) / mass_sum
    eta_duals_new = eta_duals + PENALTY * (eta_value - eta_level)
    second_avg = second_full.reshape(N2, HS, 4, GEN // 4).transpose(0, 2, 1, 3).reshape(4 * N2, HS, GEN // 4)
    return (duals_new, first_avg, second_avg, third_avg, jnp.reshape(eta_level, (1,)), eta_duals_new)
```

```python
import functools

import jax
import jax.numpy as jnp
from jax import lax
from jax.experimental import pallas as pl
from jax.experimental.pallas import tpu as pltpu
from jax.sharding import PartitionSpec as P

BRANCH = 16
PENALTY = 1.0
CVAR_WEIGHT = 0.25
CVAR_LEVEL = 0.75
CHUNKS = 4
F32 = jnp.float32
BF16 = jnp.bfloat16

ANY = pl.BlockSpec(memory_space=pl.ANY)
HBM = pl.BlockSpec(memory_space=pltpu.HBM)
SMEM = pl.BlockSpec(memory_space=pltpu.SMEM)
VMEM = pl.BlockSpec(memory_space=pltpu.VMEM)


def partner(value, mask):
    pairs = [(source, source ^ mask) for source in range(lax.axis_size("node"))]
    return lax.ppermute(value, "node", pairs)


def in_hbm(value):
    return pltpu.with_memory_space_constraint(value, pltpu.HBM)


def params(mib):
    return pltpu.CompilerParams(vmem_limit_bytes=mib << 20)


def build_target(target, anchor_of, c_v, y_v, start, length):
    def step(i, carry):
        rows = []
        for k in range(2):
            s = 2 * i + k
            own = pl.ds(start, length)
            rows.append(
                PENALTY * anchor_of(s).astype(F32)
                - c_v[s, own, :].astype(F32)
                - y_v[s, own, :].astype(F32)
            )
        block = jnp.concatenate(rows, axis=0).astype(BF16)
        target[pl.ds(pl.multiple_of(i * 2 * length, 2 * length), 2 * length), :] = block
        return carry

    lax.fori_loop(0, c_v.shape[0] // 2, step, 0)


def multiply(target, inv_v, z, c_v, y_v, cost, start, length, before, fold):
    scenarios = c_v.shape[0]
    width = inv_v.shape[1] // CHUNKS
    for j in range(CHUNKS):
        before(j)
        cols = slice(j * width, (j + 1) * width)
        z[:, :, cols] = jnp.dot(
            target[...], inv_v[:, cols], preferred_element_type=F32
        ).reshape(scenarios, length, width)

        def step(s, carry):
            own = pl.ds(start, length)
            sol = z[s, :, cols]
            z[s, :, cols] = sol + y_v[s, own, cols].astype(F32)
            prod = c_v[s, own, cols].astype(F32) * sol
            part = prod[:, :128]
            for k in range(1, width // 128):
                part = part + prod[:, k * 128 : (k + 1) * 128]
            cost[s] = cost[s] + part
            return fold(s, cols, sol, carry)

        total = lax.fori_loop(0, scenarios, step, jnp.zeros((length, width), F32), unroll=4)
        fold(None, cols, None, total)


def first_kernel(w, sec, pf, c_hbm, y_hbm, inv_hbm, c_v, y_v, inv_v, z, a1, mass, cost, target, sems):
    scenarios, hours, columns = c_hbm.shape
    length = hours // 3
    width = columns // CHUNKS

    def rows(k):
        own = pl.ds(k * length, length)
        return (
            pltpu.make_async_copy(c_hbm.at[:, own, :], c_v.at[:, own, :], sems.at[2 * k]),
            pltpu.make_async_copy(y_hbm.at[:, own, :], y_v.at[:, own, :], sems.at[2 * k + 1]),
        )

    def chunk(j):
        own = pl.ds(j * width, width)
        return pltpu.make_async_copy(inv_hbm.at[:, own], inv_v.at[:, own], sems.at[6 + j])

    for copy in rows(0):
        copy.start()
    for j in range(CHUNKS):
        chunk(j).start()
    for k in (2, 1):
        for copy in rows(k):
            copy.start()

    mass[...] = jnp.zeros_like(mass)
    cost[...] = jnp.zeros_like(cost)

    def count(s, carry):
        node = pl.ds(sec[s] % BRANCH, 1)
        mass[node, :] = mass[node, :] + w[s].astype(F32)
        return carry

    lax.fori_loop(0, scenarios, count, 0)
    for copy in rows(0):
        copy.wait()
    build_target(target, lambda s: pf[...], c_v, y_v, 0, length)

    def fold(s, cols, sol, carry):
        if s is None:
            a1[:, cols] = carry
            return None
        return carry + w[s].astype(F32) * sol

    multiply(target, inv_v, z, c_v, y_v, cost, 0, length, lambda j: chunk(j).wait(), fold)
    for k in (2, 1):
        for copy in rows(k):
            copy.wait()


def third_kernel(w, sec, p0, p1, p2, p3, c_v, y_v, inv_v, cost_in, z, cost, keep, send, target, table, acc, sems):
    scenarios, hours, columns = c_v.shape
    length = hours // 3
    quarter = lax.axis_index("node") % 4
    shares = BRANCH // 4
    copies = [
        pltpu.make_async_copy(part, table.at[pl.ds(k * shares, shares)], sems.at[k])
        for k, part in enumerate((p0, p1, p2, p3))
    ]
    for copy in copies:
        copy.start()
    acc[...] = jnp.zeros_like(acc)
    cost[...] = cost_in[...]
    for copy in copies:
        copy.wait()

    def anchor_of(s):
        node = sec[s] % BRANCH
        return table[((node // shares) ^ quarter) * shares + node % shares]

    build_target(target, anchor_of, c_v, y_v, 2 * length, length)

    def fold(s, cols, sol, carry):
        if s is None:
            return None
        node = sec[s] % BRANCH
        half = (node // shares) % 2
        place = ((half ^ (quarter % 2)) * 2 + node // (2 * shares)) * shares + node % shares
        acc[place, :, cols] = acc[place, :, cols] + w[s].astype(F32) * sol
        return carry

    multiply(target, inv_v, z, c_v, y_v, cost, 2 * length, length, lambda j: None, fold)
    keep[...] = acc[: BRANCH // 2]
    send[...] = acc[BRANCH // 2 :].astype(BF16)


def second_kernel(
    w, mean, w_row, duals_row, p0, p1, p2, p3, c_v, y_v, inv_v, cost_in, z, a2, eta, scal, target, table, cost, sems
):
    scenarios, hours, columns = c_v.shape
    length = hours // 3
    quarter = lax.axis_index("node") % 4
    share = columns // 4
    copies = [
        pltpu.make_async_copy(
            part.at[0], table.at[:, pl.ds(pl.multiple_of((quarter ^ k) * share, share), share)], sems.at[k]
        )
        for k, part in enumerate((p0, p1, p2, p3))
    ]
    for copy in copies:
        copy.start()
    cost[...] = cost_in[...]
    for copy in copies:
        copy.wait()
    build_target(target, lambda s: table[...], c_v, y_v, length, length)

    def fold(s, cols, sol, carry):
        if s is None:
            a2[:, cols] = carry
            return None
        return carry + w[s].astype(F32) * sol

    multiply(target, inv_v, z, c_v, y_v, cost, length, length, lambda j: None, fold)
    lanes = jnp.sum(cost[...], axis=1)
    scen_cost = jnp.sum(lanes.T, axis=0, keepdims=True) / (hours * columns)
    p = w_row[...].astype(F32)
    low = mean[0] - (CVAR_WEIGHT + duals_row[...]) / PENALTY
    high = low + CVAR_WEIGHT / ((1.0 - CVAR_LEVEL) * PENALTY)
    level = jnp.minimum(jnp.maximum(scen_cost, low), high)
    eta[...] = level
    total = jnp.sum(p * level, axis=1, keepdims=True)
    mass = jnp.sum(p, axis=1, keepdims=True)
    row = lax.broadcasted_iota(jnp.int32, scal.shape, 0)
    scal[...] = jnp.where(row == 0, total, jnp.where(row == 1, mass, 0.0))


def chip_sum_kernel(keep, got, mass_own, mass_got, total, send, mass):
    value = keep[...] + got[...].astype(F32)
    total[...] = value
    send[...] = value.astype(BF16)
    mass[...] = mass_own[...] + mass_got[...]


def third_avg_kernel(total, got, mass_own, mass_got, avg, send, third_avg, mass):
    shares = BRANCH // 4
    quarter = lax.axis_index("node") % 4
    mass[...] = mass_own[...] + mass_got[...]
    for k in range(BRANCH // 2):
        node = ((k // shares) * 2 + quarter % 2) * shares + k % shares
        value = (total[k] + got[k].astype(F32)) / mass[pl.ds(node, 1), :][:, :1]
        avg[k] = value
        send[k] = value.astype(BF16)
    third_avg[...] = avg[pl.ds((quarter // 2) * shares, shares)]


def write_duals(z, avg_of, out, buf, sems, start, length):
    scenarios = z.shape[0]
    group = scenarios // 4

    def copy(g):
        own = pl.ds(g * group, group)
        return pltpu.make_async_copy(buf.at[own], out.at[own, pl.ds(start, length), :], sems.at[g])

    for g in range(4):

        def step(i, carry):
            s = g * group + i
            buf[s] = (z[s] - PENALTY * avg_of(s)).astype(BF16)
            return carry

        lax.fori_loop(0, group, step, 0)
        copy(g).start()
    return [copy(g) for g in range(4)]


def third_duals_kernel(sec, z, avg, got, out, buf, table, sems):
    length = z.shape[1]
    shares = BRANCH // 4
    quarter = lax.axis_index("node") % 4
    half_size = BRANCH // 2
    table[:half_size] = avg[...]
    table[half_size:] = got[...].astype(F32)

    def avg_of(s):
        node = sec[s] % BRANCH
        half = (node // shares) % 2
        return table[((half ^ (quarter % 2)) * 2 + node // (2 * shares)) * shares + node % shares]

    for copy in write_duals(z, avg_of, out, buf, sems, 2 * length, length):
        copy.wait()


def second_duals_kernel(z, a_own, a_got, mass, prior, out, second_avg, buf, full, sems):
    length, columns = full.shape
    quarter = lax.axis_index("node") % 4
    share = columns // 4
    whole = jnp.sum(mass[...], axis=0, keepdims=True)[:, :1]
    full[...] = (a_own[...] + a_got[...]) / whole
    second_avg[0] = full[:, pl.ds(pl.multiple_of(quarter * share, share), share)]
    for copy in write_duals(z, lambda s: full[...], out, buf, sems, length, length):
        copy.wait()


def first_duals_kernel(
    z, a_own, a_got, s_own, s_got, eta, duals_row, prior, out, first_avg, eta_avg, eta_duals, buf, sems
):
    scal = s_own[...] + s_got[...]
    total = jnp.sum(scal[0:1, 0:1])
    mass = jnp.sum(scal[1:2, 0:1])
    first_avg[...] = (a_own[...] + a_got[...]) / mass
    copies = write_duals(z, lambda s: first_avg[...], out, buf, sems, 0, first_avg.shape[0])
    level = scal[0:1, 0:1] / scal[1:2, 0:1]
    eta_avg[0] = jnp.sum(level)
    eta_duals[...] = duals_row[...] + PENALTY * (eta[...] - level)
    for copy in copies:
        copy.wait()


def body(
    unit_costs,
    hour_duals,
    inverse,
    weights,
    section_three,
    prev_first,
    prev_second,
    prev_third,
    eta_mean,
    eta_duals,
):
    scenarios, hours, columns = unit_costs.shape
    length = hours // 3
    half = BRANCH // 2
    nodes = lax.axis_size("node")
    dma = pltpu.SemaphoreType.DMA
    shape = jax.ShapeDtypeStruct
    w_row = weights.reshape(1, scenarios)
    duals_row = eta_duals.reshape(1, scenarios)

    y_third, y_second = partner((prev_third, prev_second), 2)

    c_v, y_v, inv_v, z1, a1, mass, cost = pl.pallas_call(
        first_kernel,
        name="first",
        in_specs=[SMEM, SMEM, VMEM, HBM, HBM, HBM],
        out_specs=[VMEM] * 7,
        out_shape=[
            pltpu.VMEM(unit_costs.shape, BF16),
            pltpu.VMEM(hour_duals.shape, BF16),
            pltpu.VMEM(inverse.shape, BF16),
            pltpu.VMEM((scenarios, length, columns), F32),
            shape((length, columns), F32),
            shape((BRANCH, 128), F32),
            pltpu.VMEM((scenarios, length, 128), F32),
        ],
        scratch_shapes=[pltpu.VMEM((scenarios * length, columns), BF16), dma((6 + CHUNKS,))],
        compiler_params=params(30),
    )(weights, section_three, prev_first, in_hbm(unit_costs), in_hbm(hour_duals), in_hbm(inverse))

    core_third, diag_third, core_second, diag_second, core_mass = partner(
        (prev_third, y_third, prev_second, y_second, mass), 1
    )

    z3, cost, keep, send = pl.pallas_call(
        third_kernel,
        name="third",
        in_specs=[SMEM, SMEM, ANY, ANY, ANY, ANY, VMEM, VMEM, VMEM, VMEM],
        out_specs=[VMEM] * 4,
        out_shape=[
            pltpu.VMEM((scenarios, length, columns), F32),
            pltpu.VMEM((scenarios, length, 128), F32),
            pltpu.VMEM((half, length, columns), F32),
            shape((half, length, columns), BF16),
        ],
        scratch_shapes=[
            pltpu.VMEM((scenarios * length, columns), BF16),
            pltpu.VMEM((BRANCH, length, columns), BF16),
            pltpu.VMEM((BRANCH, length, columns), F32),
            dma((4,)),
        ],
        compiler_params=params(30),
    )(weights, section_three, prev_third, core_third, y_third, diag_third, c_v, y_v, inv_v, cost)

    chip_got = partner(send, 1)
    chip_total, chip_send, chip_mass = pl.pallas_call(
        chip_sum_kernel,
        name="chip_sum",
        in_specs=[VMEM] * 4,
        out_specs=[VMEM] * 3,
        out_shape=[
            pltpu.VMEM((half, length, columns), F32),
            shape((half, length, columns), BF16),
            shape((BRANCH, 128), F32),
        ],
        compiler_params=params(8),
    )(keep, chip_got, mass, core_mass)
    node_got, mass_got = partner((chip_send, chip_mass), 2)

    z2, a2, eta, scal = pl.pallas_call(
        second_kernel,
        name="second",
        in_specs=[SMEM, SMEM, VMEM, VMEM, ANY, ANY, ANY, ANY, VMEM, VMEM, VMEM, VMEM],
        out_specs=[VMEM] * 4,
        out_shape=[
            pltpu.VMEM((scenarios, length, columns), F32),
            shape((length, columns), F32),
            shape((1, scenarios), F32),
            shape((8, 128), F32),
        ],
        scratch_shapes=[
            pltpu.VMEM((scenarios * length, columns), BF16),
            pltpu.VMEM((length, columns), BF16),
            pltpu.VMEM((scenarios, length, 128), F32),
            dma((4,)),
        ],
        compiler_params=params(30),
    )(
        weights, eta_mean, w_row, duals_row, prev_second, core_second, y_second, diag_second, c_v, y_v, inv_v, cost
    )

    got = partner((scal, a1, a2), 1)
    scal, a1, a2 = scal + got[0], a1 + got[1], a2 + got[2]
    mask = 4
    while mask < nodes:
        got = partner((scal, a1), mask)
        scal, a1 = scal + got[0], a1 + got[1]
        mask *= 2
    y_scal, y_a1, y_a2 = partner((scal, a1, a2), 2)

    avg, avg_send, third_avg, node_mass = pl.pallas_call(
        third_avg_kernel,
        name="third_avg",
        in_specs=[VMEM] * 4,
        out_specs=[VMEM] * 4,
        out_shape=[
            pltpu.VMEM((half, length, columns), F32),
            shape((half, length, columns), BF16),
            shape((BRANCH // 4, length, columns), F32),
            shape((BRANCH, 128), F32),
        ],
        compiler_params=params(8),
    )(chip_total, node_got, chip_mass, mass_got)
    avg_got = partner(avg_send, 1)

    buf = pltpu.VMEM((scenarios, length, columns), BF16)
    duals_shape = shape(hour_duals.shape, BF16)
    duals = pl.pallas_call(
        third_duals_kernel,
        name="third_duals",
        in_specs=[SMEM, VMEM, VMEM, VMEM],
        out_specs=ANY,
        out_shape=duals_shape,
        scratch_shapes=[buf, pltpu.VMEM((BRANCH, length, columns), F32), dma((4,))],
        compiler_params=params(8),
    )(section_three, z3, avg, avg_got)
    duals, second_avg = pl.pallas_call(
        second_duals_kernel,
        name="second_duals",
        in_specs=[VMEM, VMEM, VMEM, VMEM, ANY],
        out_specs=[ANY, VMEM],
        out_shape=[duals_shape, shape((1, length, columns // 4), F32)],
        scratch_shapes=[buf, pltpu.VMEM((length, columns), F32), dma((4,))],
        input_output_aliases={4: 0},
        compiler_params=params(8),
    )(z2, a2, y_a2, node_mass, duals)
    duals, first_avg, eta_avg, eta_duals_new = pl.pallas_call(
        first_duals_kernel,
        name="first_duals",
        in_specs=[VMEM] * 7 + [ANY],
        out_specs=[ANY, VMEM, SMEM, VMEM],
        out_shape=[
            duals_shape,
            shape((length, columns), F32),
            shape((1,), F32),
            shape((1, scenarios), F32),
        ],
        scratch_shapes=[buf, dma((4,))],
        input_output_aliases={7: 0},
        compiler_params=params(8),
    )(z1, a1, y_a1, scal, y_scal, eta, duals_row, duals)
    return duals, first_avg, second_avg, third_avg, eta_avg, eta_duals_new.reshape(scenarios)


def solution(mesh):
    row = P(("groups", "node"))
    in_specs = (row, row, P(), row, row, P("groups"), row, row, P("groups"), row)
    out_specs = (row, P("groups"), row, row, P("groups"), row)
    return jax.shard_map(body, mesh=mesh, in_specs=in_specs, out_specs=out_specs, check_vma=False)
```

```python
import jax
import jax.numpy as jnp
from jax import lax
from jax.experimental import pallas as pl
from jax.experimental.pallas import tpu as pltpu
from jax.sharding import PartitionSpec as P

BRANCH = 16
SHARES = BRANCH // 4
HALF = BRANCH // 2
PENALTY = 1.0
CVAR_WEIGHT = 0.25
CVAR_LEVEL = 0.75
CHUNKS = 4
LANES = 128
F32 = jnp.float32
BF16 = jnp.bfloat16

ANY = pl.BlockSpec(memory_space=pl.ANY)
HBM = pl.BlockSpec(memory_space=pltpu.HBM)
SMEM = pl.BlockSpec(memory_space=pltpu.SMEM)
VMEM = pl.BlockSpec(memory_space=pltpu.VMEM)


def partner(value, mask):
    pairs = [(source, source ^ mask) for source in range(lax.axis_size("node"))]
    return lax.ppermute(value, "node", pairs)


def in_hbm(value):
    return pltpu.with_memory_space_constraint(value, pltpu.HBM)


def call(kernel, mib, **kwargs):
    return pl.pallas_call(kernel, compiler_params=pltpu.CompilerParams(vmem_limit_bytes=mib << 20), **kwargs)


def quarter_of():
    return lax.axis_index("node") % 4


def place_of(node, quarter):
    half = (node // SHARES) % 2
    return ((half ^ (quarter % 2)) * 2 + node // (2 * SHARES)) * SHARES + node % SHARES


def build_target(target, anchor_of, c_v, y_v):
    scenarios, length, _ = c_v.shape

    def step(i, carry):
        rows = []
        for k in range(2):
            s = 2 * i + k
            rows.append(PENALTY * anchor_of(s).astype(F32) - c_v[s].astype(F32) - y_v[s].astype(F32))
        block = jnp.concatenate(rows, axis=0).astype(BF16)
        target[pl.ds(pl.multiple_of(i * 2 * length, 2 * length), 2 * length), :] = block
        return carry

    lax.fori_loop(0, scenarios // 2, step, 0, unroll=2)


def multiply(target, inv_v, sol, c_v, cost, before, w, after):
    scenarios, length, columns = sol.shape
    width = columns // CHUNKS
    for j in range(CHUNKS):
        before(j)
        cols = slice(j * width, (j + 1) * width)
        sol[:, :, cols] = jnp.dot(target[...], inv_v[:, cols], preferred_element_type=F32).reshape(
            scenarios, length, width
        )

        def step(s, carry):
            own = sol[s, :, cols]
            prod = c_v[s, :, cols].astype(F32) * own
            part = prod[:, :LANES]
            for k in range(1, width // LANES):
                part = part + prod[:, k * LANES : (k + 1) * LANES]
            cost[s] = cost[s] + part
            return carry if w is None else carry + w[s].astype(F32) * own

        after(cols, lax.fori_loop(0, scenarios, step, jnp.zeros((length, width), F32), unroll=8))


def first_kernel(
    w_hbm, sec_hbm, pf_hbm, c_hbm, y_hbm, inv_hbm,
    w, sec, y_v, inv_v, sol, a1, mass, pick, cost, c_v, pf, target, sems,
):
    scenarios, length, columns = sol.shape
    width = columns // CHUNKS
    own = pl.ds(0, length)

    def chunk(j):
        part = pl.ds(j * width, width)
        return pltpu.make_async_copy(inv_hbm.at[:, part], inv_v.at[:, part], sems.at[5 + j])

    small = [
        pltpu.make_async_copy(w_hbm, w, sems.at[0]),
        pltpu.make_async_copy(sec_hbm, sec, sems.at[1]),
        pltpu.make_async_copy(pf_hbm, pf, sems.at[2]),
    ]
    rows = [
        pltpu.make_async_copy(c_hbm.at[:, own, :], c_v, sems.at[3]),
        pltpu.make_async_copy(y_hbm.at[:, own, :], y_v, sems.at[4]),
    ]
    for copy in small + rows + [chunk(j) for j in range(CHUNKS)]:
        copy.start()
    cost[...] = jnp.zeros_like(cost)
    mass[...] = jnp.zeros_like(mass)
    for copy in small:
        copy.wait()

    quarter = quarter_of()
    lane = lax.broadcasted_iota(jnp.int32, (1, scenarios * length), 1)

    def count(s, carry):
        total, place, weight = carry
        node = sec[s] % BRANCH
        p = w[s].astype(F32)
        mass[pl.ds(node, 1), :] = mass[pl.ds(node, 1), :] + p
        mine = lane // length == s
        return total + p, jnp.where(mine, place_of(node, quarter), place), jnp.where(mine, p, weight)

    total, place, weight = lax.fori_loop(
        0, scenarios, count, (jnp.float32(0), jnp.zeros(lane.shape, jnp.int32), jnp.zeros(lane.shape, F32))
    )
    a1[:, columns:] = jnp.full((length, LANES), total, F32)
    row = lax.broadcasted_iota(jnp.int32, pick.shape, 0)
    column = lax.broadcasted_iota(jnp.int32, pick.shape, 1)
    chosen = (row // length == place) & (row % length == column % length)
    pick[...] = jnp.where(chosen, weight, 0.0).astype(BF16)

    for copy in rows:
        copy.wait()
    build_target(target, lambda s: pf[...], c_v, y_v)

    def after(cols, total):
        a1[:, cols] = total

    multiply(target, inv_v, sol, c_v, cost, lambda j: chunk(j).wait(), w, after)


def section_copies(c_hbm, y_hbm, c_v, y_v, sems, section):
    length = c_v.shape[1]
    own = pl.ds(section * length, length)
    return [
        pltpu.make_async_copy(c_hbm.at[:, own, :], c_v, sems.at[0]),
        pltpu.make_async_copy(y_hbm.at[:, own, :], y_v, sems.at[1]),
    ]


def load_kernel(c_hbm, y_hbm, c_v, y_v, sems):
    copies = section_copies(c_hbm, y_hbm, c_v, y_v, sems, 2)
    for copy in copies:
        copy.start()
    for copy in copies:
        copy.wait()


def third_kernel(
    sec, p0, p1, p2, p3, c_hbm, y_hbm, c_v, y_v, inv_v, pick, cost_in,
    c2_v, y2_v, sol, cost, keep, send, target, table, acc, sems, sems2,
):
    scenarios, length, _ = sol.shape
    quarter = quarter_of()
    copies = [
        pltpu.make_async_copy(part, table.at[pl.ds(k * SHARES, SHARES)], sems.at[k])
        for k, part in enumerate((p0, p1, p2, p3))
    ]
    for copy in copies:
        copy.start()
    ahead = section_copies(c_hbm, y_hbm, c2_v, y2_v, sems2, 1)
    for copy in ahead:
        copy.start()
    cost[...] = cost_in[...]
    for copy in copies:
        copy.wait()

    def anchor_of(s):
        node = sec[s] % BRANCH
        return table[((node // SHARES) ^ quarter) * SHARES + node % SHARES]

    build_target(target, anchor_of, c_v, y_v)

    def after(cols, total):
        own = sol[:, :, cols]
        flat = own.reshape(scenarios * length, own.shape[2]).astype(BF16)
        sums = jnp.dot(pick[...], flat, preferred_element_type=F32).reshape(BRANCH, length, own.shape[2])
        keep[:, :, cols] = sums[:HALF]
        send[:, :, cols] = sums[HALF:].astype(BF16)

    multiply(target, inv_v, sol, c_v, cost, lambda j: None, None, after)
    for copy in ahead:
        copy.wait()


def second_kernel(
    w, w_row, low_row, p0, p1, p2, p3, c_v, y_v, inv_v, cost_in, sol, a2, eta, scal, target, table, cost, sems
):
    _, length, columns = sol.shape
    quarter = quarter_of()
    share = columns // 4
    copies = [
        pltpu.make_async_copy(
            part.at[0], table.at[:, pl.ds(pl.multiple_of((quarter ^ k) * share, share), share)], sems.at[k]
        )
        for k, part in enumerate((p0, p1, p2, p3))
    ]
    for copy in copies:
        copy.start()
    cost[...] = cost_in[...]
    for copy in copies:
        copy.wait()
    build_target(target, lambda s: table[...], c_v, y_v)

    def after(cols, total):
        a2[:, cols] = total

    multiply(target, inv_v, sol, c_v, cost, lambda j: None, w, after)
    lanes = jnp.sum(cost[...], axis=1)
    scen_cost = jnp.sum(lanes.T, axis=0, keepdims=True) / (3 * length * columns)
    p = w_row[...].astype(F32)
    low = low_row[...]
    high = low + CVAR_WEIGHT / ((1.0 - CVAR_LEVEL) * PENALTY)
    level = jnp.minimum(jnp.maximum(scen_cost, low), high)
    eta[...] = level
    total = jnp.sum(p * level, axis=1, keepdims=True)
    mass = jnp.sum(p, axis=1, keepdims=True)
    row = lax.broadcasted_iota(jnp.int32, scal.shape, 0)
    scal[...] = jnp.where(row == 0, total, jnp.where(row == 1, mass, 0.0))


def chip_sum_kernel(keep, got, mass_own, mass_got, total, send, mass):
    value = keep[...] + got[...].astype(F32)
    total[...] = value
    send[...] = value.astype(BF16)
    mass[...] = mass_own[...] + mass_got[...]


def third_avg_kernel(total, got, mass_own, mass_got, avg, send, third_avg, mass):
    quarter = quarter_of()
    mass[...] = mass_own[...] + mass_got[...]
    for k in range(HALF):
        node = ((k // SHARES) * 2 + quarter % 2) * SHARES + k % SHARES
        value = (total[k] + got[k].astype(F32)) / mass[pl.ds(node, 1), :][:, :1]
        avg[k] = value
        send[k] = value.astype(BF16)
    third_avg[...] = avg[pl.ds((quarter // 2) * SHARES, SHARES)]


def write_duals(sol, y_v, avg_of, out, buf, sems, section):
    scenarios, length, _ = sol.shape
    group = scenarios // 4

    def copy(g):
        own = pl.ds(g * group, group)
        return pltpu.make_async_copy(
            buf.at[own], out.at[own, pl.ds(section * length, length), :], sems.at[g]
        )

    for g in range(4):

        def step(i, carry):
            s = g * group + i
            buf[s] = (y_v[s].astype(F32) + PENALTY * (sol[s] - avg_of(s))).astype(BF16)
            return carry

        lax.fori_loop(0, group, step, 0, unroll=2)
        copy(g).start()
    return [copy(g) for g in range(4)]


def third_duals_kernel(sec, sol, y_v, avg, got, out, buf, table, sems):
    quarter = quarter_of()
    table[:HALF] = avg[...]
    table[HALF:] = got[...].astype(F32)
    for copy in write_duals(
        sol, y_v, lambda s: table[place_of(sec[s] % BRANCH, quarter)], out, buf, sems, 2
    ):
        copy.wait()


def second_duals_kernel(sol, y_v, a_own, a_got, mass, prior, out, second_avg, buf, full, sems):
    _, columns = full.shape
    quarter = quarter_of()
    share = columns // 4
    whole = jnp.sum(mass[...], axis=0, keepdims=True)[:, :1]
    full[...] = (a_own[...] + a_got[...]) / whole
    second_avg[0] = full[:, pl.ds(pl.multiple_of(quarter * share, share), share)]
    for copy in write_duals(sol, y_v, lambda s: full[...], out, buf, sems, 1):
        copy.wait()


def first_duals_kernel(sol, y_v, a_own, a_got, prior, out, first_avg, buf, sems):
    columns = first_avg.shape[1]
    whole = a_own[...] + a_got[...]
    first_avg[...] = whole[:, :columns] / whole[:, columns : columns + 1]
    for copy in write_duals(sol, y_v, lambda s: first_avg[...], out, buf, sems, 0):
        copy.wait()


def eta_kernel(s_own, s_got, eta, duals_row, eta_avg, eta_duals):
    scal = s_own[...] + s_got[...]
    level = scal[0:1, 0:1] / scal[1:2, 0:1]
    eta_avg[0] = jnp.sum(level)
    eta_duals[...] = duals_row[...] + PENALTY * (eta[...] - level)


def step(
    unit_costs,
    hour_duals,
    inverse,
    weights,
    section_three,
    prev_first,
    prev_second,
    prev_third,
    eta_mean,
    eta_duals,
):
    scenarios, hours, columns = unit_costs.shape
    length = hours // 3
    nodes = lax.axis_size("node")
    dma = pltpu.SemaphoreType.DMA
    shape = jax.ShapeDtypeStruct
    block = (scenarios, length, columns)
    rows = scenarios * length
    w_row = weights.reshape(1, scenarios)
    duals_row = eta_duals.reshape(1, scenarios)
    costs, duals, matrix = in_hbm(unit_costs), in_hbm(hour_duals), in_hbm(inverse)

    low_row = eta_mean[:, None] - (CVAR_WEIGHT + duals_row) / PENALTY
    y_third, y_second = partner((prev_third, prev_second), 2)

    w, sec, y1, inv_v, sol1, a1, mass, pick, cost = call(
        first_kernel,
        30,
        in_specs=[HBM] * 6,
        out_specs=[SMEM] * 2 + [VMEM] * 7,
        out_shape=[
            pltpu.SMEM((scenarios,), jnp.int32),
            pltpu.SMEM((scenarios,), jnp.int32),
            pltpu.VMEM(block, BF16),
            pltpu.VMEM(inverse.shape, BF16),
            pltpu.VMEM(block, F32),
            shape((length, columns + LANES), F32),
            shape((BRANCH, LANES), F32),
            pltpu.VMEM((BRANCH * length, rows), BF16),
            pltpu.VMEM((scenarios, length, LANES), F32),
        ],
        scratch_shapes=[
            pltpu.VMEM(block, BF16),
            pltpu.VMEM((length, columns), BF16),
            pltpu.VMEM((rows, columns), BF16),
            dma((5 + CHUNKS,)),
        ],
    )(in_hbm(weights), in_hbm(section_three), in_hbm(prev_first), costs, duals, matrix)

    core_third, diag_third, core_second, diag_second, core_mass, core_a1 = partner(
        (prev_third, y_third, prev_second, y_second, mass, a1), 1
    )
    c3, y3 = call(
        load_kernel,
        8,
        in_specs=[HBM] * 2,
        out_specs=[VMEM] * 2,
        out_shape=[pltpu.VMEM(block, BF16)] * 2,
        scratch_shapes=[dma((2,))],
    )(costs, duals)
    a1 = a1 + core_a1

    c2, y2, sol3, cost, keep, send = call(
        third_kernel,
        30,
        in_specs=[SMEM, ANY, ANY, ANY, ANY, HBM, HBM] + [VMEM] * 5,
        out_specs=[VMEM] * 6,
        out_shape=[
            pltpu.VMEM(block, BF16),
            pltpu.VMEM(block, BF16),
            pltpu.VMEM(block, F32),
            pltpu.VMEM((scenarios, length, LANES), F32),
            pltpu.VMEM((HALF, length, columns), F32),
            shape((HALF, length, columns), BF16),
        ],
        scratch_shapes=[
            pltpu.VMEM((rows, columns), BF16),
            pltpu.VMEM((BRANCH, length, columns), BF16),
            pltpu.VMEM((BRANCH, length, columns), F32),
            dma((4,)),
            dma((2,)),
        ],
    )(sec, prev_third, core_third, y_third, diag_third, costs, duals, c3, y3, inv_v, pick, cost)

    chip_got = partner(send, 1)
    a1 = a1 + partner(a1, 2)

    sol2, a2, eta, scal = call(
        second_kernel,
        30,
        in_specs=[SMEM, VMEM, VMEM, ANY, ANY, ANY, ANY, VMEM, VMEM, VMEM, VMEM],
        out_specs=[VMEM] * 4,
        out_shape=[
            pltpu.VMEM(block, F32),
            shape((length, columns), F32),
            shape((1, scenarios), F32),
            shape((8, LANES), F32),
        ],
        scratch_shapes=[
            pltpu.VMEM((rows, columns), BF16),
            pltpu.VMEM((length, columns), BF16),
            pltpu.VMEM((scenarios, length, LANES), F32),
            dma((4,)),
        ],
    )(w, w_row, low_row, prev_second, core_second, y_second, diag_second, c2, y2, inv_v, cost)

    core_scal, core_a2 = partner((scal, a2), 1)
    chip_total, chip_send, chip_mass = call(
        chip_sum_kernel,
        8,
        in_specs=[VMEM] * 4,
        out_specs=[VMEM] * 3,
        out_shape=[
            pltpu.VMEM((HALF, length, columns), F32),
            shape((HALF, length, columns), BF16),
            shape((BRANCH, LANES), F32),
        ],
    )(keep, chip_got, mass, core_mass)
    node_got, mass_got = partner((chip_send, chip_mass), 2)
    scal, a2 = scal + core_scal, a2 + core_a2

    masks = []
    while 4 << len(masks) < nodes:
        masks.append(4 << len(masks))
    y_a2 = partner(a2, 2)
    for mask in masks:
        a1_got = partner(a1, mask)
        scal = scal + partner(scal, mask)
        a1_own, a1 = a1, a1 + a1_got
    y_scal = partner(scal, 2)

    avg, avg_send, third_avg, node_mass = call(
        third_avg_kernel,
        8,
        in_specs=[VMEM] * 4,
        out_specs=[VMEM] * 4,
        out_shape=[
            pltpu.VMEM((HALF, length, columns), F32),
            shape((HALF, length, columns), BF16),
            shape((SHARES, length, columns), F32),
            shape((BRANCH, LANES), F32),
        ],
    )(chip_total, node_got, chip_mass, mass_got)
    avg_got = partner(avg_send, 1)

    buf = pltpu.VMEM(block, BF16)
    duals_shape = shape(hour_duals.shape, BF16)
    out, first_avg = call(
        first_duals_kernel,
        8,
        in_specs=[VMEM] * 4 + [SMEM],
        out_specs=[ANY, VMEM],
        out_shape=[duals_shape, shape((length, columns), F32)],
        scratch_shapes=[buf, dma((4,))],
    )(sol1, y1, a1_own, a1_got, sec)
    out, second_avg = call(
        second_duals_kernel,
        8,
        in_specs=[VMEM] * 5 + [ANY],
        out_specs=[ANY, VMEM],
        out_shape=[duals_shape, shape((1, length, columns // 4), F32)],
        scratch_shapes=[buf, pltpu.VMEM((length, columns), F32), dma((4,))],
        input_output_aliases={5: 0},
    )(sol2, y2, a2, y_a2, node_mass, out)
    out = call(
        lambda sec, sol, y_v, avg, got, prior, *rest: third_duals_kernel(sec, sol, y_v, avg, got, *rest),
        8,
        in_specs=[SMEM] + [VMEM] * 4 + [ANY],
        out_specs=ANY,
        out_shape=duals_shape,
        scratch_shapes=[buf, pltpu.VMEM((BRANCH, length, columns), F32), dma((4,))],
        input_output_aliases={5: 0},
    )(sec, sol3, y3, avg, avg_got, out)
    eta_avg, eta_duals_new = call(
        eta_kernel,
        8,
        in_specs=[VMEM] * 4,
        out_specs=[SMEM, VMEM],
        out_shape=[shape((1,), F32), shape((1, scenarios), F32)],
    )(scal, y_scal, eta, duals_row)
    return out, first_avg, second_avg, third_avg, eta_avg, eta_duals_new.reshape(scenarios)


def solution(mesh):
    row = P(("groups", "node"))
    in_specs = (row, row, P(), row, row, P("groups"), row, row, P("groups"), row)
    out_specs = (row, P("groups"), row, row, P("groups"), row)
    return jax.shard_map(step, mesh=mesh, in_specs=in_specs, out_specs=out_specs, check_vma=False)
```

```python
import jax
import jax.numpy as jnp
from jax import lax
from jax.experimental import pallas as pl
from jax.experimental.pallas import tpu as pltpu
from jax.sharding import PartitionSpec as P

BRANCH = 16
SHARES = BRANCH // 4
HALF = BRANCH // 2
PENALTY = 1.0
CVAR_WEIGHT = 0.25
CVAR_LEVEL = 0.75
CHUNKS = 4
LANES = 128
F32 = jnp.float32
BF16 = jnp.bfloat16

ANY = pl.BlockSpec(memory_space=pl.ANY)
HBM = pl.BlockSpec(memory_space=pltpu.HBM)
SMEM = pl.BlockSpec(memory_space=pltpu.SMEM)
VMEM = pl.BlockSpec(memory_space=pltpu.VMEM)


def partner(value, mask):
    pairs = [(source, source ^ mask) for source in range(lax.axis_size("node"))]
    return lax.ppermute(value, "node", pairs)


def in_hbm(value):
    return pltpu.with_memory_space_constraint(value, pltpu.HBM)


def call(kernel, mib, **kwargs):
    return pl.pallas_call(kernel, compiler_params=pltpu.CompilerParams(vmem_limit_bytes=mib << 20), **kwargs)


def quarter_of():
    return lax.axis_index("node") % 4


def place_of(node, quarter):
    half = (node // SHARES) % 2
    return ((half ^ (quarter % 2)) * 2 + node // (2 * SHARES)) * SHARES + node % SHARES


def build_target(target, anchor_of, c_v, y_v):
    scenarios, length, _ = c_v.shape

    def step(i, carry):
        rows = []
        for k in range(2):
            s = 2 * i + k
            rows.append(PENALTY * anchor_of(s).astype(F32) - c_v[s].astype(F32) - y_v[s].astype(F32))
        block = jnp.concatenate(rows, axis=0).astype(BF16)
        target[pl.ds(pl.multiple_of(i * 2 * length, 2 * length), 2 * length), :] = block
        return carry

    lax.fori_loop(0, scenarios // 2, step, 0, unroll=2)


def multiply(target, inv_v, sol, c_v, cost, before, w, after):
    scenarios, length, columns = sol.shape
    width = columns // CHUNKS

    def product(j):
        before(j)
        cols = slice(j * width, (j + 1) * width)
        sol[:, :, cols] = jnp.dot(target[...], inv_v[:, cols], preferred_element_type=F32).reshape(
            scenarios, length, width
        )

    def finish(j):
        cols = slice(j * width, (j + 1) * width)
        total = jnp.zeros((length, width), F32)
        for s in range(scenarios):
            own = sol[s, :, cols]
            prod = c_v[s, :, cols].astype(F32) * own
            part = prod[:, :LANES]
            for k in range(1, width // LANES):
                part = part + prod[:, k * LANES : (k + 1) * LANES]
            cost[s] = cost[s] + part
            if w is not None:
                total = total + w[s].astype(F32) * own
        after(cols, total)

    for j in range(CHUNKS):
        product(j)
        if j:
            finish(j - 1)
    finish(CHUNKS - 1)


def first_kernel(
    w_hbm, sec_hbm, pf_hbm, c_hbm, y_hbm, inv_hbm,
    w, sec, y1, c3, y3, inv_v, sol, a1, mass, pick, cost, c1, pf, target, sems,
):
    scenarios, length, columns = sol.shape
    width = columns // CHUNKS

    def chunk(j):
        part = pl.ds(j * width, width)
        return pltpu.make_async_copy(inv_hbm.at[:, part], inv_v.at[:, part], sems.at[9 + j])

    def rows(k, c_v, y_v):
        own = pl.ds(k * length, length)
        return [
            pltpu.make_async_copy(c_hbm.at[:, own, :], c_v, sems.at[3 + 2 * k]),
            pltpu.make_async_copy(y_hbm.at[:, own, :], y_v, sems.at[4 + 2 * k]),
        ]

    small = [
        pltpu.make_async_copy(w_hbm, w, sems.at[0]),
        pltpu.make_async_copy(sec_hbm, sec, sems.at[1]),
        pltpu.make_async_copy(pf_hbm, pf, sems.at[2]),
    ]
    first = rows(0, c1, y1)
    later = rows(2, c3, y3)
    for copy in small + first + [chunk(j) for j in range(CHUNKS)] + later:
        copy.start()
    cost[...] = jnp.zeros_like(cost)
    for copy in small:
        copy.wait()

    quarter = quarter_of()
    lane = lax.broadcasted_iota(jnp.int32, (1, scenarios * length), 1)
    slot = lax.broadcasted_iota(jnp.int32, mass.shape, 1)

    def count(s, carry):
        place, weight, masses = carry
        node = sec[s] % BRANCH
        p = w[s].astype(F32)
        mine = lane // length == s
        return (
            jnp.where(mine, place_of(node, quarter), place),
            jnp.where(mine, p, weight),
            masses + jnp.where(slot == node, p, 0.0),
        )

    place, weight, masses = lax.fori_loop(
        0, scenarios, count, (jnp.zeros(lane.shape, jnp.int32), jnp.zeros(lane.shape, F32), jnp.zeros(mass.shape, F32))
    )
    mass[...] = masses
    row = lax.broadcasted_iota(jnp.int32, pick.shape, 0)
    column = lax.broadcasted_iota(jnp.int32, pick.shape, 1)
    chosen = (row // length == place) & (row % length == column % length)
    pick[...] = jnp.where(chosen, weight, 0.0).astype(BF16)

    for copy in first:
        copy.wait()
    build_target(target, lambda s: pf[...], c1, y1)

    def after(cols, total):
        a1[:, cols] = total

    multiply(target, inv_v, sol, c1, cost, lambda j: chunk(j).wait(), w, after)
    for copy in later:
        copy.wait()


def packed(value):
    high = value.astype(BF16)
    rest = value - high.astype(F32)
    middle = rest.astype(BF16)
    return jnp.concatenate((high, middle, (rest - middle.astype(F32)).astype(BF16)), axis=1)


def unpacked(tiles):
    high, middle, low = (tiles[:, k * LANES : (k + 1) * LANES].astype(F32) for k in range(3))
    return high + middle + low


def node_mass(scal, node):
    row = scal[2:3, :]
    slot = lax.broadcasted_iota(jnp.int32, row.shape, 1)
    return jnp.sum(jnp.where(slot == node, row, 0.0), axis=1, keepdims=True)


def third_kernel(
    sec, p0, p1, p2, p3, c_hbm, y_hbm, c_v, y_v, inv_v, pick, cost_in,
    c2, y2, sol, cost, keep, send, target, table, sems,
):
    scenarios, length, _ = sol.shape
    quarter = quarter_of()
    copies = [
        pltpu.make_async_copy(part, table.at[pl.ds(k * SHARES, SHARES)], sems.at[k])
        for k, part in enumerate((p0, p1, p2, p3))
    ]
    own = pl.ds(length, length)
    ahead = [
        pltpu.make_async_copy(c_hbm.at[:, own, :], c2, sems.at[4]),
        pltpu.make_async_copy(y_hbm.at[:, own, :], y2, sems.at[5]),
    ]
    for copy in copies + ahead:
        copy.start()
    cost[...] = cost_in[...]
    for copy in copies:
        copy.wait()

    def anchor_of(s):
        node = sec[s] % BRANCH
        return table[((node // SHARES) ^ quarter) * SHARES + node % SHARES]

    build_target(target, anchor_of, c_v, y_v)

    def after(cols, total):
        own = sol[:, :, cols]
        flat = own.reshape(scenarios * length, own.shape[2]).astype(BF16)
        sums = jnp.dot(pick[...], flat, preferred_element_type=F32).reshape(BRANCH, length, own.shape[2])
        keep[:, :, cols] = sums[:HALF]
        send[:, :, cols] = sums[HALF:].astype(BF16)

    multiply(target, inv_v, sol, c_v, cost, lambda j: None, None, after)
    for copy in ahead:
        copy.wait()


def second_kernel(
    w, w_row, low_row, p0, p1, p2, p3, c_v, y_v, inv_v, cost_in, a1, mass,
    sol, eta, sums, target, table, cost, sems,
):
    _, length, columns = sol.shape
    share = columns // 4
    quarter = quarter_of()
    copies = [
        pltpu.make_async_copy(
            part.at[0], table.at[:, pl.ds(pl.multiple_of((quarter ^ k) * share, share), share)], sems.at[k]
        )
        for k, part in enumerate((p0, p1, p2, p3))
    ]
    for copy in copies:
        copy.start()
    cost[...] = cost_in[...]
    sums[:, :columns] = a1[...].astype(BF16)
    for copy in copies:
        copy.wait()
    build_target(target, lambda s: table[...], c_v, y_v)

    def after(cols, total):
        sums[:, columns + cols.start : columns + cols.stop] = total.astype(BF16)

    multiply(target, inv_v, sol, c_v, cost, lambda j: None, w, after)
    lanes = jnp.sum(cost[...], axis=1)
    scen_cost = jnp.sum(lanes.T, axis=0, keepdims=True) / (3 * length * columns)
    p = w_row[...].astype(F32)
    low = low_row[...]
    high = low + CVAR_WEIGHT / ((1.0 - CVAR_LEVEL) * PENALTY)
    level = jnp.minimum(jnp.maximum(scen_cost, low), high)
    eta[...] = level
    total = jnp.sum(p * level, axis=1, keepdims=True)
    whole = jnp.sum(p, axis=1, keepdims=True)
    row = lax.broadcasted_iota(jnp.int32, (length, LANES), 0)
    scal = jnp.where(row == 0, total, jnp.where(row == 1, whole, jnp.where(row == 2, mass[...], 0.0)))
    sums[:, 2 * columns :] = packed(scal)


def chip_sum_kernel(keep, got, s_own, s_got, total, send, sums):
    wide = sums.shape[1] - 3 * LANES
    value = keep[...] + got[...].astype(F32)
    total[...] = value
    send[...] = value.astype(BF16)
    sums[:, :wide] = (s_own[:, :wide].astype(F32) + s_got[:, :wide].astype(F32)).astype(BF16)
    sums[:, wide:] = packed(unpacked(s_own[:, wide:]) + unpacked(s_got[:, wide:]))


def node_sum_kernel(s_own, s_got, sums, a2, scal):
    columns = a2.shape[1]
    sums[:, :columns] = (s_own[:, :columns].astype(F32) + s_got[:, :columns].astype(F32)).astype(BF16)
    a2[...] = s_own[:, columns : 2 * columns].astype(F32) + s_got[:, columns : 2 * columns].astype(F32)
    value = unpacked(s_own[:, 2 * columns :]) + unpacked(s_got[:, 2 * columns :])
    scal[...] = value
    sums[:, columns:] = packed(value)


def far_sum_kernel(s_own, s_got, sums):
    columns = sums.shape[1] - 3 * LANES
    sums[:, :columns] = (s_own[:, :columns].astype(F32) + s_got[:, :columns].astype(F32)).astype(BF16)
    sums[:, columns:] = packed(unpacked(s_own[:, columns:]) + unpacked(s_got[:, columns:]))


def third_avg_kernel(total, got, scal, avg, send, third_avg, sem):
    quarter = quarter_of()
    for k in range(HALF):
        node = ((k // SHARES) * 2 + quarter % 2) * SHARES + k % SHARES
        value = (total[k] + got[k].astype(F32)) / node_mass(scal, node)
        avg[k] = value
        send[k] = value.astype(BF16)
    copy = pltpu.make_async_copy(avg.at[pl.ds((quarter // 2) * SHARES, SHARES)], third_avg, sem)
    copy.start()
    copy.wait()


def write_duals(sol, y_v, avg_of, out, buf, sems, section):
    scenarios, length, _ = sol.shape
    group = scenarios // 4

    def copy(g):
        own = pl.ds(g * group, group)
        return pltpu.make_async_copy(
            buf.at[own], out.at[own, pl.ds(section * length, length), :], sems.at[g]
        )

    for g in range(4):

        def step(i, carry):
            s = g * group + i
            buf[s] = (y_v[s].astype(F32) + PENALTY * (sol[s] - avg_of(s))).astype(BF16)
            return carry

        lax.fori_loop(0, group, step, 0, unroll=4)
        copy(g).start()
    return [copy(g) for g in range(4)]


def second_duals_kernel(sol, y_v, a2, scal, out, second_avg, buf, full, sems, sem):
    _, columns = full.shape
    quarter = quarter_of()
    share = columns // 4
    full[...] = a2[...] / jnp.sum(scal[2:3, :], axis=1, keepdims=True)
    own = pl.ds(pl.multiple_of(quarter * share, share), share)
    copy = pltpu.make_async_copy(full.at[:, own], second_avg.at[0], sem)
    copy.start()
    for other in write_duals(sol, y_v, lambda s: full[...], out, buf, sems, 1):
        other.wait()
    copy.wait()


def third_duals_kernel(sec, sol, y_v, avg, got, prior, out, buf, table, sems):
    quarter = quarter_of()
    table[:HALF] = avg[...]
    table[HALF:] = got[...].astype(F32)
    for copy in write_duals(
        sol, y_v, lambda s: table[place_of(sec[s] % BRANCH, quarter)], out, buf, sems, 2
    ):
        copy.wait()


def last_kernel(
    sol, y_v, s_own, s_got, eta, duals_row, prior, out, first_avg, eta_avg, eta_duals, buf, full, row, sems, sems2
):
    columns = full.shape[1]
    scal = unpacked(s_own[:, columns:]) + unpacked(s_got[:, columns:])
    total, mass = scal[0:1, 0:1], scal[1:2, 0:1]
    full[...] = (s_own[:, :columns].astype(F32) + s_got[:, :columns].astype(F32)) / mass
    level = total / mass
    row[...] = duals_row[...] + PENALTY * (eta[...] - level)
    copies = [
        pltpu.make_async_copy(full, first_avg, sems2.at[0]),
        pltpu.make_async_copy(row, eta_duals, sems2.at[1]),
    ]
    for copy in copies:
        copy.start()
    copies += write_duals(sol, y_v, lambda s: full[...], out, buf, sems, 0)
    eta_avg[0] = jnp.sum(level)
    for copy in copies:
        copy.wait()


def step(
    unit_costs,
    hour_duals,
    inverse,
    weights,
    section_three,
    prev_first,
    prev_second,
    prev_third,
    eta_mean,
    eta_duals,
):
    scenarios, hours, columns = unit_costs.shape
    length = hours // 3
    nodes = lax.axis_size("node")
    dma = pltpu.SemaphoreType.DMA
    shape = jax.ShapeDtypeStruct
    block = (scenarios, length, columns)
    rows = scenarios * length
    w_row = weights.reshape(1, scenarios)
    duals_row = eta_duals.reshape(1, scenarios)
    costs, duals, matrix = in_hbm(unit_costs), in_hbm(hour_duals), in_hbm(inverse)

    y_third, y_second = partner((prev_third, prev_second), 2)

    w, sec, y1, c3, y3, inv_v, sol1, a1, mass, pick, cost = call(
        first_kernel,
        32,
        in_specs=[HBM] * 6,
        out_specs=[SMEM, SMEM] + [VMEM] * 9,
        out_shape=[
            pltpu.SMEM((scenarios,), jnp.int32),
            pltpu.SMEM((scenarios,), jnp.int32),
            *[pltpu.VMEM(block, BF16)] * 3,
            pltpu.VMEM(inverse.shape, BF16),
            pltpu.VMEM(block, F32),
            pltpu.VMEM((length, columns), F32),
            pltpu.VMEM((1, LANES), F32),
            pltpu.VMEM((BRANCH * length, rows), BF16),
            pltpu.VMEM((scenarios, length, LANES), F32),
        ],
        scratch_shapes=[
            pltpu.VMEM(block, BF16),
            pltpu.VMEM((length, columns), BF16),
            pltpu.VMEM((rows, columns), BF16),
            dma((9 + CHUNKS,)),
        ],
    )(in_hbm(weights), in_hbm(section_three), in_hbm(prev_first), costs, duals, matrix)

    level_mean, y_third = lax.optimization_barrier((eta_mean, y_third))
    low_row = level_mean[:, None] - (CVAR_WEIGHT + duals_row) / PENALTY
    core_third, diag_third = partner((prev_third, y_third), 1)
    core_second, diag_second = partner((prev_second, y_second), 1)

    c2, y2, sol3, cost, keep, send = call(
        third_kernel,
        30,
        in_specs=[SMEM, ANY, ANY, ANY, ANY, HBM, HBM] + [VMEM] * 5,
        out_specs=[VMEM] * 6,
        out_shape=[
            pltpu.VMEM(block, BF16),
            pltpu.VMEM(block, BF16),
            pltpu.VMEM(block, F32),
            pltpu.VMEM((scenarios, length, LANES), F32),
            pltpu.VMEM((HALF, length, columns), F32),
            pltpu.VMEM((HALF, length, columns), BF16),
        ],
        scratch_shapes=[
            pltpu.VMEM((rows, columns), BF16),
            pltpu.VMEM((BRANCH, length, columns), BF16),
            dma((6,)),
        ],
    )(sec, prev_third, core_third, y_third, diag_third, costs, duals, c3, y3, inv_v, pick, cost)

    chip_got = partner(send, 1)

    sol2, eta, sums = call(
        second_kernel,
        30,
        in_specs=[SMEM, VMEM, VMEM, ANY, ANY, ANY, ANY] + [VMEM] * 6,
        out_specs=[VMEM] * 3,
        out_shape=[
            pltpu.VMEM(block, F32),
            pltpu.VMEM((1, scenarios), F32),
            pltpu.VMEM((length, 2 * columns + 3 * LANES), BF16),
        ],
        scratch_shapes=[
            pltpu.VMEM((rows, columns), BF16),
            pltpu.VMEM((length, columns), BF16),
            pltpu.VMEM((scenarios, length, LANES), F32),
            dma((4,)),
        ],
    )(
        w, w_row, low_row, prev_second, core_second, y_second, diag_second, c2, y2, inv_v, cost, a1, mass
    )

    core_sums = partner(sums, 1)
    chip_total, chip_send, sums = call(
        chip_sum_kernel,
        8,
        in_specs=[VMEM] * 4,
        out_specs=[VMEM] * 3,
        out_shape=[
            pltpu.VMEM((HALF, length, columns), F32),
            pltpu.VMEM((HALF, length, columns), BF16),
            pltpu.VMEM(sums.shape, BF16),
        ],
    )(keep, chip_got, sums, core_sums)
    y_sums = partner(sums, 2)
    node_got = partner(chip_send, 2)
    far_shape = pltpu.VMEM((length, columns + 3 * LANES), BF16)
    far, a2, scal = call(
        node_sum_kernel,
        8,
        in_specs=[VMEM] * 2,
        out_specs=[VMEM] * 3,
        out_shape=[far_shape, pltpu.VMEM((length, columns), F32), pltpu.VMEM((length, LANES), F32)],
    )(sums, y_sums)
    far_got = partner(far, 4)
    mask = 8
    while mask < nodes:
        far = call(far_sum_kernel, 8, in_specs=[VMEM] * 2, out_specs=VMEM, out_shape=far_shape)(far, far_got)
        far_got = partner(far, mask)
        mask *= 2

    buf = pltpu.VMEM(block, BF16)
    duals_shape = shape(hour_duals.shape, BF16)
    out, second_avg = call(
        second_duals_kernel,
        8,
        in_specs=[VMEM] * 4,
        out_specs=[HBM, HBM],
        out_shape=[duals_shape, shape((1, length, columns // 4), F32)],
        scratch_shapes=[buf, pltpu.VMEM((length, columns), F32), dma((4,)), dma],
    )(sol2, y2, a2, scal)

    avg, avg_send, third_avg = call(
        third_avg_kernel,
        8,
        in_specs=[VMEM] * 3,
        out_specs=[VMEM, VMEM, HBM],
        out_shape=[
            pltpu.VMEM((HALF, length, columns), F32),
            pltpu.VMEM((HALF, length, columns), BF16),
            shape((SHARES, length, columns), F32),
        ],
        scratch_shapes=[dma],
    )(chip_total, node_got, scal)
    avg_got = partner(avg_send, 1)
    out = call(
        third_duals_kernel,
        8,
        in_specs=[SMEM] + [VMEM] * 4 + [HBM],
        out_specs=HBM,
        out_shape=duals_shape,
        scratch_shapes=[buf, pltpu.VMEM((BRANCH, length, columns), F32), dma((4,))],
        input_output_aliases={5: 0},
    )(sec, sol3, y3, avg, avg_got, out)
    out, first_avg, eta_avg, eta_duals_new = call(
        last_kernel,
        8,
        in_specs=[VMEM] * 6 + [HBM],
        out_specs=[HBM, HBM, SMEM, HBM],
        out_shape=[
            duals_shape,
            shape((length, columns), F32),
            shape((1,), F32),
            shape((1, scenarios), F32),
        ],
        scratch_shapes=[
            buf,
            pltpu.VMEM((length, columns), F32),
            pltpu.VMEM((1, scenarios), F32),
            dma((4,)),
            dma((2,)),
        ],
        input_output_aliases={6: 0},
    )(sol1, y1, far, far_got, eta, duals_row, out)
    return out, first_avg, second_avg, third_avg, eta_avg, eta_duals_new.reshape(scenarios)


def solution(mesh):
    row = P(("groups", "node"))
    in_specs = (row, row, P(), row, row, P("groups"), row, row, P("groups"), row)
    out_specs = (row, P("groups"), row, row, P("groups"), row)
    return jax.shard_map(step, mesh=mesh, in_specs=in_specs, out_specs=out_specs, check_vma=False)
```

```python
import jax
import jax.numpy as jnp
from jax import lax
from jax.experimental import pallas as pl
from jax.experimental.pallas import tpu as pltpu
from jax.sharding import PartitionSpec as P

BRANCH = 16
SHARES = BRANCH // 4
HALF = BRANCH // 2
PENALTY = 1.0
CVAR_WEIGHT = 0.25
CVAR_LEVEL = 0.75
CHUNKS = 4
LANES = 128
F32 = jnp.float32
BF16 = jnp.bfloat16

ANY = pl.BlockSpec(memory_space=pl.ANY)
HBM = pl.BlockSpec(memory_space=pltpu.HBM)
SMEM = pl.BlockSpec(memory_space=pltpu.SMEM)
VMEM = pl.BlockSpec(memory_space=pltpu.VMEM)


def partner(value, mask):
    pairs = [(source, source ^ mask) for source in range(lax.axis_size("node"))]
    return lax.ppermute(value, "node", pairs)


def in_hbm(value):
    return pltpu.with_memory_space_constraint(value, pltpu.HBM)


def call(kernel, mib, **kwargs):
    return pl.pallas_call(kernel, compiler_params=pltpu.CompilerParams(vmem_limit_bytes=mib << 20), **kwargs)


def quarter_of():
    return lax.axis_index("node") % 4


def place_of(node, quarter):
    half = (node // SHARES) % 2
    return ((half ^ (quarter % 2)) * 2 + node // (2 * SHARES)) * SHARES + node % SHARES


def build_target(target, anchor_of, c_v, y_v):
    scenarios, length, _ = c_v.shape

    def step(i, carry):
        rows = []
        for k in range(2):
            s = 2 * i + k
            rows.append(PENALTY * anchor_of(s).astype(F32) - c_v[s].astype(F32) - y_v[s].astype(F32))
        block = jnp.concatenate(rows, axis=0).astype(BF16)
        target[pl.ds(pl.multiple_of(i * 2 * length, 2 * length), 2 * length), :] = block
        return carry

    lax.fori_loop(0, scenarios // 2, step, 0, unroll=2)


def multiply(target, inv_v, sol, c_v, cost, before, w, after, start=0):
    scenarios, length, columns = sol.shape
    width = inv_v.shape[1] // CHUNKS

    def product(j):
        before(j)
        sol[:, :, j * width : (j + 1) * width] = jnp.dot(
            target[...], inv_v[:, start + j * width : start + (j + 1) * width], preferred_element_type=F32
        ).reshape(scenarios, length, width)

    def finish(j):
        cols = slice(j * width, (j + 1) * width)
        total = jnp.zeros((length, width), F32)
        for s in range(scenarios):
            own = sol[s, :, cols]
            prod = c_v[s, :, start + cols.start : start + cols.stop].astype(F32) * own
            part = prod[:, :LANES]
            for k in range(1, width // LANES):
                part = part + prod[:, k * LANES : (k + 1) * LANES]
            cost[s] = cost[s] + part
            if w is not None:
                total = total + w[s].astype(F32) * own
        after(cols, total)

    count = columns // width
    for j in range(count):
        product(j)
        if j:
            finish(j - 1)
    finish(count - 1)


def first_kernel(
    w_hbm, sec_hbm, w_row_hbm, sec_row_hbm, pf_hbm, c_hbm, y_hbm, inv_hbm,
    w, sec, y1, c2, y2, c3, y3, inv_v, sol, a1, mass, pick, cost, c1, pf, w_row, sec_row, target, sems,
):
    scenarios, length, columns = sol.shape
    width = columns // CHUNKS

    def chunk(j):
        part = pl.ds(j * width, width)
        return pltpu.make_async_copy(inv_hbm.at[:, part], inv_v.at[:, part], sems.at[11 + j])

    def rows(k, c_v, y_v):
        own = pl.ds(k * length, length)
        return [
            pltpu.make_async_copy(c_hbm.at[:, own, :], c_v, sems.at[5 + 2 * k]),
            pltpu.make_async_copy(y_hbm.at[:, own, :], y_v, sems.at[6 + 2 * k]),
        ]

    small = [
        pltpu.make_async_copy(source, into, sems.at[k])
        for k, (source, into) in enumerate(
            ((w_row_hbm, w_row), (sec_row_hbm, sec_row), (w_hbm, w), (sec_hbm, sec), (pf_hbm, pf))
        )
    ]
    first = rows(0, c1, y1)
    later = rows(2, c3, y3) + rows(1, c2, y2)
    for copy in small + first + [chunk(j) for j in range(CHUNKS)] + later:
        copy.start()
    cost[...] = jnp.zeros_like(cost)
    for copy in small:
        copy.wait()

    node = sec_row[...] % BRANCH
    place = place_of(node, quarter_of())
    p = w_row[...].astype(F32)
    into_node = lax.broadcasted_iota(jnp.int32, (LANES, scenarios), 0) == node
    mass[...] = jnp.sum(jnp.where(into_node, p, 0.0).T, axis=0, keepdims=True)
    into_place = lax.broadcasted_iota(jnp.int32, (BRANCH * length, scenarios), 0) // length == place
    shape = (scenarios, scenarios * length)
    spread = lax.broadcasted_iota(jnp.int32, shape, 1) // length == lax.broadcasted_iota(jnp.int32, shape, 0)
    weight = jnp.dot(
        jnp.where(into_place, p, 0.0).astype(BF16),
        jnp.where(spread, 1.0, 0.0).astype(BF16),
        preferred_element_type=F32,
    )
    row = lax.broadcasted_iota(jnp.int32, pick.shape, 0)
    column = lax.broadcasted_iota(jnp.int32, pick.shape, 1)
    pick[...] = jnp.where(row % length == column % length, weight, 0.0).astype(BF16)

    for copy in first:
        copy.wait()
    build_target(target, lambda s: pf[...], c1, y1)

    def after(cols, total):
        a1[:, cols] = total

    multiply(target, inv_v, sol, c1, cost, lambda j: chunk(j).wait(), w, after)
    for copy in later:
        copy.wait()


def packed(value):
    high = value.astype(BF16)
    rest = value - high.astype(F32)
    middle = rest.astype(BF16)
    return jnp.concatenate((high, middle, (rest - middle.astype(F32)).astype(BF16)), axis=1)


def unpacked(tiles):
    high, middle, low = (tiles[:, k * LANES : (k + 1) * LANES].astype(F32) for k in range(3))
    return high + middle + low


def node_mass(scal, node):
    row = scal[2:3, :]
    slot = lax.broadcasted_iota(jnp.int32, row.shape, 1)
    return jnp.sum(jnp.where(slot == node, row, 0.0), axis=1, keepdims=True)


def third_kernel(
    sec, p0, p1, p2, p3, c_v, y_v, inv_v, pick, cost_in, sol, cost, keep, send, target, table
):
    scenarios, length, _ = sol.shape
    quarter = quarter_of()
    cost[...] = cost_in[...]
    for k, part in enumerate((p0, p1, p2, p3)):
        table[k * SHARES : (k + 1) * SHARES] = part[:SHARES]

    def anchor_of(s):
        node = sec[s] % BRANCH
        return table[((node // SHARES) ^ quarter) * SHARES + node % SHARES]

    build_target(target, anchor_of, c_v, y_v)

    def after(cols, total):
        own = sol[:, :, cols]
        flat = own.reshape(scenarios * length, own.shape[2]).astype(BF16)
        sums = jnp.dot(pick[...], flat, preferred_element_type=F32).reshape(BRANCH, length, own.shape[2])
        keep[:, :, cols] = sums[:HALF]
        send[:, :, cols] = sums[HALF:].astype(BF16)

    multiply(target, inv_v, sol, c_v, cost, lambda j: None, None, after)


def left_kernel(w, p0, p1, p2, p3, c_v, y_v, inv_v, cost_in, target, sol, a2, cost, table):
    share = table.shape[1] // 4
    quarter = quarter_of()
    cost[...] = cost_in[...]
    for k, part in enumerate((p0, p1, p2, p3)):
        table[:, pl.ds(pl.multiple_of((quarter ^ k) * share, share), share)] = part[SHARES, :, :share]
    build_target(target, lambda s: table[...], c_v, y_v)

    def after(cols, total):
        a2[:, cols] = total

    multiply(target, inv_v, sol, c_v, cost, lambda j: None, w, after)


def right_kernel(w, w_row, level_row, target, c_v, inv_v, cost_in, a1, a2, mass, sol, eta, sums, cost):
    scenarios, length, half = sol.shape
    columns = 2 * half
    cost[...] = cost_in[...]
    sums[:, :columns] = a1[...].astype(BF16)
    sums[:, columns : columns + half] = a2[...].astype(BF16)

    def after(cols, total):
        first = columns + half + cols.start
        sums[:, first : first + cols.stop - cols.start] = total.astype(BF16)

    multiply(target, inv_v, sol, c_v, cost, lambda j: None, w, after, half)
    lanes = jnp.sum(cost[...], axis=1)
    scen_cost = jnp.sum(lanes.T, axis=0, keepdims=True) / (3 * length * columns)
    p = w_row[...].astype(F32)
    low = level_row[:, scenarios:] - (CVAR_WEIGHT + level_row[:, :scenarios]) / PENALTY
    high = low + CVAR_WEIGHT / ((1.0 - CVAR_LEVEL) * PENALTY)
    level = jnp.minimum(jnp.maximum(scen_cost, low), high)
    eta[...] = level
    total = jnp.sum(p * level, axis=1, keepdims=True)
    whole = jnp.sum(p, axis=1, keepdims=True)
    row = lax.broadcasted_iota(jnp.int32, (length, LANES), 0)
    scal = jnp.where(row == 0, total, jnp.where(row == 1, whole, jnp.where(row == 2, mass[...], 0.0)))
    sums[:, 2 * columns :] = packed(scal)


def chip_sum_kernel(keep, got, total, send1, send2):
    cut = send1.shape[0]
    value = keep[...] + got[...].astype(F32)
    total[...] = value
    send1[...] = value[:cut].astype(BF16)
    send2[...] = value[cut:].astype(BF16)


def node_sum_kernel(s_own, s_got, sums, a2, scal):
    columns = a2.shape[1]
    sums[:, :columns] = (s_own[:, :columns].astype(F32) + s_got[:, :columns].astype(F32)).astype(BF16)
    a2[...] = s_own[:, columns : 2 * columns].astype(F32) + s_got[:, columns : 2 * columns].astype(F32)
    value = unpacked(s_own[:, 2 * columns :]) + unpacked(s_got[:, 2 * columns :])
    scal[...] = value
    sums[:, columns:] = packed(value)


def far_sum_kernel(s_own, s_got, sums):
    columns = sums.shape[1] - 3 * LANES
    sums[:, :columns] = (s_own[:, :columns].astype(F32) + s_got[:, :columns].astype(F32)).astype(BF16)
    sums[:, columns:] = packed(unpacked(s_own[:, columns:]) + unpacked(s_got[:, columns:]))


def third_avg_kernel(total, got1, got2, scal, avg, send):
    quarter = quarter_of()
    cut = got1.shape[0]
    for k in range(HALF):
        node = ((k // SHARES) * 2 + quarter % 2) * SHARES + k % SHARES
        got = got1[k] if k < cut else got2[k - cut]
        value = (total[k] + got.astype(F32)) / node_mass(scal, node)
        avg[k] = value
        send[k] = value.astype(BF16)


def write_duals(sols, y_v, avg_of, out, buf, sems, section):
    scenarios, length, _ = y_v.shape
    group = scenarios // 4

    def copy(g):
        own = pl.ds(g * group, group)
        return pltpu.make_async_copy(
            buf.at[own], out.at[own, pl.ds(section * length, length), :], sems.at[g]
        )

    for g in range(4):

        def step(i, carry):
            s = g * group + i
            avg = avg_of(s)
            start = 0
            for sol in sols:
                cols = slice(start, start + sol.shape[2])
                fresh = y_v[s, :, cols].astype(F32) + PENALTY * (sol[s] - avg[:, cols])
                buf[s, :, cols] = fresh.astype(BF16)
                start = cols.stop
            return carry

        lax.fori_loop(0, group, step, 0, unroll=4)
        copy(g).start()
    return [copy(g) for g in range(4)]


def second_duals_kernel(left, right, y_v, a2, scal, out, second_avg, buf, full, sems, sem):
    _, columns = full.shape
    quarter = quarter_of()
    share = columns // 4
    full[...] = a2[...] / jnp.sum(scal[2:3, :], axis=1, keepdims=True)
    own = pl.ds(pl.multiple_of(quarter * share, share), share)
    copy = pltpu.make_async_copy(full.at[:, own], second_avg.at[0], sem)
    copy.start()
    for other in write_duals((left, right), y_v, lambda s: full[...], out, buf, sems, 1):
        other.wait()
    copy.wait()


def third_duals_kernel(sec, sol, y_v, avg, got, prior, out, third_avg, buf, table, sems, sem):
    quarter = quarter_of()
    copy = pltpu.make_async_copy(avg.at[pl.ds((quarter // 2) * SHARES, SHARES)], third_avg, sem)
    copy.start()
    table[:HALF] = avg[...]
    table[HALF:] = got[...].astype(F32)
    for other in write_duals(
        (sol,), y_v, lambda s: table[place_of(sec[s] % BRANCH, quarter)], out, buf, sems, 2
    ):
        other.wait()
    copy.wait()


def last_kernel(
    sol, y_v, s_own, s_got, eta, duals_row, prior,
    out, first_avg, eta_avg, eta_duals, buf, full, row, one, sems, sems2,
):
    columns = full.shape[1]
    scal = unpacked(s_own[:, columns:]) + unpacked(s_got[:, columns:])
    total, mass = scal[0:1, 0:1], scal[1:2, 0:1]
    full[...] = (s_own[:, :columns].astype(F32) + s_got[:, :columns].astype(F32)) / mass
    level = total / mass
    row[...] = duals_row[...] + PENALTY * (eta[...] - level)
    one[0] = jnp.sum(level)
    copies = [
        pltpu.make_async_copy(full, first_avg, sems2.at[0]),
        pltpu.make_async_copy(row, eta_duals, sems2.at[1]),
        pltpu.make_async_copy(one, eta_avg, sems2.at[2]),
    ]
    for copy in copies:
        copy.start()
    copies += write_duals((sol,), y_v, lambda s: full[...], out, buf, sems, 0)
    for copy in copies:
        copy.wait()


def step(
    unit_costs,
    hour_duals,
    inverse,
    weights,
    section_three,
    prev_first,
    prev_second,
    prev_third,
    eta_mean,
    eta_duals,
):
    scenarios, hours, columns = unit_costs.shape
    length = hours // 3
    nodes = lax.axis_size("node")
    dma = pltpu.SemaphoreType.DMA
    shape = jax.ShapeDtypeStruct
    block = (scenarios, length, columns)
    rows = scenarios * length
    w_row = weights.reshape(1, scenarios)
    duals_row = eta_duals.reshape(1, scenarios)
    costs, duals, matrix = in_hbm(unit_costs), in_hbm(hour_duals), in_hbm(inverse)

    tail = jnp.pad(prev_second, ((0, 0), (0, 0), (0, columns - columns // 4)))
    prev = jnp.concatenate((prev_third, tail))
    y_prev = partner(prev, 2)

    w, sec, y1, c2, y2, c3, y3, inv_v, sol1, a1, mass, pick, cost = call(
        first_kernel,
        32,
        in_specs=[HBM] * 8,
        out_specs=[SMEM, SMEM] + [VMEM] * 11,
        out_shape=[
            pltpu.SMEM((scenarios,), jnp.int32),
            pltpu.SMEM((scenarios,), jnp.int32),
            *[pltpu.VMEM(block, BF16)] * 5,
            pltpu.VMEM(inverse.shape, BF16),
            pltpu.VMEM(block, F32),
            pltpu.VMEM((length, columns), F32),
            pltpu.VMEM((1, LANES), F32),
            pltpu.VMEM((BRANCH * length, rows), BF16),
            pltpu.VMEM((scenarios, length, LANES), F32),
        ],
        scratch_shapes=[
            pltpu.VMEM(block, BF16),
            pltpu.VMEM((length, columns), BF16),
            pltpu.VMEM((1, scenarios), jnp.int32),
            pltpu.VMEM((1, scenarios), jnp.int32),
            pltpu.VMEM((rows, columns), BF16),
            dma((11 + CHUNKS,)),
        ],
    )(
        in_hbm(weights),
        in_hbm(section_three),
        in_hbm(w_row),
        in_hbm(section_three.reshape(1, scenarios)),
        in_hbm(prev_first),
        costs,
        duals,
        matrix,
    )

    y_prev, joined = lax.optimization_barrier((y_prev, (eta_mean, eta_duals)))
    level_row = jnp.concatenate((joined[1], joined[0])).reshape(1, scenarios + 1)
    core_prev, diag_prev = partner((prev, y_prev), 1)
    pieces = (prev, core_prev, y_prev, diag_prev)

    sol3, cost, keep, send = call(
        third_kernel,
        30,
        in_specs=[SMEM] + [VMEM] * 9,
        out_specs=[VMEM] * 4,
        out_shape=[
            pltpu.VMEM(block, F32),
            pltpu.VMEM((scenarios, length, LANES), F32),
            pltpu.VMEM((HALF, length, columns), F32),
            pltpu.VMEM((HALF, length, columns), BF16),
        ],
        scratch_shapes=[pltpu.VMEM((rows, columns), BF16), pltpu.VMEM((BRANCH, length, columns), BF16)],
    )(sec, *pieces, c3, y3, inv_v, pick, cost)

    chip_got = partner(send, 1)
    half_block = (scenarios, length, columns // 2)
    target2, left, a2, cost = call(
        left_kernel,
        30,
        in_specs=[SMEM] + [VMEM] * 8,
        out_specs=[VMEM] * 4,
        out_shape=[
            pltpu.VMEM((rows, columns), BF16),
            pltpu.VMEM(half_block, F32),
            pltpu.VMEM((length, columns // 2), F32),
            pltpu.VMEM((scenarios, length, LANES), F32),
        ],
        scratch_shapes=[pltpu.VMEM((length, columns), BF16)],
    )(w, *pieces, c2, y2, inv_v, cost)
    cut = HALF // 2
    chip_total, chip_send1, chip_send2 = call(
        chip_sum_kernel,
        8,
        in_specs=[VMEM] * 2,
        out_specs=[VMEM] * 3,
        out_shape=[
            pltpu.VMEM((HALF, length, columns), F32),
            pltpu.VMEM((cut, length, columns), BF16),
            pltpu.VMEM((HALF - cut, length, columns), BF16),
        ],
    )(keep, chip_got)
    node_got1 = partner(chip_send1, 2)

    right, eta, sums = call(
        right_kernel,
        30,
        in_specs=[SMEM] + [VMEM] * 9,
        out_specs=[VMEM] * 3,
        out_shape=[
            pltpu.VMEM(half_block, F32),
            pltpu.VMEM((1, scenarios), F32),
            pltpu.VMEM((length, 2 * columns + 3 * LANES), BF16),
        ],
        scratch_shapes=[pltpu.VMEM((scenarios, length, LANES), F32)],
    )(w, w_row, level_row, target2, c2, inv_v, cost, a1, a2, mass)

    core_sums = partner(sums, 1)
    sums = call(
        far_sum_kernel, 8, in_specs=[VMEM] * 2, out_specs=VMEM, out_shape=pltpu.VMEM(sums.shape, BF16)
    )(sums, core_sums)
    y_sums = partner(sums, 2)
    node_got2 = partner(chip_send2, 2)
    far_shape = pltpu.VMEM((length, columns + 3 * LANES), BF16)
    far, a2, scal = call(
        node_sum_kernel,
        8,
        in_specs=[VMEM] * 2,
        out_specs=[VMEM] * 3,
        out_shape=[far_shape, pltpu.VMEM((length, columns), F32), pltpu.VMEM((length, LANES), F32)],
    )(sums, y_sums)
    far_got = partner(far, 4)
    mask = 8
    while mask < nodes:
        far = call(far_sum_kernel, 8, in_specs=[VMEM] * 2, out_specs=VMEM, out_shape=far_shape)(far, far_got)
        far_got = partner(far, mask)
        mask *= 2

    buf = pltpu.VMEM(block, BF16)
    duals_shape = shape(hour_duals.shape, BF16)
    out, second_avg = call(
        second_duals_kernel,
        8,
        in_specs=[VMEM] * 5,
        out_specs=[HBM, HBM],
        out_shape=[duals_shape, shape((1, length, columns // 4), F32)],
        scratch_shapes=[buf, pltpu.VMEM((length, columns), F32), dma((4,)), dma],
    )(left, right, y2, a2, scal)

    avg, avg_send = call(
        third_avg_kernel,
        8,
        in_specs=[VMEM] * 4,
        out_specs=[VMEM] * 2,
        out_shape=[
            pltpu.VMEM((HALF, length, columns), F32),
            pltpu.VMEM((HALF, length, columns), BF16),
        ],
    )(chip_total, node_got1, node_got2, scal)
    avg_got = partner(avg_send, 1)
    out, third_avg = call(
        third_duals_kernel,
        8,
        in_specs=[SMEM] + [VMEM] * 4 + [HBM],
        out_specs=[HBM, HBM],
        out_shape=[duals_shape, shape((SHARES, length, columns), F32)],
        scratch_shapes=[buf, pltpu.VMEM((BRANCH, length, columns), F32), dma((4,)), dma],
        input_output_aliases={5: 0},
    )(sec, sol3, y3, avg, avg_got, out)
    out, first_avg, eta_avg, eta_duals_new = call(
        last_kernel,
        8,
        in_specs=[VMEM] * 6 + [HBM],
        out_specs=[HBM] * 4,
        out_shape=[
            duals_shape,
            shape((length, columns), F32),
            shape((1,), F32),
            shape((1, scenarios), F32),
        ],
        scratch_shapes=[
            buf,
            pltpu.VMEM((length, columns), F32),
            pltpu.VMEM((1, scenarios), F32),
            pltpu.SMEM((1,), F32),
            dma((4,)),
            dma((3,)),
        ],
        input_output_aliases={6: 0},
    )(sol1, y1, far, far_got, eta, duals_row, out)
    return out, first_avg, second_avg, third_avg, eta_avg, eta_duals_new.reshape(scenarios)


def solution(mesh):
    row = P(("groups", "node"))
    in_specs = (row, row, P(), row, row, P("groups"), row, row, P("groups"), row)
    out_specs = (row, P("groups"), row, row, P("groups"), row)
    return jax.shard_map(step, mesh=mesh, in_specs=in_specs, out_specs=out_specs, check_vma=False)
```

```python
import jax
import jax.numpy as jnp
from jax import lax
from jax.experimental import pallas as pl
from jax.experimental.pallas import tpu as pltpu
from jax.sharding import PartitionSpec as P

BRANCH = 16
SHARES = BRANCH // 4
HALF = BRANCH // 2
PENALTY = 1.0
CVAR_WEIGHT = 0.25
CVAR_LEVEL = 0.75
CHUNKS = 4
LANES = 128
F32 = jnp.float32
BF16 = jnp.bfloat16

ANY = pl.BlockSpec(memory_space=pl.ANY)
HBM = pl.BlockSpec(memory_space=pltpu.HBM)
SMEM = pl.BlockSpec(memory_space=pltpu.SMEM)
VMEM = pl.BlockSpec(memory_space=pltpu.VMEM)


def partner(value, mask):
    pairs = [(source, source ^ mask) for source in range(lax.axis_size("node"))]
    return lax.ppermute(value, "node", pairs)


def in_hbm(value):
    return pltpu.with_memory_space_constraint(value, pltpu.HBM)


def call(kernel, mib, **kwargs):
    return pl.pallas_call(kernel, compiler_params=pltpu.CompilerParams(vmem_limit_bytes=mib << 20), **kwargs)


def quarter_of():
    return lax.axis_index("node") % 4


def place_of(node, quarter):
    half = (node // SHARES) % 2
    return ((half ^ (quarter % 2)) * 2 + node // (2 * SHARES)) * SHARES + node % SHARES


def build_target(target, anchor_of, c_v, y_v):
    scenarios, length, _ = c_v.shape

    def step(i, carry):
        rows = []
        for k in range(2):
            s = 2 * i + k
            rows.append(PENALTY * anchor_of(s).astype(F32) - c_v[s].astype(F32) - y_v[s].astype(F32))
        block = jnp.concatenate(rows, axis=0).astype(BF16)
        target[pl.ds(pl.multiple_of(i * 2 * length, 2 * length), 2 * length), :] = block
        return carry

    lax.fori_loop(0, scenarios // 2, step, 0, unroll=2)


def multiply(target, inv_v, sol, c_v, cost, before, w, after, start=0):
    scenarios, length, columns = sol.shape
    width = inv_v.shape[1] // CHUNKS

    def product(j):
        before(j)
        sol[:, :, j * width : (j + 1) * width] = jnp.dot(
            target[...], inv_v[:, start + j * width : start + (j + 1) * width], preferred_element_type=F32
        ).reshape(scenarios, length, width)

    def finish(j):
        cols = slice(j * width, (j + 1) * width)
        total = jnp.zeros((length, width), F32)
        for s in range(scenarios):
            own = sol[s, :, cols]
            prod = c_v[s, :, start + cols.start : start + cols.stop].astype(F32) * own
            part = prod[:, :LANES]
            for k in range(1, width // LANES):
                part = part + prod[:, k * LANES : (k + 1) * LANES]
            cost[s] = cost[s] + part
            if w is not None:
                total = total + w[s].astype(F32) * own
        after(cols, total)

    count = columns // width
    for j in range(count):
        product(j)
        if j:
            finish(j - 1)
    finish(count - 1)


def join_kernel(third, second, joined, sems):
    shares, share = third.shape[0], second.shape[2]
    copies = [
        pltpu.make_async_copy(third, joined.at[pl.ds(0, shares)], sems.at[0]),
        pltpu.make_async_copy(second.at[0], joined.at[shares, :, pl.ds(0, share)], sems.at[1]),
    ]
    for copy in copies:
        copy.start()
    for copy in copies:
        copy.wait()


def section_rows(c_hbm, y_hbm, c_v, y_v, sems, section):
    length = c_v.shape[1]
    own = pl.ds(section * length, length)
    return [
        pltpu.make_async_copy(c_hbm.at[:, own, :], c_v, sems.at[0]),
        pltpu.make_async_copy(y_hbm.at[:, own, :], y_v, sems.at[1]),
    ]


def first_kernel(
    w_hbm, sec_hbm, w_row_hbm, sec_row_hbm, pf_hbm, c_hbm, y_hbm, inv_hbm,
    w, sec, c1, y1, inv_v, sol, a1, mass, pick, cost, target, pf, w_row, sec_row, sems, row_sems,
):
    scenarios, length, columns = c1.shape
    width = columns // CHUNKS

    def chunk(j):
        part = pl.ds(j * width, width)
        return pltpu.make_async_copy(inv_hbm.at[:, part], inv_v.at[:, part], sems.at[5 + j])

    small = [
        pltpu.make_async_copy(source, into, sems.at[k])
        for k, (source, into) in enumerate(
            ((w_row_hbm, w_row), (sec_row_hbm, sec_row), (w_hbm, w), (sec_hbm, sec), (pf_hbm, pf))
        )
    ]
    first = section_rows(c_hbm, y_hbm, c1, y1, row_sems, 0)
    for copy in small + first + [chunk(j) for j in range(CHUNKS)]:
        copy.start()
    cost[...] = jnp.zeros_like(cost)
    for copy in small:
        copy.wait()

    node = sec_row[...] % BRANCH
    place = place_of(node, quarter_of())
    p = w_row[...].astype(F32)
    into_node = lax.broadcasted_iota(jnp.int32, (LANES, scenarios), 0) == node
    mass[...] = jnp.sum(jnp.where(into_node, p, 0.0).T, axis=0, keepdims=True)
    into_place = lax.broadcasted_iota(jnp.int32, (BRANCH * length, scenarios), 0) // length == place
    shape = (scenarios, scenarios * length)
    spread = lax.broadcasted_iota(jnp.int32, shape, 1) // length == lax.broadcasted_iota(jnp.int32, shape, 0)
    weight = jnp.dot(
        jnp.where(into_place, p, 0.0).astype(BF16),
        jnp.where(spread, 1.0, 0.0).astype(BF16),
        preferred_element_type=F32,
    )
    row = lax.broadcasted_iota(jnp.int32, pick.shape, 0)
    column = lax.broadcasted_iota(jnp.int32, pick.shape, 1)
    pick[...] = jnp.where(row % length == column % length, weight, 0.0).astype(BF16)

    for copy in first:
        copy.wait()
    build_target(target, lambda s: pf[...], c1, y1)

    def after(cols, total):
        a1[:, cols] = total

    multiply(target, inv_v, sol, c1, cost, lambda j: chunk(j).wait(), w, after)
    chunk(CHUNKS - 1).wait()


def rest_kernel(w, target, c1, inv_v, cost_in, c_hbm, y_hbm, c3, y3, sol, a1, cost, sems):
    ahead = section_rows(c_hbm, y_hbm, c3, y3, sems, 2)
    for copy in ahead:
        copy.start()
    cost[...] = cost_in[...]

    def after(cols, total):
        a1[:, cols] = total

    multiply(target, inv_v, sol, c1, cost, lambda j: None, w, after, c1.shape[2] - sol.shape[2])
    for copy in ahead:
        copy.wait()


def packed(value):
    high = value.astype(BF16)
    rest = value - high.astype(F32)
    middle = rest.astype(BF16)
    return jnp.concatenate((high, middle, (rest - middle.astype(F32)).astype(BF16)), axis=1)


def unpacked(tiles):
    high, middle, low = (tiles[:, k * LANES : (k + 1) * LANES].astype(F32) for k in range(3))
    return high + middle + low


def node_mass(scal, node):
    row = scal[2:3, :]
    slot = lax.broadcasted_iota(jnp.int32, row.shape, 1)
    return jnp.sum(jnp.where(slot == node, row, 0.0), axis=1, keepdims=True)


def third_kernel(
    sec, p0, p1, p2, p3, c_v, y_v, inv_v, pick, cost_in, a_left, a_right, c_hbm, y_hbm,
    c2, y2, sol, cost, keep, send, target, table, sems,
):
    scenarios, length, _ = sol.shape
    quarter = quarter_of()
    ahead = section_rows(c_hbm, y_hbm, c2, y2, sems, 1)
    for copy in ahead:
        copy.start()
    cut = a_left.shape[1]
    send[HALF, :, :cut] = a_left[...].astype(BF16)
    send[HALF, :, cut:] = a_right[...].astype(BF16)
    cost[...] = cost_in[...]
    for k, part in enumerate((p0, p1, p2, p3)):
        table[k * SHARES : (k + 1) * SHARES] = part[:SHARES]

    def anchor_of(s):
        node = sec[s] % BRANCH
        return table[((node // SHARES) ^ quarter) * SHARES + node % SHARES]

    build_target(target, anchor_of, c_v, y_v)

    def after(cols, total):
        own = sol[:, :, cols]
        flat = own.reshape(scenarios * length, own.shape[2]).astype(BF16)
        sums = jnp.dot(pick[...], flat, preferred_element_type=F32).reshape(BRANCH, length, own.shape[2])
        keep[:, :, cols] = sums[:HALF]
        send[:HALF, :, cols] = sums[HALF:].astype(BF16)

    multiply(target, inv_v, sol, c_v, cost, lambda j: None, None, after)
    for copy in ahead:
        copy.wait()


def left_kernel(w, p0, p1, p2, p3, c_v, y_v, inv_v, cost_in, target, sol, a2, cost, table):
    share = table.shape[1] // 4
    quarter = quarter_of()
    cost[...] = cost_in[...]
    for k, part in enumerate((p0, p1, p2, p3)):
        table[:, pl.ds(pl.multiple_of((quarter ^ k) * share, share), share)] = part[SHARES, :, :share]
    build_target(target, lambda s: table[...], c_v, y_v)

    def after(cols, total):
        a2[:, cols] = total

    multiply(target, inv_v, sol, c_v, cost, lambda j: None, w, after)


def right_kernel(w, w_row, mean, duals_row, target, c_v, inv_v, cost_in, a2, mass, sol, eta, sums, cost):
    _, length, half = sol.shape
    columns = 2 * half
    cost[...] = cost_in[...]
    sums[:, :half] = a2[...].astype(BF16)

    def after(cols, total):
        sums[:, half + cols.start : half + cols.stop] = total.astype(BF16)

    multiply(target, inv_v, sol, c_v, cost, lambda j: None, w, after, half)
    lanes = jnp.sum(cost[...], axis=1)
    scen_cost = jnp.sum(lanes.T, axis=0, keepdims=True) / (3 * length * columns)
    p = w_row[...].astype(F32)
    low = mean[...] - (CVAR_WEIGHT + duals_row[...]) / PENALTY
    high = low + CVAR_WEIGHT / ((1.0 - CVAR_LEVEL) * PENALTY)
    level = jnp.minimum(jnp.maximum(scen_cost, low), high)
    eta[...] = level
    total = jnp.sum(p * level, axis=1, keepdims=True)
    whole = jnp.sum(p, axis=1, keepdims=True)
    row = lax.broadcasted_iota(jnp.int32, (length, LANES), 0)
    scal = jnp.where(row == 0, total, jnp.where(row == 1, whole, jnp.where(row == 2, mass[...], 0.0)))
    sums[:, columns:] = packed(scal)


def chip_sum_kernel(keep, sent, got, total, send1, send2):
    half = keep.shape[0]
    cut = half - send2.shape[0]
    value = keep[...] + got[:half].astype(F32)
    total[...] = value
    send1[:cut] = value[:cut].astype(BF16)
    send1[cut] = (sent[half].astype(F32) + got[half].astype(F32)).astype(BF16)
    send2[...] = value[cut:].astype(BF16)


def node_sum_kernel(s_own, s_got, sent, got, sums, a2, scal):
    columns = a2.shape[1]
    last = sent.shape[0] - 1
    sums[:, :columns] = (sent[last].astype(F32) + got[last].astype(F32)).astype(BF16)
    a2[...] = s_own[:, :columns].astype(F32) + s_got[:, :columns].astype(F32)
    value = unpacked(s_own[:, columns:]) + unpacked(s_got[:, columns:])
    scal[...] = value
    sums[:, columns:] = packed(value)


def far_sum_kernel(s_own, s_got, sums):
    columns = sums.shape[1] - 3 * LANES
    sums[:, :columns] = (s_own[:, :columns].astype(F32) + s_got[:, :columns].astype(F32)).astype(BF16)
    sums[:, columns:] = packed(unpacked(s_own[:, columns:]) + unpacked(s_got[:, columns:]))


def third_avg_kernel(total, got1, got2, scal, avg, send):
    quarter = quarter_of()
    cut = total.shape[0] - got2.shape[0]
    for k in range(HALF):
        node = ((k // SHARES) * 2 + quarter % 2) * SHARES + k % SHARES
        got = got1[k] if k < cut else got2[k - cut]
        value = (total[k] + got.astype(F32)) / node_mass(scal, node)
        avg[k] = value
        send[k] = value.astype(BF16)


def write_duals(sols, y_v, avg_of, out, buf, sems, section):
    scenarios, length, _ = y_v.shape
    group = scenarios // 4

    def copy(g):
        own = pl.ds(g * group, group)
        return pltpu.make_async_copy(
            buf.at[own], out.at[own, pl.ds(section * length, length), :], sems.at[g]
        )

    for g in range(4):

        def step(i, carry):
            s = g * group + i
            avg = avg_of(s)
            start = 0
            for sol in sols:
                cols = slice(start, start + sol.shape[2])
                fresh = y_v[s, :, cols].astype(F32) + PENALTY * (sol[s] - avg[:, cols])
                buf[s, :, cols] = fresh.astype(BF16)
                start = cols.stop
            return carry

        lax.fori_loop(0, group, step, 0, unroll=4)
        copy(g).start()
    return [copy(g) for g in range(4)]


def second_duals_kernel(left, right, y_v, a2, scal, out, second_avg, buf, full, sems, sem):
    _, columns = full.shape
    quarter = quarter_of()
    share = columns // 4
    full[...] = a2[...] / jnp.sum(scal[2:3, :], axis=1, keepdims=True)
    own = pl.ds(pl.multiple_of(quarter * share, share), share)
    copy = pltpu.make_async_copy(full.at[:, own], second_avg.at[0], sem)
    copy.start()
    for other in write_duals((left, right), y_v, lambda s: full[...], out, buf, sems, 1):
        other.wait()
    copy.wait()


def third_duals_kernel(sec, sol, y_v, avg, got, prior, out, third_avg, buf, table, sems, sem):
    quarter = quarter_of()
    copy = pltpu.make_async_copy(avg.at[pl.ds((quarter // 2) * SHARES, SHARES)], third_avg, sem)
    copy.start()
    table[:HALF] = avg[...]
    table[HALF:] = got[...].astype(F32)
    for other in write_duals(
        (sol,), y_v, lambda s: table[place_of(sec[s] % BRANCH, quarter)], out, buf, sems, 2
    ):
        other.wait()
    copy.wait()


def last_kernel(
    left, right, y_v, s_own, s_got, eta, duals_row, prior,
    out, first_avg, eta_avg, eta_duals, buf, full, row, one, sems, sems2,
):
    columns = full.shape[1]
    scal = unpacked(s_own[:, columns:]) + unpacked(s_got[:, columns:])
    total, mass = scal[0:1, 0:1], scal[1:2, 0:1]
    full[...] = (s_own[:, :columns].astype(F32) + s_got[:, :columns].astype(F32)) / mass
    level = total / mass
    row[...] = duals_row[...] + PENALTY * (eta[...] - level)
    one[0] = jnp.sum(level)
    copies = [
        pltpu.make_async_copy(full, first_avg, sems2.at[0]),
        pltpu.make_async_copy(row, eta_duals, sems2.at[1]),
        pltpu.make_async_copy(one, eta_avg, sems2.at[2]),
    ]
    for copy in copies:
        copy.start()
    copies += write_duals((left, right), y_v, lambda s: full[...], out, buf, sems, 0)
    for copy in copies:
        copy.wait()


def step(
    unit_costs,
    hour_duals,
    inverse,
    weights,
    section_three,
    prev_first,
    prev_second,
    prev_third,
    eta_mean,
    eta_duals,
):
    scenarios, hours, columns = unit_costs.shape
    length = hours // 3
    nodes = lax.axis_size("node")
    dma = pltpu.SemaphoreType.DMA
    shape = jax.ShapeDtypeStruct
    block = (scenarios, length, columns)
    rows = scenarios * length
    w_row = weights.reshape(1, scenarios)
    duals_row = eta_duals.reshape(1, scenarios)
    costs, duals, matrix = in_hbm(unit_costs), in_hbm(hour_duals), in_hbm(inverse)

    prev = call(
        join_kernel,
        8,
        in_specs=[HBM, HBM],
        out_specs=VMEM,
        out_shape=pltpu.VMEM((SHARES + 1, length, columns), BF16),
        scratch_shapes=[dma((2,))],
    )(in_hbm(prev_third), in_hbm(prev_second))
    y_prev = partner(prev, 2)
    mean = partner(eta_mean, 0)

    most = columns - columns // CHUNKS
    w, sec, c1, y1, inv_v, sol1, a_left, mass, pick, cost, target1 = call(
        first_kernel,
        32,
        in_specs=[HBM] * 8,
        out_specs=[SMEM, SMEM] + [VMEM] * 9,
        out_shape=[
            pltpu.SMEM((scenarios,), jnp.int32),
            pltpu.SMEM((scenarios,), jnp.int32),
            pltpu.VMEM(block, BF16),
            pltpu.VMEM(block, BF16),
            pltpu.VMEM(inverse.shape, BF16),
            pltpu.VMEM((scenarios, length, most), F32),
            pltpu.VMEM((length, most), F32),
            pltpu.VMEM((1, LANES), F32),
            pltpu.VMEM((BRANCH * length, rows), BF16),
            pltpu.VMEM((scenarios, length, LANES), F32),
            pltpu.VMEM((rows, columns), BF16),
        ],
        scratch_shapes=[
            pltpu.VMEM((length, columns), BF16),
            pltpu.VMEM((1, scenarios), jnp.int32),
            pltpu.VMEM((1, scenarios), jnp.int32),
            dma((5 + CHUNKS,)),
            dma((2,)),
        ],
    )(
        in_hbm(weights),
        in_hbm(section_three),
        in_hbm(w_row),
        in_hbm(section_three.reshape(1, scenarios)),
        in_hbm(prev_first),
        costs,
        duals,
        matrix,
    )

    core_prev, diag_prev = partner((prev, y_prev), 1)
    pieces = (prev, core_prev, y_prev, diag_prev)
    c3, y3, sol1_rest, a_right, cost = call(
        rest_kernel,
        30,
        in_specs=[SMEM] + [VMEM] * 4 + [HBM] * 2,
        out_specs=[VMEM] * 5,
        out_shape=[
            pltpu.VMEM(block, BF16),
            pltpu.VMEM(block, BF16),
            pltpu.VMEM((scenarios, length, columns - most), F32),
            pltpu.VMEM((length, columns - most), F32),
            pltpu.VMEM((scenarios, length, LANES), F32),
        ],
        scratch_shapes=[dma((2,))],
    )(w, target1, c1, inv_v, cost, costs, duals)

    c2, y2, sol3, cost, keep, send = call(
        third_kernel,
        30,
        in_specs=[SMEM] + [VMEM] * 11 + [HBM] * 2,
        out_specs=[VMEM] * 6,
        out_shape=[
            pltpu.VMEM(block, BF16),
            pltpu.VMEM(block, BF16),
            pltpu.VMEM(block, F32),
            pltpu.VMEM((scenarios, length, LANES), F32),
            pltpu.VMEM((HALF, length, columns), F32),
            pltpu.VMEM((HALF + 1, length, columns), BF16),
        ],
        scratch_shapes=[
            pltpu.VMEM((rows, columns), BF16),
            pltpu.VMEM((BRANCH, length, columns), BF16),
            dma((2,)),
        ],
    )(sec, *pieces, c3, y3, inv_v, pick, cost, a_left, a_right, costs, duals)

    chip_got = partner(send, 1)
    half_block = (scenarios, length, columns // 2)
    target2, left, a2, cost = call(
        left_kernel,
        30,
        in_specs=[SMEM] + [VMEM] * 8,
        out_specs=[VMEM] * 4,
        out_shape=[
            pltpu.VMEM((rows, columns), BF16),
            pltpu.VMEM(half_block, F32),
            pltpu.VMEM((length, columns // 2), F32),
            pltpu.VMEM((scenarios, length, LANES), F32),
        ],
        scratch_shapes=[pltpu.VMEM((length, columns), BF16)],
    )(w, *pieces, c2, y2, inv_v, cost)
    cut = HALF // 2
    chip_total, chip_send1, chip_send2 = call(
        chip_sum_kernel,
        8,
        in_specs=[VMEM] * 3,
        out_specs=[VMEM] * 3,
        out_shape=[
            pltpu.VMEM((HALF, length, columns), F32),
            pltpu.VMEM((cut + 1, length, columns), BF16),
            pltpu.VMEM((HALF - cut, length, columns), BF16),
        ],
    )(keep, send, chip_got)
    node_got1 = partner(chip_send1, 2)

    right, eta, sums = call(
        right_kernel,
        30,
        in_specs=[SMEM] + [VMEM] * 9,
        out_specs=[VMEM] * 3,
        out_shape=[
            pltpu.VMEM(half_block, F32),
            pltpu.VMEM((1, scenarios), F32),
            pltpu.VMEM((length, columns + 3 * LANES), BF16),
        ],
        scratch_shapes=[pltpu.VMEM((scenarios, length, LANES), F32)],
    )(w, w_row, mean.reshape(1, 1), duals_row, target2, c2, inv_v, cost, a2, mass)

    core_sums = partner(sums, 1)
    sums = call(
        far_sum_kernel, 8, in_specs=[VMEM] * 2, out_specs=VMEM, out_shape=pltpu.VMEM(sums.shape, BF16)
    )(sums, core_sums)
    y_sums = partner(sums, 2)
    node_got2 = partner(chip_send2, 2)
    far_shape = pltpu.VMEM((length, columns + 3 * LANES), BF16)
    far, a2, scal = call(
        node_sum_kernel,
        8,
        in_specs=[VMEM] * 4,
        out_specs=[VMEM] * 3,
        out_shape=[far_shape, pltpu.VMEM((length, columns), F32), pltpu.VMEM((length, LANES), F32)],
    )(sums, y_sums, chip_send1, node_got1)
    far_got = partner(far, 4)
    mask = 8
    while mask < nodes:
        far = call(far_sum_kernel, 8, in_specs=[VMEM] * 2, out_specs=VMEM, out_shape=far_shape)(far, far_got)
        far_got = partner(far, mask)
        mask *= 2

    buf = pltpu.VMEM(block, BF16)
    duals_shape = shape(hour_duals.shape, BF16)
    out, second_avg = call(
        second_duals_kernel,
        8,
        in_specs=[VMEM] * 5,
        out_specs=[HBM, HBM],
        out_shape=[duals_shape, shape((1, length, columns // 4), F32)],
        scratch_shapes=[buf, pltpu.VMEM((length, columns), F32), dma((4,)), dma],
    )(left, right, y2, a2, scal)

    avg, avg_send = call(
        third_avg_kernel,
        8,
        in_specs=[VMEM] * 4,
        out_specs=[VMEM] * 2,
        out_shape=[
            pltpu.VMEM((HALF, length, columns), F32),
            pltpu.VMEM((HALF, length, columns), BF16),
        ],
    )(chip_total, node_got1, node_got2, scal)
    avg_got = partner(avg_send, 1)
    out, third_avg = call(
        third_duals_kernel,
        8,
        in_specs=[SMEM] + [VMEM] * 4 + [HBM],
        out_specs=[HBM, HBM],
        out_shape=[duals_shape, shape((SHARES, length, columns), F32)],
        scratch_shapes=[buf, pltpu.VMEM((BRANCH, length, columns), F32), dma((4,)), dma],
        input_output_aliases={5: 0},
    )(sec, sol3, y3, avg, avg_got, out)
    out, first_avg, eta_avg, eta_duals_new = call(
        last_kernel,
        8,
        in_specs=[VMEM] * 7 + [HBM],
        out_specs=[HBM] * 4,
        out_shape=[
            duals_shape,
            shape((length, columns), F32),
            shape((1,), F32),
            shape((1, scenarios), F32),
        ],
        scratch_shapes=[
            buf,
            pltpu.VMEM((length, columns), F32),
            pltpu.VMEM((1, scenarios), F32),
            pltpu.SMEM((1,), F32),
            dma((4,)),
            dma((3,)),
        ],
        input_output_aliases={7: 0},
    )(sol1, sol1_rest, y1, far, far_got, eta, duals_row, out)
    return out, first_avg, second_avg, third_avg, eta_avg, eta_duals_new.reshape(scenarios)


def solution(mesh):
    row = P(("groups", "node"))
    in_specs = (row, row, P(), row, row, P("groups"), row, row, P("groups"), row)
    out_specs = (row, P("groups"), row, row, P("groups"), row)
    return jax.shard_map(step, mesh=mesh, in_specs=in_specs, out_specs=out_specs, check_vma=False)
```

```python
import jax
import jax.numpy as jnp
from jax import lax
from jax.experimental import pallas as pl
from jax.experimental.pallas import tpu as pltpu
from jax.sharding import PartitionSpec as P

BRANCH = 16
SHARES = BRANCH // 4
HALF = BRANCH // 2
PENALTY = 1.0
CVAR_WEIGHT = 0.25
CVAR_LEVEL = 0.75
CHUNKS = 4
LANES = 128
F32 = jnp.float32
BF16 = jnp.bfloat16

ANY = pl.BlockSpec(memory_space=pl.ANY)
HBM = pl.BlockSpec(memory_space=pltpu.HBM)
SMEM = pl.BlockSpec(memory_space=pltpu.SMEM)
VMEM = pl.BlockSpec(memory_space=pltpu.VMEM)


def partner(value, mask):
    pairs = [(source, source ^ mask) for source in range(lax.axis_size("node"))]
    return lax.ppermute(value, "node", pairs)


def in_hbm(value):
    return pltpu.with_memory_space_constraint(value, pltpu.HBM)


def call(kernel, mib, **kwargs):
    return pl.pallas_call(kernel, compiler_params=pltpu.CompilerParams(vmem_limit_bytes=mib << 20), **kwargs)


def quarter_of():
    return lax.axis_index("node") % 4


def place_of(node, quarter):
    half = (node // SHARES) % 2
    return ((half ^ (quarter % 2)) * 2 + node // (2 * SHARES)) * SHARES + node % SHARES


def build_target(target, anchor_of, c_v, y_v):
    scenarios, length, columns = c_v.shape
    width = columns // 1
    for j in range(1):
        cols = slice(j * width, (j + 1) * width)
        for i in range(scenarios // 2):
            rows = [
                PENALTY * anchor_of(s, cols).astype(F32) - c_v[s, :, cols].astype(F32) - y_v[s, :, cols].astype(F32)
                for s in (2 * i, 2 * i + 1)
            ]
            target[i * 2 * length : (i + 1) * 2 * length, cols] = jnp.concatenate(rows, axis=0).astype(BF16)


def multiply(target, inv_v, sol, c_v, cost, before, w, after, start=0):
    scenarios, length, columns = sol.shape
    width = inv_v.shape[1] // CHUNKS

    def product(j):
        before(j)
        sol[:, :, j * width : (j + 1) * width] = jnp.dot(
            target[...], inv_v[:, start + j * width : start + (j + 1) * width], preferred_element_type=F32
        ).reshape(scenarios, length, width)

    def finish(j):
        cols = slice(j * width, (j + 1) * width)
        total = jnp.zeros((length, width), F32)
        for s in range(scenarios):
            own = sol[s, :, cols]
            prod = c_v[s, :, start + cols.start : start + cols.stop].astype(F32) * own
            part = prod[:, :LANES]
            for k in range(1, width // LANES):
                part = part + prod[:, k * LANES : (k + 1) * LANES]
            cost[s] = cost[s] + part
            if w is not None:
                total = total + w[s].astype(F32) * own
        after(cols, total)

    count = columns // width
    for j in range(count):
        product(j)
        if j:
            finish(j - 1)
    finish(count - 1)


def first_kernel(
    w_hbm, sec_hbm, w_row_hbm, sec_row_hbm, pf_hbm, c_hbm, y_hbm, inv_hbm,
    w, sec, y1, c2, y2, c3, y3, inv_v, sol, a1, mass, pick, cost, c1, pf, w_row, sec_row, target, sems,
):
    scenarios, length, columns = sol.shape
    width = columns // CHUNKS

    def chunk(j):
        part = pl.ds(j * width, width)
        return pltpu.make_async_copy(inv_hbm.at[:, part], inv_v.at[:, part], sems.at[11 + j])

    def rows(k, c_v, y_v):
        own = pl.ds(k * length, length)
        return [
            pltpu.make_async_copy(c_hbm.at[:, own, :], c_v, sems.at[5 + 2 * k]),
            pltpu.make_async_copy(y_hbm.at[:, own, :], y_v, sems.at[6 + 2 * k]),
        ]

    small = [
        pltpu.make_async_copy(source, into, sems.at[k])
        for k, (source, into) in enumerate(
            ((w_row_hbm, w_row), (sec_row_hbm, sec_row), (w_hbm, w), (sec_hbm, sec), (pf_hbm, pf))
        )
    ]
    first = rows(0, c1, y1)
    later = rows(2, c3, y3) + rows(1, c2, y2)
    for copy in small + first + [chunk(j) for j in range(CHUNKS)] + later:
        copy.start()
    cost[...] = jnp.zeros_like(cost)
    for copy in small:
        copy.wait()

    node = sec_row[...] % BRANCH
    place = place_of(node, quarter_of())
    p = w_row[...].astype(F32)
    into_node = lax.broadcasted_iota(jnp.int32, (LANES, scenarios), 0) == node
    mass[...] = jnp.sum(jnp.where(into_node, p, 0.0).T, axis=0, keepdims=True)
    into_place = lax.broadcasted_iota(jnp.int32, (BRANCH * length, scenarios), 0) // length == place
    shape = (scenarios, scenarios * length)
    spread = lax.broadcasted_iota(jnp.int32, shape, 1) // length == lax.broadcasted_iota(jnp.int32, shape, 0)
    weight = jnp.dot(
        jnp.where(into_place, p, 0.0).astype(BF16),
        jnp.where(spread, 1.0, 0.0).astype(BF16),
        preferred_element_type=F32,
    )
    row = lax.broadcasted_iota(jnp.int32, pick.shape, 0)
    column = lax.broadcasted_iota(jnp.int32, pick.shape, 1)
    pick[...] = jnp.where(row % length == column % length, weight, 0.0).astype(BF16)

    for copy in first:
        copy.wait()
    build_target(target, lambda s, cols: pf[:, cols], c1, y1)

    def after(cols, total):
        a1[:, cols] = total

    multiply(target, inv_v, sol, c1, cost, lambda j: chunk(j).wait(), w, after)
    for copy in later:
        copy.wait()


def packed(value):
    high = value.astype(BF16)
    rest = value - high.astype(F32)
    middle = rest.astype(BF16)
    return jnp.concatenate((high, middle, (rest - middle.astype(F32)).astype(BF16)), axis=1)


def unpacked(tiles):
    high, middle, low = (tiles[:, k * LANES : (k + 1) * LANES].astype(F32) for k in range(3))
    return high + middle + low


def node_mass(scal, node):
    row = scal[2:3, :]
    slot = lax.broadcasted_iota(jnp.int32, row.shape, 1)
    return jnp.sum(jnp.where(slot == node, row, 0.0), axis=1, keepdims=True)


def third_kernel(
    sec, p0, p1, p2, p3, c_v, y_v, inv_v, pick, cost_in, a1, sol, cost, keep, send, target, table
):
    scenarios, length, _ = sol.shape
    quarter = quarter_of()
    send[HALF] = a1[...].astype(BF16)
    cost[...] = cost_in[...]
    for k, part in enumerate((p0, p1, p2, p3)):
        table[k * SHARES : (k + 1) * SHARES] = part[:SHARES]

    def anchor_of(s, cols):
        node = sec[s] % BRANCH
        return table[((node // SHARES) ^ quarter) * SHARES + node % SHARES, :, cols]

    build_target(target, anchor_of, c_v, y_v)

    def after(cols, total):
        own = sol[:, :, cols]
        flat = own.reshape(scenarios * length, own.shape[2]).astype(BF16)
        sums = jnp.dot(pick[...], flat, preferred_element_type=F32).reshape(BRANCH, length, own.shape[2])
        keep[:, :, cols] = sums[:HALF]
        send[:HALF, :, cols] = sums[HALF:].astype(BF16)

    multiply(target, inv_v, sol, c_v, cost, lambda j: None, None, after)


def left_kernel(w, p0, p1, p2, p3, c_v, y_v, inv_v, cost_in, target, sol, a2, cost, table):
    share = table.shape[1] // 4
    quarter = quarter_of()
    cost[...] = cost_in[...]
    for k, part in enumerate((p0, p1, p2, p3)):
        table[:, pl.ds(pl.multiple_of((quarter ^ k) * share, share), share)] = part[SHARES, :, :share]
    build_target(target, lambda s, cols: table[:, cols], c_v, y_v)

    def after(cols, total):
        a2[:, cols] = total

    multiply(target, inv_v, sol, c_v, cost, lambda j: None, w, after)


def right_kernel(w, w_row, level_row, target, c_v, inv_v, cost_in, a2, mass, sol, eta, sums, cost):
    scenarios, length, half = sol.shape
    columns = 2 * half
    cost[...] = cost_in[...]
    sums[:, :half] = a2[...].astype(BF16)

    def after(cols, total):
        sums[:, half + cols.start : half + cols.stop] = total.astype(BF16)

    multiply(target, inv_v, sol, c_v, cost, lambda j: None, w, after, half)
    lanes = jnp.sum(cost[...], axis=1)
    scen_cost = jnp.sum(lanes.T, axis=0, keepdims=True) / (3 * length * columns)
    p = w_row[...].astype(F32)
    low = level_row[:, scenarios:] - (CVAR_WEIGHT + level_row[:, :scenarios]) / PENALTY
    high = low + CVAR_WEIGHT / ((1.0 - CVAR_LEVEL) * PENALTY)
    level = jnp.minimum(jnp.maximum(scen_cost, low), high)
    eta[...] = level
    total = jnp.sum(p * level, axis=1, keepdims=True)
    whole = jnp.sum(p, axis=1, keepdims=True)
    row = lax.broadcasted_iota(jnp.int32, (length, LANES), 0)
    scal = jnp.where(row == 0, total, jnp.where(row == 1, whole, jnp.where(row == 2, mass[...], 0.0)))
    sums[:, columns:] = packed(scal)


def chip_sum_kernel(keep, sent, got, total, send1, send2):
    half = keep.shape[0]
    cut = half - send2.shape[0]
    value = keep[...] + got[:half].astype(F32)
    total[...] = value
    send1[:cut] = value[:cut].astype(BF16)
    send1[cut] = (sent[half].astype(F32) + got[half].astype(F32)).astype(BF16)
    send2[...] = value[cut:].astype(BF16)


def node_sum_kernel(s_own, s_got, sent, got, sums, a2, scal):
    columns = a2.shape[1]
    last = sent.shape[0] - 1
    sums[:, :columns] = (sent[last].astype(F32) + got[last].astype(F32)).astype(BF16)
    a2[...] = s_own[:, :columns].astype(F32) + s_got[:, :columns].astype(F32)
    value = unpacked(s_own[:, columns:]) + unpacked(s_got[:, columns:])
    scal[...] = value
    sums[:, columns:] = packed(value)


def far_sum_kernel(s_own, s_got, sums):
    columns = sums.shape[1] - 3 * LANES
    sums[:, :columns] = (s_own[:, :columns].astype(F32) + s_got[:, :columns].astype(F32)).astype(BF16)
    sums[:, columns:] = packed(unpacked(s_own[:, columns:]) + unpacked(s_got[:, columns:]))


def third_avg_kernel(total, got1, got2, scal, avg, send):
    quarter = quarter_of()
    cut = total.shape[0] - got2.shape[0]
    for k in range(HALF):
        node = ((k // SHARES) * 2 + quarter % 2) * SHARES + k % SHARES
        got = got1[k] if k < cut else got2[k - cut]
        value = (total[k] + got.astype(F32)) / node_mass(scal, node)
        avg[k] = value
        send[k] = value.astype(BF16)


def write_duals(sols, y_v, avg_of, out, buf, sems, section):
    scenarios, length, _ = y_v.shape
    group = scenarios // 4

    def copy(g):
        own = pl.ds(g * group, group)
        return pltpu.make_async_copy(
            buf.at[own], out.at[own, pl.ds(section * length, length), :], sems.at[g]
        )

    for g in range(4):

        def step(i, carry):
            s = g * group + i
            avg = avg_of(s)
            start = 0
            for sol in sols:
                cols = slice(start, start + sol.shape[2])
                fresh = y_v[s, :, cols].astype(F32) + PENALTY * (sol[s] - avg[:, cols])
                buf[s, :, cols] = fresh.astype(BF16)
                start = cols.stop
            return carry

        lax.fori_loop(0, group, step, 0, unroll=4)
        copy(g).start()
    return [copy(g) for g in range(4)]


def second_duals_kernel(left, right, y_v, a2, scal, out, second_avg, buf, full, sems, sem):
    _, columns = full.shape
    quarter = quarter_of()
    share = columns // 4
    full[...] = a2[...] / jnp.sum(scal[2:3, :], axis=1, keepdims=True)
    own = pl.ds(pl.multiple_of(quarter * share, share), share)
    copy = pltpu.make_async_copy(full.at[:, own], second_avg.at[0], sem)
    copy.start()
    for other in write_duals((left, right), y_v, lambda s: full[...], out, buf, sems, 1):
        other.wait()
    copy.wait()


def third_duals_kernel(sec, sol, y_v, avg, got, prior, out, third_avg, buf, table, sems, sem):
    quarter = quarter_of()
    copy = pltpu.make_async_copy(avg.at[pl.ds((quarter // 2) * SHARES, SHARES)], third_avg, sem)
    copy.start()
    table[:HALF] = avg[...]
    table[HALF:] = got[...].astype(F32)
    for other in write_duals(
        (sol,), y_v, lambda s: table[place_of(sec[s] % BRANCH, quarter)], out, buf, sems, 2
    ):
        other.wait()
    copy.wait()


def last_kernel(
    sol, y_v, s_own, s_got, eta, duals_row, prior,
    out, first_avg, eta_avg, eta_duals, buf, full, row, one, sems, sems2,
):
    columns = full.shape[1]
    scal = unpacked(s_own[:, columns:]) + unpacked(s_got[:, columns:])
    total, mass = scal[0:1, 0:1], scal[1:2, 0:1]
    full[...] = (s_own[:, :columns].astype(F32) + s_got[:, :columns].astype(F32)) / mass
    level = total / mass
    row[...] = duals_row[...] + PENALTY * (eta[...] - level)
    one[0] = jnp.sum(level)
    copies = [
        pltpu.make_async_copy(full, first_avg, sems2.at[0]),
        pltpu.make_async_copy(row, eta_duals, sems2.at[1]),
        pltpu.make_async_copy(one, eta_avg, sems2.at[2]),
    ]
    for copy in copies:
        copy.start()
    copies += write_duals((sol,), y_v, lambda s: full[...], out, buf, sems, 0)
    for copy in copies:
        copy.wait()


def step(
    unit_costs,
    hour_duals,
    inverse,
    weights,
    section_three,
    prev_first,
    prev_second,
    prev_third,
    eta_mean,
    eta_duals,
):
    scenarios, hours, columns = unit_costs.shape
    length = hours // 3
    nodes = lax.axis_size("node")
    dma = pltpu.SemaphoreType.DMA
    shape = jax.ShapeDtypeStruct
    block = (scenarios, length, columns)
    rows = scenarios * length
    w_row = weights.reshape(1, scenarios)
    duals_row = eta_duals.reshape(1, scenarios)
    costs, duals, matrix = in_hbm(unit_costs), in_hbm(hour_duals), in_hbm(inverse)

    tail = jnp.pad(prev_second, ((0, 0), (0, 0), (0, columns - columns // 4)))
    prev = jnp.concatenate((prev_third, tail))
    y_prev = partner(prev, 2)

    w, sec, y1, c2, y2, c3, y3, inv_v, sol1, a1, mass, pick, cost = call(
        first_kernel,
        32,
        in_specs=[HBM] * 8,
        out_specs=[SMEM, SMEM] + [VMEM] * 11,
        out_shape=[
            pltpu.SMEM((scenarios,), jnp.int32),
            pltpu.SMEM((scenarios,), jnp.int32),
            *[pltpu.VMEM(block, BF16)] * 5,
            pltpu.VMEM(inverse.shape, BF16),
            pltpu.VMEM(block, F32),
            pltpu.VMEM((length, columns), F32),
            pltpu.VMEM((1, LANES), F32),
            pltpu.VMEM((BRANCH * length, rows), BF16),
            pltpu.VMEM((scenarios, length, LANES), F32),
        ],
        scratch_shapes=[
            pltpu.VMEM(block, BF16),
            pltpu.VMEM((length, columns), BF16),
            pltpu.VMEM((1, scenarios), jnp.int32),
            pltpu.VMEM((1, scenarios), jnp.int32),
            pltpu.VMEM((rows, columns), BF16),
            dma((11 + CHUNKS,)),
        ],
    )(
        in_hbm(weights),
        in_hbm(section_three),
        in_hbm(w_row),
        in_hbm(section_three.reshape(1, scenarios)),
        in_hbm(prev_first),
        costs,
        duals,
        matrix,
    )

    y_prev, joined = lax.optimization_barrier((y_prev, (eta_mean, eta_duals)))
    level_row = jnp.concatenate((joined[1], joined[0])).reshape(1, scenarios + 1)
    core_prev, diag_prev = partner((prev, y_prev), 1)
    pieces = (prev, core_prev, y_prev, diag_prev)

    sol3, cost, keep, send = call(
        third_kernel,
        30,
        in_specs=[SMEM] + [VMEM] * 10,
        out_specs=[VMEM] * 4,
        out_shape=[
            pltpu.VMEM(block, F32),
            pltpu.VMEM((scenarios, length, LANES), F32),
            pltpu.VMEM((HALF, length, columns), F32),
            pltpu.VMEM((HALF + 1, length, columns), BF16),
        ],
        scratch_shapes=[pltpu.VMEM((rows, columns), BF16), pltpu.VMEM((BRANCH, length, columns), BF16)],
    )(sec, *pieces, c3, y3, inv_v, pick, cost, a1)

    chip_got = partner(send, 1)
    half_block = (scenarios, length, columns // 2)
    target2, left, a2, cost = call(
        left_kernel,
        30,
        in_specs=[SMEM] + [VMEM] * 8,
        out_specs=[VMEM] * 4,
        out_shape=[
            pltpu.VMEM((rows, columns), BF16),
            pltpu.VMEM(half_block, F32),
            pltpu.VMEM((length, columns // 2), F32),
            pltpu.VMEM((scenarios, length, LANES), F32),
        ],
        scratch_shapes=[pltpu.VMEM((length, columns), BF16)],
    )(w, *pieces, c2, y2, inv_v, cost)
    cut = HALF // 2
    chip_total, chip_send1, chip_send2 = call(
        chip_sum_kernel,
        8,
        in_specs=[VMEM] * 3,
        out_specs=[VMEM] * 3,
        out_shape=[
            pltpu.VMEM((HALF, length, columns), F32),
            pltpu.VMEM((cut + 1, length, columns), BF16),
            pltpu.VMEM((HALF - cut, length, columns), BF16),
        ],
    )(keep, send, chip_got)
    node_got1 = partner(chip_send1, 2)

    right, eta, sums = call(
        right_kernel,
        30,
        in_specs=[SMEM] + [VMEM] * 8,
        out_specs=[VMEM] * 3,
        out_shape=[
            pltpu.VMEM(half_block, F32),
            pltpu.VMEM((1, scenarios), F32),
            pltpu.VMEM((length, columns + 3 * LANES), BF16),
        ],
        scratch_shapes=[pltpu.VMEM((scenarios, length, LANES), F32)],
    )(w, w_row, level_row, target2, c2, inv_v, cost, a2, mass)

    core_sums = partner(sums, 1)
    sums = call(
        far_sum_kernel, 8, in_specs=[VMEM] * 2, out_specs=VMEM, out_shape=pltpu.VMEM(sums.shape, BF16)
    )(sums, core_sums)
    y_sums = partner(sums, 2)
    node_got2 = partner(chip_send2, 2)
    far_shape = pltpu.VMEM((length, columns + 3 * LANES), BF16)
    far, a2, scal = call(
        node_sum_kernel,
        8,
        in_specs=[VMEM] * 4,
        out_specs=[VMEM] * 3,
        out_shape=[far_shape, pltpu.VMEM((length, columns), F32), pltpu.VMEM((length, LANES), F32)],
    )(sums, y_sums, chip_send1, node_got1)
    far_got = partner(far, 4)
    mask = 8
    while mask < nodes:
        far = call(far_sum_kernel, 8, in_specs=[VMEM] * 2, out_specs=VMEM, out_shape=far_shape)(far, far_got)
        far_got = partner(far, mask)
        mask *= 2

    buf = pltpu.VMEM(block, BF16)
    duals_shape = shape(hour_duals.shape, BF16)
    out, second_avg = call(
        second_duals_kernel,
        8,
        in_specs=[VMEM] * 5,
        out_specs=[HBM, HBM],
        out_shape=[duals_shape, shape((1, length, columns // 4), F32)],
        scratch_shapes=[buf, pltpu.VMEM((length, columns), F32), dma((4,)), dma],
    )(left, right, y2, a2, scal)

    avg, avg_send = call(
        third_avg_kernel,
        8,
        in_specs=[VMEM] * 4,
        out_specs=[VMEM] * 2,
        out_shape=[
            pltpu.VMEM((HALF, length, columns), F32),
            pltpu.VMEM((HALF, length, columns), BF16),
        ],
    )(chip_total, node_got1, node_got2, scal)
    avg_got = partner(avg_send, 1)
    out, third_avg = call(
        third_duals_kernel,
        8,
        in_specs=[SMEM] + [VMEM] * 4 + [HBM],
        out_specs=[HBM, HBM],
        out_shape=[duals_shape, shape((SHARES, length, columns), F32)],
        scratch_shapes=[buf, pltpu.VMEM((BRANCH, length, columns), F32), dma((4,)), dma],
        input_output_aliases={5: 0},
    )(sec, sol3, y3, avg, avg_got, out)
    out, first_avg, eta_avg, eta_duals_new = call(
        last_kernel,
        8,
        in_specs=[VMEM] * 6 + [HBM],
        out_specs=[HBM] * 4,
        out_shape=[
            duals_shape,
            shape((length, columns), F32),
            shape((1,), F32),
            shape((1, scenarios), F32),
        ],
        scratch_shapes=[
            buf,
            pltpu.VMEM((length, columns), F32),
            pltpu.VMEM((1, scenarios), F32),
            pltpu.SMEM((1,), F32),
            dma((4,)),
            dma((3,)),
        ],
        input_output_aliases={6: 0},
    )(sol1, y1, far, far_got, eta, duals_row, out)
    return out, first_avg, second_avg, third_avg, eta_avg, eta_duals_new.reshape(scenarios)


def solution(mesh):
    row = P(("groups", "node"))
    in_specs = (row, row, P(), row, row, P("groups"), row, row, P("groups"), row)
    out_specs = (row, P("groups"), row, row, P("groups"), row)
    return jax.shard_map(step, mesh=mesh, in_specs=in_specs, out_specs=out_specs, check_vma=False)
```

```python
import jax
import jax.numpy as jnp
from jax import lax
from jax.experimental import pallas as pl
from jax.experimental.pallas import tpu as pltpu
from jax.sharding import PartitionSpec as P

BRANCH = 16
SHARES = BRANCH // 4
HALF = BRANCH // 2
PENALTY = 1.0
CVAR_WEIGHT = 0.25
CVAR_LEVEL = 0.75
CHUNKS = 4
LANES = 128
F32 = jnp.float32
BF16 = jnp.bfloat16

ANY = pl.BlockSpec(memory_space=pl.ANY)
HBM = pl.BlockSpec(memory_space=pltpu.HBM)
SMEM = pl.BlockSpec(memory_space=pltpu.SMEM)
VMEM = pl.BlockSpec(memory_space=pltpu.VMEM)


def partner(value, mask):
    pairs = [(source, source ^ mask) for source in range(lax.axis_size("node"))]
    return lax.ppermute(value, "node", pairs)


def in_hbm(value):
    return pltpu.with_memory_space_constraint(value, pltpu.HBM)


def call(kernel, mib, **kwargs):
    return pl.pallas_call(kernel, compiler_params=pltpu.CompilerParams(vmem_limit_bytes=mib << 20), **kwargs)


def quarter_of():
    return lax.axis_index("node") % 4


def place_of(node, quarter):
    half = (node // SHARES) % 2
    return ((half ^ (quarter % 2)) * 2 + node // (2 * SHARES)) * SHARES + node % SHARES


def build_target(target, anchor_of, c_v, y_v):
    scenarios, length, _ = c_v.shape
    for i in range(scenarios // 2):
        rows = [
            PENALTY * anchor_of(s).astype(F32) - c_v[s].astype(F32) - y_v[s].astype(F32)
            for s in (2 * i, 2 * i + 1)
        ]
        target[i * 2 * length : (i + 1) * 2 * length, :] = jnp.concatenate(rows, axis=0).astype(BF16)


def multiply(target, inv_v, sol, c_v, cost, before, w, after, start=0):
    scenarios, length, columns = sol.shape
    width = inv_v.shape[1] // CHUNKS

    def product(j):
        before(j)
        sol[:, :, j * width : (j + 1) * width] = jnp.dot(
            target[...], inv_v[:, start + j * width : start + (j + 1) * width], preferred_element_type=F32
        ).reshape(scenarios, length, width)

    def finish(j):
        cols = slice(j * width, (j + 1) * width)
        total = jnp.zeros((length, width), F32)
        for s in range(scenarios):
            own = sol[s, :, cols]
            prod = c_v[s, :, start + cols.start : start + cols.stop].astype(F32) * own
            part = prod[:, :LANES]
            for k in range(1, width // LANES):
                part = part + prod[:, k * LANES : (k + 1) * LANES]
            cost[s] = cost[s] + part
            if w is not None:
                total = total + w[s].astype(F32) * own
        after(cols, total)

    count = columns // width
    for j in range(count):
        product(j)
        if j:
            finish(j - 1)
    finish(count - 1)


def first_kernel(
    w_hbm, sec_hbm, w_row_hbm, sec_row_hbm, pf_hbm, c_hbm, y_hbm, inv_hbm,
    w, sec, y1, c2, y2, c3, y3, inv_v, sol, a1, mass, pick, cost, c1, pf, w_row, sec_row, target, sems,
):
    scenarios, length, columns = sol.shape
    width = columns // CHUNKS

    def chunk(j):
        part = pl.ds(j * width, width)
        return pltpu.make_async_copy(inv_hbm.at[:, part], inv_v.at[:, part], sems.at[11 + j])

    def rows(k, c_v, y_v):
        own = pl.ds(k * length, length)
        return [
            pltpu.make_async_copy(c_hbm.at[:, own, :], c_v, sems.at[5 + 2 * k]),
            pltpu.make_async_copy(y_hbm.at[:, own, :], y_v, sems.at[6 + 2 * k]),
        ]

    small = [
        pltpu.make_async_copy(source, into, sems.at[k])
        for k, (source, into) in enumerate(
            ((w_row_hbm, w_row), (sec_row_hbm, sec_row), (w_hbm, w), (sec_hbm, sec), (pf_hbm, pf))
        )
    ]
    first = rows(0, c1, y1)
    later = rows(2, c3, y3) + rows(1, c2, y2)
    for copy in small + first + [chunk(j) for j in range(CHUNKS)] + later:
        copy.start()
    cost[...] = jnp.zeros_like(cost)
    for copy in small:
        copy.wait()

    node = sec_row[...] % BRANCH
    place = place_of(node, quarter_of())
    p = w_row[...].astype(F32)
    into_node = lax.broadcasted_iota(jnp.int32, (LANES, scenarios), 0) == node
    mass[...] = jnp.sum(jnp.where(into_node, p, 0.0).T, axis=0, keepdims=True)
    into_place = lax.broadcasted_iota(jnp.int32, (BRANCH * length, scenarios), 0) // length == place
    shape = (scenarios, scenarios * length)
    spread = lax.broadcasted_iota(jnp.int32, shape, 1) // length == lax.broadcasted_iota(jnp.int32, shape, 0)
    weight = jnp.dot(
        jnp.where(into_place, p, 0.0).astype(BF16),
        jnp.where(spread, 1.0, 0.0).astype(BF16),
        preferred_element_type=F32,
    )
    row = lax.broadcasted_iota(jnp.int32, pick.shape, 0)
    column = lax.broadcasted_iota(jnp.int32, pick.shape, 1)
    pick[...] = jnp.where(row % length == column % length, weight, 0.0).astype(BF16)

    for copy in first:
        copy.wait()
    build_target(target, lambda s: pf[...], c1, y1)

    def after(cols, total):
        a1[:, cols] = total

    multiply(target, inv_v, sol, c1, cost, lambda j: chunk(j).wait(), w, after)
    for copy in later:
        copy.wait()


def packed(value):
    high = value.astype(BF16)
    rest = value - high.astype(F32)
    middle = rest.astype(BF16)
    return jnp.concatenate((high, middle, (rest - middle.astype(F32)).astype(BF16)), axis=1)


def unpacked(tiles):
    high, middle, low = (tiles[:, k * LANES : (k + 1) * LANES].astype(F32) for k in range(3))
    return high + middle + low


def node_mass(scal, node):
    row = scal[2:3, :]
    slot = lax.broadcasted_iota(jnp.int32, row.shape, 1)
    return jnp.sum(jnp.where(slot == node, row, 0.0), axis=1, keepdims=True)


def third_kernel(
    sec, p0, p1, p2, p3, c_v, y_v, inv_v, pick, cost_in, a1, sol, cost, keep, send, target, table
):
    scenarios, length, _ = sol.shape
    quarter = quarter_of()
    send[HALF] = a1[...].astype(BF16)
    cost[...] = cost_in[...]
    for k, part in enumerate((p0, p1, p2, p3)):
        table[k * SHARES : (k + 1) * SHARES] = part[:SHARES]

    def anchor_of(s):
        node = sec[s] % BRANCH
        return table[((node // SHARES) ^ quarter) * SHARES + node % SHARES]

    build_target(target, anchor_of, c_v, y_v)

    def after(cols, total):
        own = sol[:, :, cols]
        flat = own.reshape(scenarios * length, own.shape[2]).astype(BF16)
        sums = jnp.dot(pick[...], flat, preferred_element_type=F32).reshape(BRANCH, length, own.shape[2])
        keep[:, :, cols] = sums[:HALF]
        send[:HALF, :, cols] = sums[HALF:].astype(BF16)

    multiply(target, inv_v, sol, c_v, cost, lambda j: None, None, after)


def left_kernel(w, p0, p1, p2, p3, c_v, y_v, inv_v, cost_in, target, sol, a2, cost, table):
    share = table.shape[1] // 4
    quarter = quarter_of()
    cost[...] = cost_in[...]
    for k, part in enumerate((p0, p1, p2, p3)):
        table[:, pl.ds(pl.multiple_of((quarter ^ k) * share, share), share)] = part[SHARES, :, :share]
    build_target(target, lambda s: table[...], c_v, y_v)

    def after(cols, total):
        a2[:, cols] = total

    multiply(target, inv_v, sol, c_v, cost, lambda j: None, w, after)


def right_kernel(w, w_row, level_row, target, c_v, inv_v, cost_in, a2, mass, sol, eta, sums, cost):
    scenarios, length, half = sol.shape
    columns = 2 * half
    cost[...] = cost_in[...]
    sums[:, :half] = a2[...].astype(BF16)

    def after(cols, total):
        sums[:, half + cols.start : half + cols.stop] = total.astype(BF16)

    multiply(target, inv_v, sol, c_v, cost, lambda j: None, w, after, half)
    lanes = jnp.sum(cost[...], axis=1)
    scen_cost = jnp.sum(lanes.T, axis=0, keepdims=True) / (3 * length * columns)
    p = w_row[...].astype(F32)
    low = level_row[:, scenarios:] - (CVAR_WEIGHT + level_row[:, :scenarios]) / PENALTY
    high = low + CVAR_WEIGHT / ((1.0 - CVAR_LEVEL) * PENALTY)
    level = jnp.minimum(jnp.maximum(scen_cost, low), high)
    eta[...] = level
    total = jnp.sum(p * level, axis=1, keepdims=True)
    whole = jnp.sum(p, axis=1, keepdims=True)
    row = lax.broadcasted_iota(jnp.int32, (length, LANES), 0)
    scal = jnp.where(row == 0, total, jnp.where(row == 1, whole, jnp.where(row == 2, mass[...], 0.0)))
    sums[:, columns:] = packed(scal)


def chip_sum_kernel(keep, sent, got, total, send1, send2):
    half = keep.shape[0]
    cut = half - send2.shape[0]
    value = keep[...] + got[:half].astype(F32)
    total[...] = value
    send1[:cut] = value[:cut].astype(BF16)
    send1[cut] = (sent[half].astype(F32) + got[half].astype(F32)).astype(BF16)
    send2[...] = value[cut:].astype(BF16)


def core_sum_kernel(s_own, s_got, scal, a2):
    columns = a2.shape[1]
    scal[...] = packed(unpacked(s_own[:, columns:]) + unpacked(s_got[:, columns:]))
    a2[...] = (s_own[:, :columns].astype(F32) + s_got[:, :columns].astype(F32)).astype(BF16)


def node_sum_kernel(s_own, s_got, sent, got, sums, scal):
    columns = sent.shape[2]
    last = sent.shape[0] - 1
    sums[:, :columns] = (sent[last].astype(F32) + got[last].astype(F32)).astype(BF16)
    value = unpacked(s_own[...]) + unpacked(s_got[...])
    scal[...] = value
    sums[:, columns:] = packed(value)


def far_sum_kernel(s_own, s_got, sums):
    columns = sums.shape[1] - 3 * LANES
    sums[:, :columns] = (s_own[:, :columns].astype(F32) + s_got[:, :columns].astype(F32)).astype(BF16)
    sums[:, columns:] = packed(unpacked(s_own[:, columns:]) + unpacked(s_got[:, columns:]))


def third_avg_kernel(total, got1, got2, scal, avg, send):
    quarter = quarter_of()
    cut = total.shape[0] - got2.shape[0]
    for k in range(HALF):
        node = ((k // SHARES) * 2 + quarter % 2) * SHARES + k % SHARES
        got = got1[k] if k < cut else got2[k - cut]
        value = (total[k] + got.astype(F32)) / node_mass(scal, node)
        avg[k] = value
        send[k] = value.astype(BF16)


def write_duals(sols, y_v, avg_of, out, buf, sems, section):
    scenarios, length, _ = y_v.shape
    group = scenarios // 4

    def copy(g):
        own = pl.ds(g * group, group)
        return pltpu.make_async_copy(
            buf.at[own], out.at[own, pl.ds(section * length, length), :], sems.at[g]
        )

    for g in range(4):
        for s in range(g * group, (g + 1) * group):
            avg = avg_of(s)
            start = 0
            for sol in sols:
                cols = slice(start, start + sol.shape[2])
                fresh = y_v[s, :, cols].astype(F32) + PENALTY * (sol[s] - avg[:, cols])
                buf[s, :, cols] = fresh.astype(BF16)
                start = cols.stop
        copy(g).start()
    return [copy(g) for g in range(4)]


def later_duals_kernel(
    sec, left, right, y2, a_own, a_got, scal, sol3, y3, avg, got,
    out, second_avg, third_avg, buf2, buf3, full, table, sems2, sems3, sems,
):
    _, columns = full.shape
    quarter = quarter_of()
    share = columns // 4
    whole = jnp.sum(scal[2:3, :], axis=1, keepdims=True)
    full[...] = (a_own[...].astype(F32) + a_got[...].astype(F32)) / whole
    own = pl.ds(pl.multiple_of(quarter * share, share), share)
    copies = [
        pltpu.make_async_copy(full.at[:, own], second_avg.at[0], sems.at[0]),
        pltpu.make_async_copy(avg.at[pl.ds((quarter // 2) * SHARES, SHARES)], third_avg, sems.at[1]),
    ]
    for copy in copies:
        copy.start()
    copies += write_duals((left, right), y2, lambda s: full[...], out, buf2, sems2, 1)
    table[:HALF] = avg[...]
    table[HALF:] = got[...].astype(F32)
    copies += write_duals(
        (sol3,), y3, lambda s: table[place_of(sec[s] % BRANCH, quarter)], out, buf3, sems3, 2
    )
    for copy in copies:
        copy.wait()


def last_kernel(
    sol, y_v, s_own, s_got, eta, duals_row, prior,
    out, first_avg, eta_avg, eta_duals, buf, full, row, one, sems, sems2,
):
    columns = full.shape[1]
    scal = unpacked(s_own[:, columns:]) + unpacked(s_got[:, columns:])
    total, mass = scal[0:1, 0:1], scal[1:2, 0:1]
    full[...] = (s_own[:, :columns].astype(F32) + s_got[:, :columns].astype(F32)) / mass
    level = total / mass
    row[...] = duals_row[...] + PENALTY * (eta[...] - level)
    one[0] = jnp.sum(level)
    copies = [
        pltpu.make_async_copy(full, first_avg, sems2.at[0]),
        pltpu.make_async_copy(row, eta_duals, sems2.at[1]),
        pltpu.make_async_copy(one, eta_avg, sems2.at[2]),
    ]
    for copy in copies:
        copy.start()
    copies += write_duals((sol,), y_v, lambda s: full[...], out, buf, sems, 0)
    for copy in copies:
        copy.wait()


def step(
    unit_costs,
    hour_duals,
    inverse,
    weights,
    section_three,
    prev_first,
    prev_second,
    prev_third,
    eta_mean,
    eta_duals,
):
    scenarios, hours, columns = unit_costs.shape
    length = hours // 3
    nodes = lax.axis_size("node")
    dma = pltpu.SemaphoreType.DMA
    shape = jax.ShapeDtypeStruct
    block = (scenarios, length, columns)
    rows = scenarios * length
    w_row = weights.reshape(1, scenarios)
    duals_row = eta_duals.reshape(1, scenarios)
    costs, duals, matrix = in_hbm(unit_costs), in_hbm(hour_duals), in_hbm(inverse)

    tail = jnp.pad(prev_second, ((0, 0), (0, 0), (0, columns - columns // 4)))
    prev = jnp.concatenate((prev_third, tail))
    y_prev = partner(prev, 2)

    w, sec, y1, c2, y2, c3, y3, inv_v, sol1, a1, mass, pick, cost = call(
        first_kernel,
        32,
        in_specs=[HBM] * 8,
        out_specs=[SMEM, SMEM] + [VMEM] * 11,
        out_shape=[
            pltpu.SMEM((scenarios,), jnp.int32),
            pltpu.SMEM((scenarios,), jnp.int32),
            *[pltpu.VMEM(block, BF16)] * 5,
            pltpu.VMEM(inverse.shape, BF16),
            pltpu.VMEM(block, F32),
            pltpu.VMEM((length, columns), F32),
            pltpu.VMEM((1, LANES), F32),
            pltpu.VMEM((BRANCH * length, rows), BF16),
            pltpu.VMEM((scenarios, length, LANES), F32),
        ],
        scratch_shapes=[
            pltpu.VMEM(block, BF16),
            pltpu.VMEM((length, columns), BF16),
            pltpu.VMEM((1, scenarios), jnp.int32),
            pltpu.VMEM((1, scenarios), jnp.int32),
            pltpu.VMEM((rows, columns), BF16),
            dma((11 + CHUNKS,)),
        ],
    )(
        in_hbm(weights),
        in_hbm(section_three),
        in_hbm(w_row),
        in_hbm(section_three.reshape(1, scenarios)),
        in_hbm(prev_first),
        costs,
        duals,
        matrix,
    )

    y_prev, joined = lax.optimization_barrier((y_prev, (eta_mean, eta_duals)))
    level_row = jnp.concatenate((joined[1], joined[0])).reshape(1, scenarios + 1)
    core_prev, diag_prev = partner((prev, y_prev), 1)
    pieces = (prev, core_prev, y_prev, diag_prev)

    sol3, cost, keep, send = call(
        third_kernel,
        30,
        in_specs=[SMEM] + [VMEM] * 10,
        out_specs=[VMEM] * 4,
        out_shape=[
            pltpu.VMEM(block, F32),
            pltpu.VMEM((scenarios, length, LANES), F32),
            pltpu.VMEM((HALF, length, columns), F32),
            pltpu.VMEM((HALF + 1, length, columns), BF16),
        ],
        scratch_shapes=[pltpu.VMEM((rows, columns), BF16), pltpu.VMEM((BRANCH, length, columns), BF16)],
    )(sec, *pieces, c3, y3, inv_v, pick, cost, a1)

    chip_got = partner(send, 1)
    half_block = (scenarios, length, columns // 2)
    target2, left, a2, cost = call(
        left_kernel,
        30,
        in_specs=[SMEM] + [VMEM] * 8,
        out_specs=[VMEM] * 4,
        out_shape=[
            pltpu.VMEM((rows, columns), BF16),
            pltpu.VMEM(half_block, F32),
            pltpu.VMEM((length, columns // 2), F32),
            pltpu.VMEM((scenarios, length, LANES), F32),
        ],
        scratch_shapes=[pltpu.VMEM((length, columns), BF16)],
    )(w, *pieces, c2, y2, inv_v, cost)
    cut = HALF // 2
    chip_total, chip_send1, chip_send2 = call(
        chip_sum_kernel,
        8,
        in_specs=[VMEM] * 3,
        out_specs=[VMEM] * 3,
        out_shape=[
            pltpu.VMEM((HALF, length, columns), F32),
            pltpu.VMEM((cut + 1, length, columns), BF16),
            pltpu.VMEM((HALF - cut, length, columns), BF16),
        ],
    )(keep, send, chip_got)
    node_got1 = partner(chip_send1, 2)

    right, eta, sums = call(
        right_kernel,
        30,
        in_specs=[SMEM] + [VMEM] * 8,
        out_specs=[VMEM] * 3,
        out_shape=[
            pltpu.VMEM(half_block, F32),
            pltpu.VMEM((1, scenarios), F32),
            pltpu.VMEM((length, columns + 3 * LANES), BF16),
        ],
        scratch_shapes=[pltpu.VMEM((scenarios, length, LANES), F32)],
    )(w, w_row, level_row, target2, c2, inv_v, cost, a2, mass)

    core_sums = partner(sums, 1)
    scal_chip, a2 = call(
        core_sum_kernel,
        8,
        in_specs=[VMEM] * 2,
        out_specs=[VMEM] * 2,
        out_shape=[pltpu.VMEM((length, 3 * LANES), BF16), pltpu.VMEM((length, columns), BF16)],
    )(sums, core_sums)
    y_scal = partner(scal_chip, 2)
    node_got2 = partner(chip_send2, 2)
    a2_got = partner(a2, 2)
    far_shape = pltpu.VMEM((length, columns + 3 * LANES), BF16)
    far, scal = call(
        node_sum_kernel,
        8,
        in_specs=[VMEM] * 4,
        out_specs=[VMEM] * 2,
        out_shape=[far_shape, pltpu.VMEM((length, LANES), F32)],
    )(scal_chip, y_scal, chip_send1, node_got1)
    far_got = partner(far, 4)
    mask = 8
    while mask < nodes:
        far = call(far_sum_kernel, 8, in_specs=[VMEM] * 2, out_specs=VMEM, out_shape=far_shape)(far, far_got)
        far_got = partner(far, mask)
        mask *= 2

    buf = pltpu.VMEM(block, BF16)
    duals_shape = shape(hour_duals.shape, BF16)
    avg, avg_send = call(
        third_avg_kernel,
        8,
        in_specs=[VMEM] * 4,
        out_specs=[VMEM] * 2,
        out_shape=[
            pltpu.VMEM((HALF, length, columns), F32),
            pltpu.VMEM((HALF, length, columns), BF16),
        ],
    )(chip_total, node_got1, node_got2, scal)
    avg_got = partner(avg_send, 1)
    out, second_avg, third_avg = call(
        later_duals_kernel,
        12,
        in_specs=[SMEM] + [VMEM] * 10,
        out_specs=[HBM] * 3,
        out_shape=[
            duals_shape,
            shape((1, length, columns // 4), F32),
            shape((SHARES, length, columns), F32),
        ],
        scratch_shapes=[
            buf,
            buf,
            pltpu.VMEM((length, columns), F32),
            pltpu.VMEM((BRANCH, length, columns), F32),
            dma((4,)),
            dma((4,)),
            dma((2,)),
        ],
    )(sec, left, right, y2, a2, a2_got, scal, sol3, y3, avg, avg_got)
    out, first_avg, eta_avg, eta_duals_new = call(
        last_kernel,
        8,
        in_specs=[VMEM] * 6 + [HBM],
        out_specs=[HBM] * 4,
        out_shape=[
            duals_shape,
            shape((length, columns), F32),
            shape((1,), F32),
            shape((1, scenarios), F32),
        ],
        scratch_shapes=[
            buf,
            pltpu.VMEM((length, columns), F32),
            pltpu.VMEM((1, scenarios), F32),
            pltpu.SMEM((1,), F32),
            dma((4,)),
            dma((3,)),
        ],
        input_output_aliases={6: 0},
    )(sol1, y1, far, far_got, eta, duals_row, out)
    return out, first_avg, second_avg, third_avg, eta_avg, eta_duals_new.reshape(scenarios)


def solution(mesh):
    row = P(("groups", "node"))
    in_specs = (row, row, P(), row, row, P("groups"), row, row, P("groups"), row)
    out_specs = (row, P("groups"), row, row, P("groups"), row)
    return jax.shard_map(step, mesh=mesh, in_specs=in_specs, out_specs=out_specs, check_vma=False)
```

```python
import jax
import jax.numpy as jnp
from jax import lax
from jax.experimental import pallas as pl
from jax.experimental.pallas import tpu as pltpu
from jax.sharding import PartitionSpec as P

BRANCH = 16
SHARES = BRANCH // 4
HALF = BRANCH // 2
PENALTY = 1.0
CVAR_WEIGHT = 0.25
CVAR_LEVEL = 0.75
CHUNKS = 4
LANES = 128
F32 = jnp.float32
BF16 = jnp.bfloat16

ANY = pl.BlockSpec(memory_space=pl.ANY)
HBM = pl.BlockSpec(memory_space=pltpu.HBM)
SMEM = pl.BlockSpec(memory_space=pltpu.SMEM)
VMEM = pl.BlockSpec(memory_space=pltpu.VMEM)


def partner(value, mask):
    pairs = [(source, source ^ mask) for source in range(lax.axis_size("node"))]
    return lax.ppermute(value, "node", pairs)


def in_hbm(value):
    return pltpu.with_memory_space_constraint(value, pltpu.HBM)


def call(kernel, mib, **kwargs):
    return pl.pallas_call(kernel, compiler_params=pltpu.CompilerParams(vmem_limit_bytes=mib << 20), **kwargs)


def quarter_of():
    return lax.axis_index("node") % 4


def place_of(node, quarter):
    half = (node // SHARES) % 2
    return ((half ^ (quarter % 2)) * 2 + node // (2 * SHARES)) * SHARES + node % SHARES


def build_target(target, anchor_of, c_v, y_v):
    scenarios, length, _ = c_v.shape
    for i in range(scenarios // 2):
        rows = [
            PENALTY * anchor_of(s).astype(F32) - c_v[s].astype(F32) - y_v[s].astype(F32)
            for s in (2 * i, 2 * i + 1)
        ]
        target[i * 2 * length : (i + 1) * 2 * length, :] = jnp.concatenate(rows, axis=0).astype(BF16)


def multiply(target, inv_v, sol, c_v, cost, before, w, after, start=0):
    scenarios, length, columns = sol.shape
    width = inv_v.shape[1] // CHUNKS

    def product(j):
        before(j)
        sol[:, :, j * width : (j + 1) * width] = jnp.dot(
            target[...], inv_v[:, start + j * width : start + (j + 1) * width], preferred_element_type=F32
        ).reshape(scenarios, length, width)

    def finish(j):
        cols = slice(j * width, (j + 1) * width)
        total = jnp.zeros((length, width), F32)
        for s in range(scenarios):
            own = sol[s, :, cols]
            prod = c_v[s, :, start + cols.start : start + cols.stop].astype(F32) * own
            part = prod[:, :LANES]
            for k in range(1, width // LANES):
                part = part + prod[:, k * LANES : (k + 1) * LANES]
            cost[s] = cost[s] + part
            if w is not None:
                total = total + w[s].astype(F32) * own
        after(cols, total)

    count = columns // width
    for j in range(count):
        product(j)
        if j:
            finish(j - 1)
    finish(count - 1)


def first_kernel(
    w_hbm, sec_hbm, w_row_hbm, sec_row_hbm, pf_hbm, c_hbm, y_hbm, inv_hbm,
    w, sec, y1, c2, y2, c3, y3, inv_v, sol, a1, mass, pick, cost, c1, pf, w_row, sec_row, target, sems,
):
    scenarios, length, columns = sol.shape
    width = columns // CHUNKS

    def chunk(j):
        part = pl.ds(j * width, width)
        return pltpu.make_async_copy(inv_hbm.at[:, part], inv_v.at[:, part], sems.at[11 + j])

    def rows(k, c_v, y_v):
        own = pl.ds(k * length, length)
        return [
            pltpu.make_async_copy(c_hbm.at[:, own, :], c_v, sems.at[5 + 2 * k]),
            pltpu.make_async_copy(y_hbm.at[:, own, :], y_v, sems.at[6 + 2 * k]),
        ]

    small = [
        pltpu.make_async_copy(source, into, sems.at[k])
        for k, (source, into) in enumerate(
            ((w_row_hbm, w_row), (sec_row_hbm, sec_row), (w_hbm, w), (sec_hbm, sec), (pf_hbm, pf))
        )
    ]
    first = rows(0, c1, y1)
    later = rows(2, c3, y3) + rows(1, c2, y2)
    for copy in small + first + [chunk(j) for j in range(CHUNKS)] + later:
        copy.start()
    cost[...] = jnp.zeros_like(cost)
    for copy in small:
        copy.wait()

    node = sec_row[...] % BRANCH
    place = place_of(node, quarter_of())
    p = w_row[...].astype(F32)
    into_node = lax.broadcasted_iota(jnp.int32, (LANES, scenarios), 0) == node
    mass[...] = jnp.sum(jnp.where(into_node, p, 0.0).T, axis=0, keepdims=True)
    into_place = lax.broadcasted_iota(jnp.int32, (BRANCH * length, scenarios), 0) // length == place
    shape = (scenarios, scenarios * length)
    spread = lax.broadcasted_iota(jnp.int32, shape, 1) // length == lax.broadcasted_iota(jnp.int32, shape, 0)
    weight = jnp.dot(
        jnp.where(into_place, p, 0.0).astype(BF16),
        jnp.where(spread, 1.0, 0.0).astype(BF16),
        preferred_element_type=F32,
    )
    row = lax.broadcasted_iota(jnp.int32, pick.shape, 0)
    column = lax.broadcasted_iota(jnp.int32, pick.shape, 1)
    pick[...] = jnp.where(row % length == column % length, weight, 0.0).astype(BF16)

    for copy in first:
        copy.wait()
    build_target(target, lambda s: pf[...], c1, y1)

    def after(cols, total):
        a1[:, cols] = total

    multiply(target, inv_v, sol, c1, cost, lambda j: chunk(j).wait(), w, after)
    for copy in later:
        copy.wait()


def packed(value):
    high = value.astype(BF16)
    rest = value - high.astype(F32)
    middle = rest.astype(BF16)
    return jnp.concatenate((high, middle, (rest - middle.astype(F32)).astype(BF16)), axis=1)


def unpacked(tiles):
    high, middle, low = (tiles[:, k * LANES : (k + 1) * LANES].astype(F32) for k in range(3))
    return high + middle + low


def node_mass(scal, node):
    row = scal[2:3, :]
    slot = lax.broadcasted_iota(jnp.int32, row.shape, 1)
    return jnp.sum(jnp.where(slot == node, row, 0.0), axis=1, keepdims=True)


def third_kernel(
    sec, p0, p1, p2, p3, c_v, y_v, inv_v, pick, cost_in, a1, sol, cost, keep, send, target, table
):
    scenarios, length, _ = sol.shape
    quarter = quarter_of()
    send[HALF] = a1[...].astype(BF16)
    cost[...] = cost_in[...]
    for k, part in enumerate((p0, p1, p2, p3)):
        table[k * SHARES : (k + 1) * SHARES] = part[:SHARES]

    def anchor_of(s):
        node = sec[s] % BRANCH
        return table[((node // SHARES) ^ quarter) * SHARES + node % SHARES]

    build_target(target, anchor_of, c_v, y_v)

    def after(cols, total):
        own = sol[:, :, cols]
        flat = own.reshape(scenarios * length, own.shape[2]).astype(BF16)
        sums = jnp.dot(pick[...], flat, preferred_element_type=F32).reshape(BRANCH, length, own.shape[2])
        keep[:, :, cols] = sums[:HALF]
        send[:HALF, :, cols] = sums[HALF:].astype(BF16)

    multiply(target, inv_v, sol, c_v, cost, lambda j: None, None, after)


def left_kernel(w, p0, p1, p2, p3, c_v, y_v, inv_v, cost_in, target, sol, a2, cost, table):
    share = table.shape[1] // 4
    quarter = quarter_of()
    cost[...] = cost_in[...]
    for k, part in enumerate((p0, p1, p2, p3)):
        table[:, pl.ds(pl.multiple_of((quarter ^ k) * share, share), share)] = part[SHARES, :, :share]
    build_target(target, lambda s: table[...], c_v, y_v)

    def after(cols, total):
        a2[:, cols] = total

    multiply(target, inv_v, sol, c_v, cost, lambda j: None, w, after)


def right_kernel(w, w_row, level_row, target, c_v, inv_v, cost_in, a2, mass, sol, eta, sums, cost):
    scenarios, length, half = sol.shape
    columns = 2 * half
    cost[...] = cost_in[...]

    def keep(first, value):
        high = value.astype(BF16)
        own = slice(first, first + value.shape[1])
        sums[:, own] = high
        sums[:, columns + own.start : columns + own.stop] = (value - high.astype(F32)).astype(BF16)

    keep(0, a2[...])

    def after(cols, total):
        keep(half + cols.start, total)

    multiply(target, inv_v, sol, c_v, cost, lambda j: None, w, after, half)
    lanes = jnp.sum(cost[...], axis=1)
    scen_cost = jnp.sum(lanes.T, axis=0, keepdims=True) / (3 * length * columns)
    p = w_row[...].astype(F32)
    low = level_row[:, scenarios:] - (CVAR_WEIGHT + level_row[:, :scenarios]) / PENALTY
    high = low + CVAR_WEIGHT / ((1.0 - CVAR_LEVEL) * PENALTY)
    level = jnp.minimum(jnp.maximum(scen_cost, low), high)
    eta[...] = level
    total = jnp.sum(p * level, axis=1, keepdims=True)
    whole = jnp.sum(p, axis=1, keepdims=True)
    row = lax.broadcasted_iota(jnp.int32, (length, LANES), 0)
    scal = jnp.where(row == 0, total, jnp.where(row == 1, whole, jnp.where(row == 2, mass[...], 0.0)))
    sums[:, 2 * columns :] = packed(scal)


def chip_sum_kernel(keep, sent, got, total, send1, send2):
    half = keep.shape[0]
    cut = half - send2.shape[0]
    value = keep[...] + got[:half].astype(F32)
    total[...] = value
    send1[:cut] = value[:cut].astype(BF16)
    send1[cut] = (sent[half].astype(F32) + got[half].astype(F32)).astype(BF16)
    send2[...] = value[cut:].astype(BF16)


def core_sum_kernel(s_own, s_got, scal, a2):
    columns = a2.shape[1]
    scal[...] = packed(unpacked(s_own[:, 2 * columns :]) + unpacked(s_got[:, 2 * columns :]))
    own = s_own[:, :columns].astype(F32) + s_own[:, columns : 2 * columns].astype(F32)
    a2[...] = own + (s_got[:, :columns].astype(F32) + s_got[:, columns : 2 * columns].astype(F32))


def node_sum_kernel(s_own, s_got, sent, got, sums, scal):
    columns = sent.shape[2]
    last = sent.shape[0] - 1
    sums[:, :columns] = (sent[last].astype(F32) + got[last].astype(F32)).astype(BF16)
    value = unpacked(s_own[...]) + unpacked(s_got[...])
    scal[...] = value
    sums[:, columns:] = packed(value)


def far_sum_kernel(s_own, s_got, sums):
    columns = sums.shape[1] - 3 * LANES
    sums[:, :columns] = (s_own[:, :columns].astype(F32) + s_got[:, :columns].astype(F32)).astype(BF16)
    sums[:, columns:] = packed(unpacked(s_own[:, columns:]) + unpacked(s_got[:, columns:]))


def third_avg_kernel(total, got1, got2, scal, avg):
    quarter = quarter_of()
    cut = total.shape[0] - got2.shape[0]
    for k in range(HALF):
        node = ((k // SHARES) * 2 + quarter % 2) * SHARES + k % SHARES
        got = got1[k] if k < cut else got2[k - cut]
        value = (total[k] + got.astype(F32)) / node_mass(scal, node)
        avg[k] = value


def write_duals(sols, y_v, avg_of, out, buf, sems, section):
    scenarios, length, _ = y_v.shape
    group = scenarios // 4

    def copy(g):
        own = pl.ds(g * group, group)
        return pltpu.make_async_copy(
            buf.at[own], out.at[own, pl.ds(section * length, length), :], sems.at[g]
        )

    for g in range(4):
        for s in range(g * group, (g + 1) * group):
            avg = avg_of(s)
            start = 0
            for sol in sols:
                cols = slice(start, start + sol.shape[2])
                fresh = y_v[s, :, cols].astype(F32) + PENALTY * (sol[s] - avg[:, cols])
                buf[s, :, cols] = fresh.astype(BF16)
                start = cols.stop
        copy(g).start()
    return [copy(g) for g in range(4)]


def later_duals_kernel(
    sec, left, right, y2, a_own, a_got, scal, sol3, y3, avg, got,
    out, second_avg, third_avg, buf2, buf3, full, table, sems2, sems3, sems,
):
    _, columns = full.shape
    quarter = quarter_of()
    share = columns // 4
    whole = jnp.sum(scal[2:3, :], axis=1, keepdims=True)
    full[...] = (a_own[...] + a_got[...]) / whole
    own = pl.ds(pl.multiple_of(quarter * share, share), share)
    copies = [
        pltpu.make_async_copy(full.at[:, own], second_avg.at[0], sems.at[0]),
        pltpu.make_async_copy(avg.at[pl.ds((quarter // 2) * SHARES, SHARES)], third_avg, sems.at[1]),
    ]
    for copy in copies:
        copy.start()
    copies += write_duals((left, right), y2, lambda s: full[...], out, buf2, sems2, 1)
    table[:HALF] = avg[...]
    table[HALF:] = got[...]
    copies += write_duals(
        (sol3,), y3, lambda s: table[place_of(sec[s] % BRANCH, quarter)], out, buf3, sems3, 2
    )
    for copy in copies:
        copy.wait()


def last_kernel(
    sol, y_v, s_own, s_got, eta, duals_row, prior,
    out, first_avg, eta_avg, eta_duals, buf, full, row, one, sems, sems2,
):
    columns = full.shape[1]
    scal = unpacked(s_own[:, columns:]) + unpacked(s_got[:, columns:])
    total, mass = scal[0:1, 0:1], scal[1:2, 0:1]
    full[...] = (s_own[:, :columns].astype(F32) + s_got[:, :columns].astype(F32)) / mass
    level = total / mass
    row[...] = duals_row[...] + PENALTY * (eta[...] - level)
    one[0] = jnp.sum(level)
    copies = [
        pltpu.make_async_copy(full, first_avg, sems2.at[0]),
        pltpu.make_async_copy(row, eta_duals, sems2.at[1]),
        pltpu.make_async_copy(one, eta_avg, sems2.at[2]),
    ]
    for copy in copies:
        copy.start()
    copies += write_duals((sol,), y_v, lambda s: full[...], out, buf, sems, 0)
    for copy in copies:
        copy.wait()


def step(
    unit_costs,
    hour_duals,
    inverse,
    weights,
    section_three,
    prev_first,
    prev_second,
    prev_third,
    eta_mean,
    eta_duals,
):
    scenarios, hours, columns = unit_costs.shape
    length = hours // 3
    nodes = lax.axis_size("node")
    dma = pltpu.SemaphoreType.DMA
    shape = jax.ShapeDtypeStruct
    block = (scenarios, length, columns)
    rows = scenarios * length
    w_row = weights.reshape(1, scenarios)
    duals_row = eta_duals.reshape(1, scenarios)
    costs, duals, matrix = in_hbm(unit_costs), in_hbm(hour_duals), in_hbm(inverse)

    tail = jnp.pad(prev_second, ((0, 0), (0, 0), (0, columns - columns // 4)))
    prev = jnp.concatenate((prev_third, tail))
    y_prev = partner(prev, 2)

    w, sec, y1, c2, y2, c3, y3, inv_v, sol1, a1, mass, pick, cost = call(
        first_kernel,
        32,
        in_specs=[HBM] * 8,
        out_specs=[SMEM, SMEM] + [VMEM] * 11,
        out_shape=[
            pltpu.SMEM((scenarios,), jnp.int32),
            pltpu.SMEM((scenarios,), jnp.int32),
            *[pltpu.VMEM(block, BF16)] * 5,
            pltpu.VMEM(inverse.shape, BF16),
            pltpu.VMEM(block, F32),
            pltpu.VMEM((length, columns), F32),
            pltpu.VMEM((1, LANES), F32),
            pltpu.VMEM((BRANCH * length, rows), BF16),
            pltpu.VMEM((scenarios, length, LANES), F32),
        ],
        scratch_shapes=[
            pltpu.VMEM(block, BF16),
            pltpu.VMEM((length, columns), BF16),
            pltpu.VMEM((1, scenarios), jnp.int32),
            pltpu.VMEM((1, scenarios), jnp.int32),
            pltpu.VMEM((rows, columns), BF16),
            dma((11 + CHUNKS,)),
        ],
    )(
        in_hbm(weights),
        in_hbm(section_three),
        in_hbm(w_row),
        in_hbm(section_three.reshape(1, scenarios)),
        in_hbm(prev_first),
        costs,
        duals,
        matrix,
    )

    y_prev, joined = lax.optimization_barrier((y_prev, (eta_mean, eta_duals)))
    level_row = jnp.concatenate((joined[1], joined[0])).reshape(1, scenarios + 1)
    core_prev, diag_prev = partner((prev, y_prev), 1)
    pieces = (prev, core_prev, y_prev, diag_prev)

    sol3, cost, keep, send = call(
        third_kernel,
        30,
        in_specs=[SMEM] + [VMEM] * 10,
        out_specs=[VMEM] * 4,
        out_shape=[
            pltpu.VMEM(block, F32),
            pltpu.VMEM((scenarios, length, LANES), F32),
            pltpu.VMEM((HALF, length, columns), F32),
            pltpu.VMEM((HALF + 1, length, columns), BF16),
        ],
        scratch_shapes=[pltpu.VMEM((rows, columns), BF16), pltpu.VMEM((BRANCH, length, columns), BF16)],
    )(sec, *pieces, c3, y3, inv_v, pick, cost, a1)

    chip_got = partner(send, 1)
    half_block = (scenarios, length, columns // 2)
    target2, left, a2, cost = call(
        left_kernel,
        30,
        in_specs=[SMEM] + [VMEM] * 8,
        out_specs=[VMEM] * 4,
        out_shape=[
            pltpu.VMEM((rows, columns), BF16),
            pltpu.VMEM(half_block, F32),
            pltpu.VMEM((length, columns // 2), F32),
            pltpu.VMEM((scenarios, length, LANES), F32),
        ],
        scratch_shapes=[pltpu.VMEM((length, columns), BF16)],
    )(w, *pieces, c2, y2, inv_v, cost)
    cut = HALF // 2
    chip_total, chip_send1, chip_send2 = call(
        chip_sum_kernel,
        8,
        in_specs=[VMEM] * 3,
        out_specs=[VMEM] * 3,
        out_shape=[
            pltpu.VMEM((HALF, length, columns), F32),
            pltpu.VMEM((cut + 1, length, columns), BF16),
            pltpu.VMEM((HALF - cut, length, columns), BF16),
        ],
    )(keep, send, chip_got)
    node_got1 = partner(chip_send1, 2)

    right, eta, sums = call(
        right_kernel,
        30,
        in_specs=[SMEM] + [VMEM] * 8,
        out_specs=[VMEM] * 3,
        out_shape=[
            pltpu.VMEM(half_block, F32),
            pltpu.VMEM((1, scenarios), F32),
            pltpu.VMEM((length, 2 * columns + 3 * LANES), BF16),
        ],
        scratch_shapes=[pltpu.VMEM((scenarios, length, LANES), F32)],
    )(w, w_row, level_row, target2, c2, inv_v, cost, a2, mass)

    core_sums = partner(sums, 1)
    scal_chip, a2 = call(
        core_sum_kernel,
        8,
        in_specs=[VMEM] * 2,
        out_specs=[VMEM] * 2,
        out_shape=[pltpu.VMEM((length, 3 * LANES), BF16), pltpu.VMEM((length, columns), F32)],
    )(sums, core_sums)
    y_scal = partner(scal_chip, 2)
    node_got2 = partner(chip_send2, 2)
    a2_got = partner(a2, 2)
    far_shape = pltpu.VMEM((length, columns + 3 * LANES), BF16)
    far, scal = call(
        node_sum_kernel,
        8,
        in_specs=[VMEM] * 4,
        out_specs=[VMEM] * 2,
        out_shape=[far_shape, pltpu.VMEM((length, LANES), F32)],
    )(scal_chip, y_scal, chip_send1, node_got1)
    far_got = partner(far, 4)
    mask = 8
    while mask < nodes:
        far = call(far_sum_kernel, 8, in_specs=[VMEM] * 2, out_specs=VMEM, out_shape=far_shape)(far, far_got)
        far_got = partner(far, mask)
        mask *= 2

    buf = pltpu.VMEM(block, BF16)
    duals_shape = shape(hour_duals.shape, BF16)
    avg = call(
        third_avg_kernel, 8, in_specs=[VMEM] * 4, out_specs=VMEM, out_shape=pltpu.VMEM((HALF, length, columns), F32)
    )(chip_total, node_got1, node_got2, scal)
    avg_got = partner(avg, 1)
    out, second_avg, third_avg = call(
        later_duals_kernel,
        12,
        in_specs=[SMEM] + [VMEM] * 10,
        out_specs=[HBM] * 3,
        out_shape=[
            duals_shape,
            shape((1, length, columns // 4), F32),
            shape((SHARES, length, columns), F32),
        ],
        scratch_shapes=[
            buf,
            buf,
            pltpu.VMEM((length, columns), F32),
            pltpu.VMEM((BRANCH, length, columns), F32),
            dma((4,)),
            dma((4,)),
            dma((2,)),
        ],
    )(sec, left, right, y2, a2, a2_got, scal, sol3, y3, avg, avg_got)
    out, first_avg, eta_avg, eta_duals_new = call(
        last_kernel,
        8,
        in_specs=[VMEM] * 6 + [HBM],
        out_specs=[HBM] * 4,
        out_shape=[
            duals_shape,
            shape((length, columns), F32),
            shape((1,), F32),
            shape((1, scenarios), F32),
        ],
        scratch_shapes=[
            buf,
            pltpu.VMEM((length, columns), F32),
            pltpu.VMEM((1, scenarios), F32),
            pltpu.SMEM((1,), F32),
            dma((4,)),
            dma((3,)),
        ],
        input_output_aliases={6: 0},
    )(sol1, y1, far, far_got, eta, duals_row, out)
    return out, first_avg, second_avg, third_avg, eta_avg, eta_duals_new.reshape(scenarios)


def solution(mesh):
    row = P(("groups", "node"))
    in_specs = (row, row, P(), row, row, P("groups"), row, row, P("groups"), row)
    out_specs = (row, P("groups"), row, row, P("groups"), row)
    return jax.shard_map(step, mesh=mesh, in_specs=in_specs, out_specs=out_specs, check_vma=False)
```

```python
import jax
import jax.numpy as jnp
from jax import lax
from jax.experimental import pallas as pl
from jax.experimental.pallas import tpu as pltpu
from jax.sharding import PartitionSpec as P

BRANCH = 16
SHARES = BRANCH // 4
HALF = BRANCH // 2
PENALTY = 1.0
CVAR_WEIGHT = 0.25
CVAR_LEVEL = 0.75
CHUNKS = 4
LANES = 128
F32 = jnp.float32
BF16 = jnp.bfloat16

ANY = pl.BlockSpec(memory_space=pl.ANY)
HBM = pl.BlockSpec(memory_space=pltpu.HBM)
SMEM = pl.BlockSpec(memory_space=pltpu.SMEM)
VMEM = pl.BlockSpec(memory_space=pltpu.VMEM)


def partner(value, mask):
    pairs = [(source, source ^ mask) for source in range(lax.axis_size("node"))]
    return lax.ppermute(value, "node", pairs)


def in_hbm(value):
    return pltpu.with_memory_space_constraint(value, pltpu.HBM)


def call(kernel, mib, **kwargs):
    return pl.pallas_call(kernel, compiler_params=pltpu.CompilerParams(vmem_limit_bytes=mib << 20), **kwargs)


def quarter_of():
    return lax.axis_index("node") % 4


def place_of(node, quarter):
    half = (node // SHARES) % 2
    return ((half ^ (quarter % 2)) * 2 + node // (2 * SHARES)) * SHARES + node % SHARES


def build_target(target, anchor_of, c_v, y_v):
    scenarios, length, _ = c_v.shape
    for i in range(scenarios // 2):
        rows = [
            PENALTY * anchor_of(s).astype(F32) - c_v[s].astype(F32) - y_v[s].astype(F32)
            for s in (2 * i, 2 * i + 1)
        ]
        target[i * 2 * length : (i + 1) * 2 * length, :] = jnp.concatenate(rows, axis=0).astype(BF16)


def multiply(target, inv_v, sol, c_v, cost, before, w, after, start=0):
    scenarios, length, columns = sol.shape
    width = inv_v.shape[1] // CHUNKS

    def product(j):
        before(j)
        sol[:, :, j * width : (j + 1) * width] = jnp.dot(
            target[...], inv_v[:, start + j * width : start + (j + 1) * width], preferred_element_type=F32
        ).reshape(scenarios, length, width)

    def finish(j):
        cols = slice(j * width, (j + 1) * width)
        total = jnp.zeros((length, width), F32)
        for s in range(scenarios):
            own = sol[s, :, cols]
            prod = c_v[s, :, start + cols.start : start + cols.stop].astype(F32) * own
            part = prod[:, :LANES]
            for k in range(1, width // LANES):
                part = part + prod[:, k * LANES : (k + 1) * LANES]
            cost[s] = cost[s] + part
            if w is not None:
                total = total + w[s].astype(F32) * own
        after(cols, total)

    count = columns // width
    for j in range(count):
        product(j)
        if j:
            finish(j - 1)
    finish(count - 1)


def first_kernel(
    w_hbm, sec_hbm, w_row_hbm, sec_row_hbm, pf_hbm, c_hbm, y_hbm, inv_hbm,
    w, sec, y1, c2, y2, c3, y3, inv_v, sol, a1, mass, pick, cost, c1, pf, w_row, sec_row, target, sems,
):
    scenarios, length, columns = sol.shape
    width = columns // CHUNKS

    def chunk(j):
        part = pl.ds(j * width, width)
        return pltpu.make_async_copy(inv_hbm.at[:, part], inv_v.at[:, part], sems.at[11 + j])

    def rows(k, c_v, y_v):
        own = pl.ds(k * length, length)
        return [
            pltpu.make_async_copy(c_hbm.at[:, own, :], c_v, sems.at[5 + 2 * k]),
            pltpu.make_async_copy(y_hbm.at[:, own, :], y_v, sems.at[6 + 2 * k]),
        ]

    small = [
        pltpu.make_async_copy(source, into, sems.at[k])
        for k, (source, into) in enumerate(
            ((w_row_hbm, w_row), (sec_row_hbm, sec_row), (w_hbm, w), (sec_hbm, sec), (pf_hbm, pf))
        )
    ]
    first = rows(0, c1, y1)
    later = rows(2, c3, y3) + rows(1, c2, y2)
    for copy in small + first + [chunk(j) for j in range(CHUNKS)] + later:
        copy.start()
    cost[...] = jnp.zeros_like(cost)
    for copy in small:
        copy.wait()

    node = sec_row[...] % BRANCH
    place = place_of(node, quarter_of())
    p = w_row[...].astype(F32)
    into_node = lax.broadcasted_iota(jnp.int32, (LANES, scenarios), 0) == node
    mass[...] = jnp.sum(jnp.where(into_node, p, 0.0).T, axis=0, keepdims=True)
    into_place = lax.broadcasted_iota(jnp.int32, (BRANCH * length, scenarios), 0) // length == place
    shape = (scenarios, scenarios * length)
    spread = lax.broadcasted_iota(jnp.int32, shape, 1) // length == lax.broadcasted_iota(jnp.int32, shape, 0)
    weight = jnp.dot(
        jnp.where(into_place, p, 0.0).astype(BF16),
        jnp.where(spread, 1.0, 0.0).astype(BF16),
        preferred_element_type=F32,
    )
    row = lax.broadcasted_iota(jnp.int32, pick.shape, 0)
    column = lax.broadcasted_iota(jnp.int32, pick.shape, 1)
    pick[...] = jnp.where(row % length == column % length, weight, 0.0).astype(BF16)

    for copy in first:
        copy.wait()
    build_target(target, lambda s: pf[...], c1, y1)

    def after(cols, total):
        a1[:, cols] = total

    multiply(target, inv_v, sol, c1, cost, lambda j: chunk(j).wait(), w, after)
    for copy in later:
        copy.wait()


def packed(value):
    high = value.astype(BF16)
    rest = value - high.astype(F32)
    middle = rest.astype(BF16)
    return jnp.concatenate((high, middle, (rest - middle.astype(F32)).astype(BF16)), axis=1)


def unpacked(tiles):
    high, middle, low = (tiles[:, k * LANES : (k + 1) * LANES].astype(F32) for k in range(3))
    return high + middle + low


def node_mass(scal, node):
    row = scal[2:3, :]
    slot = lax.broadcasted_iota(jnp.int32, row.shape, 1)
    return jnp.sum(jnp.where(slot == node, row, 0.0), axis=1, keepdims=True)


def third_kernel(
    sec, p0, p1, p2, p3, c_v, y_v, inv_v, pick, cost_in, a1, sol, cost, keep, send, target, table
):
    scenarios, length, _ = sol.shape
    quarter = quarter_of()
    send[HALF] = a1[...].astype(BF16)
    cost[...] = cost_in[...]
    for k, part in enumerate((p0, p1, p2, p3)):
        table[k * SHARES : (k + 1) * SHARES] = part[:SHARES]

    def anchor_of(s):
        node = sec[s] % BRANCH
        return table[((node // SHARES) ^ quarter) * SHARES + node % SHARES]

    build_target(target, anchor_of, c_v, y_v)

    def after(cols, total):
        own = sol[:, :, cols]
        flat = own.reshape(scenarios * length, own.shape[2]).astype(BF16)
        sums = jnp.dot(pick[...], flat, preferred_element_type=F32).reshape(BRANCH, length, own.shape[2])
        keep[:, :, cols] = sums[:HALF]
        send[:HALF, :, cols] = sums[HALF:].astype(BF16)

    multiply(target, inv_v, sol, c_v, cost, lambda j: None, None, after)


def left_kernel(w, p0, p1, p2, p3, c_v, y_v, inv_v, cost_in, target, sol, a2, cost, table):
    share = table.shape[1] // 4
    quarter = quarter_of()
    cost[...] = cost_in[...]
    for k, part in enumerate((p0, p1, p2, p3)):
        table[:, pl.ds(pl.multiple_of((quarter ^ k) * share, share), share)] = part[SHARES, :, :share]
    build_target(target, lambda s: table[...], c_v, y_v)

    def after(cols, total):
        a2[:, cols] = total

    multiply(target, inv_v, sol, c_v, cost, lambda j: None, w, after)


def right_kernel(w, w_row, level_row, target, c_v, inv_v, cost_in, a2, mass, sol, eta, sums, cost):
    scenarios, length, half = sol.shape
    columns = 2 * half
    cost[...] = cost_in[...]

    def keep(first, value):
        high = value.astype(BF16)
        own = slice(first, first + value.shape[1])
        sums[:, own] = high
        sums[:, columns + own.start : columns + own.stop] = (value - high.astype(F32)).astype(BF16)

    keep(0, a2[...])

    def after(cols, total):
        keep(half + cols.start, total)

    multiply(target, inv_v, sol, c_v, cost, lambda j: None, w, after, half)
    lanes = jnp.sum(cost[...], axis=1)
    scen_cost = jnp.sum(lanes.T, axis=0, keepdims=True) / (3 * length * columns)
    p = w_row[...].astype(F32)
    low = level_row[:, scenarios:] - (CVAR_WEIGHT + level_row[:, :scenarios]) / PENALTY
    high = low + CVAR_WEIGHT / ((1.0 - CVAR_LEVEL) * PENALTY)
    level = jnp.minimum(jnp.maximum(scen_cost, low), high)
    eta[...] = level
    total = jnp.sum(p * level, axis=1, keepdims=True)
    whole = jnp.sum(p, axis=1, keepdims=True)
    row = lax.broadcasted_iota(jnp.int32, (length, LANES), 0)
    scal = jnp.where(row == 0, total, jnp.where(row == 1, whole, jnp.where(row == 2, mass[...], 0.0)))
    sums[:, 2 * columns :] = packed(scal)


def chip_sum_kernel(keep, sent, got, total, send1, send2):
    half = keep.shape[0]
    cut = half - send2.shape[0]
    value = keep[...] + got[:half].astype(F32)
    total[...] = value
    send1[:cut] = value[:cut].astype(BF16)
    send1[cut] = (sent[half].astype(F32) + got[half].astype(F32)).astype(BF16)
    send2[...] = value[cut:].astype(BF16)


def core_sum_kernel(s_own, s_got, scal, a2):
    columns = a2.shape[1]
    scal[...] = packed(unpacked(s_own[:, 2 * columns :]) + unpacked(s_got[:, 2 * columns :]))
    own = s_own[:, :columns].astype(F32) + s_own[:, columns : 2 * columns].astype(F32)
    a2[...] = own + (s_got[:, :columns].astype(F32) + s_got[:, columns : 2 * columns].astype(F32))


def node_sum_kernel(s_own, s_got, sent, got, sums, scal):
    columns = sent.shape[2]
    last = sent.shape[0] - 1
    sums[:, :columns] = (sent[last].astype(F32) + got[last].astype(F32)).astype(BF16)
    value = unpacked(s_own[...]) + unpacked(s_got[...])
    scal[...] = value
    sums[:, columns:] = packed(value)


def far_sum_kernel(s_own, s_got, sums):
    columns = sums.shape[1] - 3 * LANES
    sums[:, :columns] = (s_own[:, :columns].astype(F32) + s_got[:, :columns].astype(F32)).astype(BF16)
    sums[:, columns:] = packed(unpacked(s_own[:, columns:]) + unpacked(s_got[:, columns:]))


def third_avg_kernel(total, got1, got2, scal, avg):
    quarter = quarter_of()
    cut = total.shape[0] - got2.shape[0]
    for k in range(HALF):
        node = ((k // SHARES) * 2 + quarter % 2) * SHARES + k % SHARES
        got = got1[k] if k < cut else got2[k - cut]
        value = (total[k] + got.astype(F32)) / node_mass(scal, node)
        avg[k] = value


def write_duals(sols, y_v, avg_of, out, buf, sems, section):
    scenarios, length, _ = buf.shape
    group = scenarios // 4

    def copy(g):
        own = pl.ds(g * group, group)
        return pltpu.make_async_copy(
            buf.at[own], out.at[own, pl.ds(section * length, length), :], sems.at[g]
        )

    for g in range(4):
        for s in range(g * group, (g + 1) * group):
            avg = avg_of(s)
            start = 0
            for sol in sols:
                cols = slice(start, start + sol.shape[2])
                if y_v is None:
                    fresh = sol[s] - PENALTY * avg[:, cols]
                else:
                    fresh = y_v[s, :, cols].astype(F32) + PENALTY * (sol[s] - avg[:, cols])
                buf[s, :, cols] = fresh.astype(BF16)
                start = cols.stop
        copy(g).start()
    return [copy(g) for g in range(4)]


def later_duals_kernel(
    sec, left, right, y2, a_own, a_got, scal, sol3, y3, avg, got, sol1, y1,
    base, out, second_avg, third_avg, buf2, buf3, full, table, sems2, sems3, sems,
):
    _, columns = full.shape
    quarter = quarter_of()
    share = columns // 4
    whole = jnp.sum(scal[2:3, :], axis=1, keepdims=True)
    full[...] = (a_own[...] + a_got[...]) / whole
    own = pl.ds(pl.multiple_of(quarter * share, share), share)
    copies = [
        pltpu.make_async_copy(full.at[:, own], second_avg.at[0], sems.at[0]),
        pltpu.make_async_copy(avg.at[pl.ds((quarter // 2) * SHARES, SHARES)], third_avg, sems.at[1]),
    ]
    for copy in copies:
        copy.start()
    copies += write_duals((left, right), y2, lambda s: full[...], out, buf2, sems2, 1)
    table[:HALF] = avg[...]
    table[HALF:] = got[...]
    copies += write_duals(
        (sol3,), y3, lambda s: table[place_of(sec[s] % BRANCH, quarter)], out, buf3, sems3, 2
    )
    for k in range(sol1.shape[0]):
        base[k] = y1[k].astype(F32) + PENALTY * sol1[k]
    for copy in copies:
        copy.wait()


def last_kernel(
    base, s_own, s_got, eta, duals_row, prior,
    out, first_avg, eta_avg, eta_duals, buf, full, row, one, sems, sems2,
):
    columns = full.shape[1]
    scal = unpacked(s_own[:, columns:]) + unpacked(s_got[:, columns:])
    total, mass = scal[0:1, 0:1], scal[1:2, 0:1]
    full[...] = (s_own[:, :columns].astype(F32) + s_got[:, :columns].astype(F32)) / mass
    level = total / mass
    row[...] = duals_row[...] + PENALTY * (eta[...] - level)
    one[0] = jnp.sum(level)
    copies = [
        pltpu.make_async_copy(full, first_avg, sems2.at[0]),
        pltpu.make_async_copy(row, eta_duals, sems2.at[1]),
        pltpu.make_async_copy(one, eta_avg, sems2.at[2]),
    ]
    for copy in copies:
        copy.start()
    copies += write_duals((base,), None, lambda s: full[...], out, buf, sems, 0)
    for copy in copies:
        copy.wait()


def step(
    unit_costs,
    hour_duals,
    inverse,
    weights,
    section_three,
    prev_first,
    prev_second,
    prev_third,
    eta_mean,
    eta_duals,
):
    scenarios, hours, columns = unit_costs.shape
    length = hours // 3
    nodes = lax.axis_size("node")
    dma = pltpu.SemaphoreType.DMA
    shape = jax.ShapeDtypeStruct
    block = (scenarios, length, columns)
    rows = scenarios * length
    w_row = weights.reshape(1, scenarios)
    duals_row = eta_duals.reshape(1, scenarios)
    costs, duals, matrix = in_hbm(unit_costs), in_hbm(hour_duals), in_hbm(inverse)

    tail = jnp.pad(prev_second, ((0, 0), (0, 0), (0, columns - columns // 4)))
    prev = jnp.concatenate((prev_third, tail))
    y_prev = partner(prev, 2)

    w, sec, y1, c2, y2, c3, y3, inv_v, sol1, a1, mass, pick, cost = call(
        first_kernel,
        32,
        in_specs=[HBM] * 8,
        out_specs=[SMEM, SMEM] + [VMEM] * 11,
        out_shape=[
            pltpu.SMEM((scenarios,), jnp.int32),
            pltpu.SMEM((scenarios,), jnp.int32),
            *[pltpu.VMEM(block, BF16)] * 5,
            pltpu.VMEM(inverse.shape, BF16),
            pltpu.VMEM(block, F32),
            pltpu.VMEM((length, columns), F32),
            pltpu.VMEM((1, LANES), F32),
            pltpu.VMEM((BRANCH * length, rows), BF16),
            pltpu.VMEM((scenarios, length, LANES), F32),
        ],
        scratch_shapes=[
            pltpu.VMEM(block, BF16),
            pltpu.VMEM((length, columns), BF16),
            pltpu.VMEM((1, scenarios), jnp.int32),
            pltpu.VMEM((1, scenarios), jnp.int32),
            pltpu.VMEM((rows, columns), BF16),
            dma((11 + CHUNKS,)),
        ],
    )(
        in_hbm(weights),
        in_hbm(section_three),
        in_hbm(w_row),
        in_hbm(section_three.reshape(1, scenarios)),
        in_hbm(prev_first),
        costs,
        duals,
        matrix,
    )

    y_prev, joined = lax.optimization_barrier((y_prev, (eta_mean, eta_duals)))
    level_row = jnp.concatenate((joined[1], joined[0])).reshape(1, scenarios + 1)
    core_prev, diag_prev = partner((prev, y_prev), 1)
    pieces = (prev, core_prev, y_prev, diag_prev)

    sol3, cost, keep, send = call(
        third_kernel,
        30,
        in_specs=[SMEM] + [VMEM] * 10,
        out_specs=[VMEM] * 4,
        out_shape=[
            pltpu.VMEM(block, F32),
            pltpu.VMEM((scenarios, length, LANES), F32),
            pltpu.VMEM((HALF, length, columns), F32),
            pltpu.VMEM((HALF + 1, length, columns), BF16),
        ],
        scratch_shapes=[pltpu.VMEM((rows, columns), BF16), pltpu.VMEM((BRANCH, length, columns), BF16)],
    )(sec, *pieces, c3, y3, inv_v, pick, cost, a1)

    chip_got = partner(send, 1)
    half_block = (scenarios, length, columns // 2)
    target2, left, a2, cost = call(
        left_kernel,
        30,
        in_specs=[SMEM] + [VMEM] * 8,
        out_specs=[VMEM] * 4,
        out_shape=[
            pltpu.VMEM((rows, columns), BF16),
            pltpu.VMEM(half_block, F32),
            pltpu.VMEM((length, columns // 2), F32),
            pltpu.VMEM((scenarios, length, LANES), F32),
        ],
        scratch_shapes=[pltpu.VMEM((length, columns), BF16)],
    )(w, *pieces, c2, y2, inv_v, cost)
    cut = HALF // 2
    chip_total, chip_send1, chip_send2 = call(
        chip_sum_kernel,
        8,
        in_specs=[VMEM] * 3,
        out_specs=[VMEM] * 3,
        out_shape=[
            pltpu.VMEM((HALF, length, columns), F32),
            pltpu.VMEM((cut + 1, length, columns), BF16),
            pltpu.VMEM((HALF - cut, length, columns), BF16),
        ],
    )(keep, send, chip_got)
    node_got1 = partner(chip_send1, 2)

    right, eta, sums = call(
        right_kernel,
        30,
        in_specs=[SMEM] + [VMEM] * 8,
        out_specs=[VMEM] * 3,
        out_shape=[
            pltpu.VMEM(half_block, F32),
            pltpu.VMEM((1, scenarios), F32),
            pltpu.VMEM((length, 2 * columns + 3 * LANES), BF16),
        ],
        scratch_shapes=[pltpu.VMEM((scenarios, length, LANES), F32)],
    )(w, w_row, level_row, target2, c2, inv_v, cost, a2, mass)

    core_sums = partner(sums, 1)
    scal_chip, a2 = call(
        core_sum_kernel,
        8,
        in_specs=[VMEM] * 2,
        out_specs=[VMEM] * 2,
        out_shape=[pltpu.VMEM((length, 3 * LANES), BF16), pltpu.VMEM((length, columns), F32)],
    )(sums, core_sums)
    y_scal = partner(scal_chip, 2)
    node_got2 = partner(chip_send2, 2)
    a2_got = partner(a2, 2)
    far_shape = pltpu.VMEM((length, columns + 3 * LANES), BF16)
    far, scal = call(
        node_sum_kernel,
        8,
        in_specs=[VMEM] * 4,
        out_specs=[VMEM] * 2,
        out_shape=[far_shape, pltpu.VMEM((length, LANES), F32)],
    )(scal_chip, y_scal, chip_send1, node_got1)
    far_got = partner(far, 4)
    mask = 8
    while mask < nodes:
        far = call(far_sum_kernel, 8, in_specs=[VMEM] * 2, out_specs=VMEM, out_shape=far_shape)(far, far_got)
        far_got = partner(far, mask)
        mask *= 2

    buf = pltpu.VMEM(block, BF16)
    duals_shape = shape(hour_duals.shape, BF16)
    avg = call(
        third_avg_kernel, 8, in_specs=[VMEM] * 4, out_specs=VMEM, out_shape=pltpu.VMEM((HALF, length, columns), F32)
    )(chip_total, node_got1, node_got2, scal)
    avg_got = partner(avg, 1)
    base1, out, second_avg, third_avg = call(
        later_duals_kernel,
        12,
        in_specs=[SMEM] + [VMEM] * 12,
        out_specs=[VMEM] + [HBM] * 3,
        out_shape=[
            pltpu.VMEM(block, F32),
            duals_shape,
            shape((1, length, columns // 4), F32),
            shape((SHARES, length, columns), F32),
        ],
        scratch_shapes=[
            buf,
            buf,
            pltpu.VMEM((length, columns), F32),
            pltpu.VMEM((BRANCH, length, columns), F32),
            dma((4,)),
            dma((4,)),
            dma((2,)),
        ],
    )(sec, left, right, y2, a2, a2_got, scal, sol3, y3, avg, avg_got, sol1, y1)
    out, first_avg, eta_avg, eta_duals_new = call(
        last_kernel,
        8,
        in_specs=[VMEM] * 5 + [HBM],
        out_specs=[HBM] * 4,
        out_shape=[
            duals_shape,
            shape((length, columns), F32),
            shape((1,), F32),
            shape((1, scenarios), F32),
        ],
        scratch_shapes=[
            buf,
            pltpu.VMEM((length, columns), F32),
            pltpu.VMEM((1, scenarios), F32),
            pltpu.SMEM((1,), F32),
            dma((4,)),
            dma((3,)),
        ],
        input_output_aliases={5: 0},
    )(base1, far, far_got, eta, duals_row, out)
    return out, first_avg, second_avg, third_avg, eta_avg, eta_duals_new.reshape(scenarios)


def solution(mesh):
    row = P(("groups", "node"))
    in_specs = (row, row, P(), row, row, P("groups"), row, row, P("groups"), row)
    out_specs = (row, P("groups"), row, row, P("groups"), row)
    return jax.shard_map(step, mesh=mesh, in_specs=in_specs, out_specs=out_specs, check_vma=False)
```

```python
import jax
import jax.numpy as jnp
from jax import lax
from jax.experimental import pallas as pl
from jax.experimental.pallas import tpu as pltpu
from jax.sharding import PartitionSpec as P

BRANCH = 16
SHARES = BRANCH // 4
HALF = BRANCH // 2
PENALTY = 1.0
CVAR_WEIGHT = 0.25
CVAR_LEVEL = 0.75
CHUNKS = 4
LANES = 128
F32 = jnp.float32
BF16 = jnp.bfloat16

ANY = pl.BlockSpec(memory_space=pl.ANY)
HBM = pl.BlockSpec(memory_space=pltpu.HBM)
SMEM = pl.BlockSpec(memory_space=pltpu.SMEM)
VMEM = pl.BlockSpec(memory_space=pltpu.VMEM)


def partner(value, mask):
    pairs = [(source, source ^ mask) for source in range(lax.axis_size("node"))]
    return lax.ppermute(value, "node", pairs)


def in_hbm(value):
    return pltpu.with_memory_space_constraint(value, pltpu.HBM)


def call(kernel, mib, **kwargs):
    return pl.pallas_call(kernel, compiler_params=pltpu.CompilerParams(vmem_limit_bytes=mib << 20), **kwargs)


def quarter_of():
    return lax.axis_index("node") % 4


def place_of(node, quarter):
    half = (node // SHARES) % 2
    return ((half ^ (quarter % 2)) * 2 + node // (2 * SHARES)) * SHARES + node % SHARES


def build_target(target, anchor_of, c_v, y_v, span=None):
    scenarios, length, _ = c_v.shape
    for i in span or range(scenarios // 2):
        rows = [
            PENALTY * anchor_of(s).astype(F32) - c_v[s].astype(F32) - y_v[s].astype(F32)
            for s in (2 * i, 2 * i + 1)
        ]
        target[i * 2 * length : (i + 1) * 2 * length, :] = jnp.concatenate(rows, axis=0).astype(BF16)


def multiply(target, inv_v, sol, c_v, cost, before, w, after, start=0):
    scenarios, length, columns = sol.shape
    width = inv_v.shape[1] // CHUNKS

    def product(j):
        before(j)
        sol[:, :, j * width : (j + 1) * width] = jnp.dot(
            target[...], inv_v[:, start + j * width : start + (j + 1) * width], preferred_element_type=F32
        ).reshape(scenarios, length, width)

    def finish(j):
        cols = slice(j * width, (j + 1) * width)
        total = jnp.zeros((length, width), F32)
        for s in range(scenarios):
            own = sol[s, :, cols]
            prod = c_v[s, :, start + cols.start : start + cols.stop].astype(F32) * own
            part = prod[:, :LANES]
            for k in range(1, width // LANES):
                part = part + prod[:, k * LANES : (k + 1) * LANES]
            cost[s] = cost[s] + part
            if w is not None:
                total = total + w[s].astype(F32) * own
        after(cols, total)

    count = columns // width
    for j in range(count):
        product(j)
        if j:
            finish(j - 1)
    finish(count - 1)


def first_kernel(
    w_hbm, sec_hbm, w_row_hbm, sec_row_hbm, pf_hbm, c_hbm, y_hbm, inv_hbm,
    w, sec, y1, c2, y2, c3, y3, inv_v, sol, a1, mass, pick, cost, c1, pf, w_row, sec_row, target, sems,
):
    scenarios, length, columns = sol.shape
    width = columns // CHUNKS

    def chunk(j):
        part = pl.ds(j * width, width)
        return pltpu.make_async_copy(inv_hbm.at[:, part], inv_v.at[:, part], sems.at[11 + j])

    def rows(k, c_v, y_v):
        own = pl.ds(k * length, length)
        return [
            pltpu.make_async_copy(c_hbm.at[:, own, :], c_v, sems.at[5 + 2 * k]),
            pltpu.make_async_copy(y_hbm.at[:, own, :], y_v, sems.at[6 + 2 * k]),
        ]

    def part_rows(g):
        own = pl.ds(0, length)
        some = pl.ds(g * scenarios // 2, scenarios // 2)
        return [
            pltpu.make_async_copy(c_hbm.at[some, own, :], c1.at[some], sems.at[5 if g else 11 + CHUNKS]),
            pltpu.make_async_copy(y_hbm.at[some, own, :], y1.at[some], sems.at[6 if g else 12 + CHUNKS]),
        ]

    small = [
        pltpu.make_async_copy(source, into, sems.at[k])
        for k, (source, into) in enumerate(
            ((w_row_hbm, w_row), (sec_row_hbm, sec_row), (w_hbm, w), (sec_hbm, sec), (pf_hbm, pf))
        )
    ]
    first = part_rows(0) + part_rows(1)
    later = rows(2, c3, y3) + rows(1, c2, y2)
    for copy in small + first + [chunk(j) for j in range(CHUNKS)] + later:
        copy.start()
    cost[...] = jnp.zeros_like(cost)
    for copy in small:
        copy.wait()

    node = sec_row[...] % BRANCH
    place = place_of(node, quarter_of())
    p = w_row[...].astype(F32)
    into_node = lax.broadcasted_iota(jnp.int32, (LANES, scenarios), 0) == node
    mass[...] = jnp.sum(jnp.where(into_node, p, 0.0).T, axis=0, keepdims=True)
    into_place = lax.broadcasted_iota(jnp.int32, (BRANCH * length, scenarios), 0) // length == place
    shape = (scenarios, scenarios * length)
    spread = lax.broadcasted_iota(jnp.int32, shape, 1) // length == lax.broadcasted_iota(jnp.int32, shape, 0)
    weight = jnp.dot(
        jnp.where(into_place, p, 0.0).astype(BF16),
        jnp.where(spread, 1.0, 0.0).astype(BF16),
        preferred_element_type=F32,
    )
    row = lax.broadcasted_iota(jnp.int32, pick.shape, 0)
    column = lax.broadcasted_iota(jnp.int32, pick.shape, 1)
    pick[...] = jnp.where(row % length == column % length, weight, 0.0).astype(BF16)

    for copy in first[:2]:
        copy.wait()
    build_target(target, lambda s: pf[...], c1, y1, range(scenarios // 4))
    for copy in first[2:]:
        copy.wait()
    build_target(target, lambda s: pf[...], c1, y1, range(scenarios // 4, scenarios // 2))

    def after(cols, total):
        a1[:, cols] = total

    multiply(target, inv_v, sol, c1, cost, lambda j: chunk(j).wait(), w, after)
    for copy in later:
        copy.wait()


def packed(value):
    high = value.astype(BF16)
    rest = value - high.astype(F32)
    middle = rest.astype(BF16)
    return jnp.concatenate((high, middle, (rest - middle.astype(F32)).astype(BF16)), axis=1)


def unpacked(tiles):
    high, middle, low = (tiles[:, k * LANES : (k + 1) * LANES].astype(F32) for k in range(3))
    return high + middle + low


def node_mass(scal, node):
    row = scal[2:3, :]
    slot = lax.broadcasted_iota(jnp.int32, row.shape, 1)
    return jnp.sum(jnp.where(slot == node, row, 0.0), axis=1, keepdims=True)


def third_kernel(
    sec, p0, p1, p2, p3, c_v, y_v, inv_v, pick, cost_in, a1, sol, cost, keep, send, target, table
):
    scenarios, length, _ = sol.shape
    quarter = quarter_of()
    send[HALF] = a1[...].astype(BF16)
    cost[...] = cost_in[...]
    for k, part in enumerate((p0, p1, p2, p3)):
        table[k * SHARES : (k + 1) * SHARES] = part[:SHARES]

    def anchor_of(s):
        node = sec[s] % BRANCH
        return table[((node // SHARES) ^ quarter) * SHARES + node % SHARES]

    build_target(target, anchor_of, c_v, y_v)

    def after(cols, total):
        own = sol[:, :, cols]
        flat = own.reshape(scenarios * length, own.shape[2]).astype(BF16)
        sums = jnp.dot(pick[...], flat, preferred_element_type=F32).reshape(BRANCH, length, own.shape[2])
        keep[:, :, cols] = sums[:HALF]
        send[:HALF, :, cols] = sums[HALF:].astype(BF16)

    multiply(target, inv_v, sol, c_v, cost, lambda j: None, None, after)


def left_kernel(w, p0, p1, p2, p3, c_v, y_v, inv_v, cost_in, target, sol, a2, cost, table):
    share = table.shape[1] // 4
    quarter = quarter_of()
    cost[...] = cost_in[...]
    for k, part in enumerate((p0, p1, p2, p3)):
        table[:, pl.ds(pl.multiple_of((quarter ^ k) * share, share), share)] = part[SHARES, :, :share]
    build_target(target, lambda s: table[...], c_v, y_v)

    def after(cols, total):
        a2[:, cols] = total

    multiply(target, inv_v, sol, c_v, cost, lambda j: None, w, after)


def right_kernel(w, w_row, level_row, target, c_v, inv_v, cost_in, a2, mass, sol, eta, sums, cost):
    scenarios, length, half = sol.shape
    columns = 2 * half
    cost[...] = cost_in[...]

    def keep(first, value):
        high = value.astype(BF16)
        own = slice(first, first + value.shape[1])
        sums[:, own] = high
        sums[:, columns + own.start : columns + own.stop] = (value - high.astype(F32)).astype(BF16)

    keep(0, a2[...])

    def after(cols, total):
        keep(half + cols.start, total)

    multiply(target, inv_v, sol, c_v, cost, lambda j: None, w, after, half)
    lanes = jnp.sum(cost[...], axis=1)
    scen_cost = jnp.sum(lanes.T, axis=0, keepdims=True) / (3 * length * columns)
    p = w_row[...].astype(F32)
    low = level_row[:, scenarios:] - (CVAR_WEIGHT + level_row[:, :scenarios]) / PENALTY
    high = low + CVAR_WEIGHT / ((1.0 - CVAR_LEVEL) * PENALTY)
    level = jnp.minimum(jnp.maximum(scen_cost, low), high)
    eta[...] = level
    total = jnp.sum(p * level, axis=1, keepdims=True)
    whole = jnp.sum(p, axis=1, keepdims=True)
    row = lax.broadcasted_iota(jnp.int32, (length, LANES), 0)
    scal = jnp.where(row == 0, total, jnp.where(row == 1, whole, jnp.where(row == 2, mass[...], 0.0)))
    sums[:, 2 * columns :] = packed(scal)


def chip_sum_kernel(keep, sent, got, total, send1, send2):
    half = keep.shape[0]
    cut = half - send2.shape[0]
    value = keep[...] + got[:half].astype(F32)
    total[...] = value
    send1[:cut] = value[:cut].astype(BF16)
    send1[cut] = (sent[half].astype(F32) + got[half].astype(F32)).astype(BF16)
    send2[...] = value[cut:].astype(BF16)


def core_sum_kernel(s_own, s_got, scal, a2):
    columns = a2.shape[1]
    scal[...] = packed(unpacked(s_own[:, 2 * columns :]) + unpacked(s_got[:, 2 * columns :]))
    own = s_own[:, :columns].astype(F32) + s_own[:, columns : 2 * columns].astype(F32)
    a2[...] = own + (s_got[:, :columns].astype(F32) + s_got[:, columns : 2 * columns].astype(F32))


def node_sum_kernel(s_own, s_got, sent, got, sums, scal):
    columns = sent.shape[2]
    last = sent.shape[0] - 1
    sums[:, :columns] = (sent[last].astype(F32) + got[last].astype(F32)).astype(BF16)
    value = unpacked(s_own[...]) + unpacked(s_got[...])
    scal[...] = value
    sums[:, columns:] = packed(value)


def far_sum_kernel(s_own, s_got, sums):
    columns = sums.shape[1] - 3 * LANES
    sums[:, :columns] = (s_own[:, :columns].astype(F32) + s_got[:, :columns].astype(F32)).astype(BF16)
    sums[:, columns:] = packed(unpacked(s_own[:, columns:]) + unpacked(s_got[:, columns:]))


def third_avg_kernel(total, got1, got2, scal, avg):
    quarter = quarter_of()
    cut = total.shape[0] - got2.shape[0]
    for k in range(HALF):
        node = ((k // SHARES) * 2 + quarter % 2) * SHARES + k % SHARES
        got = got1[k] if k < cut else got2[k - cut]
        value = (total[k] + got.astype(F32)) / node_mass(scal, node)
        avg[k] = value


def write_duals(sols, y_v, avg_of, out, buf, sems, section):
    scenarios, length, _ = buf.shape
    group = scenarios // 4

    def copy(g):
        own = pl.ds(g * group, group)
        return pltpu.make_async_copy(
            buf.at[own], out.at[own, pl.ds(section * length, length), :], sems.at[g]
        )

    for g in range(4):
        for s in range(g * group, (g + 1) * group):
            avg = avg_of(s)
            start = 0
            for sol in sols:
                cols = slice(start, start + sol.shape[2])
                if y_v is None:
                    fresh = sol[s] - PENALTY * avg[:, cols]
                else:
                    fresh = y_v[s, :, cols].astype(F32) + PENALTY * (sol[s] - avg[:, cols])
                buf[s, :, cols] = fresh.astype(BF16)
                start = cols.stop
        copy(g).start()
    return [copy(g) for g in range(4)]


def later_duals_kernel(
    sec, left, right, y2, a_own, a_got, scal, sol3, y3, avg, got, sol1, y1,
    base, out, second_avg, third_avg, buf2, buf3, full, table, sems2, sems3, sems,
):
    _, columns = full.shape
    quarter = quarter_of()
    share = columns // 4
    whole = jnp.sum(scal[2:3, :], axis=1, keepdims=True)
    full[...] = (a_own[...] + a_got[...]) / whole
    own = pl.ds(pl.multiple_of(quarter * share, share), share)
    copies = [
        pltpu.make_async_copy(full.at[:, own], second_avg.at[0], sems.at[0]),
        pltpu.make_async_copy(avg.at[pl.ds((quarter // 2) * SHARES, SHARES)], third_avg, sems.at[1]),
    ]
    for copy in copies:
        copy.start()
    copies += write_duals((left, right), y2, lambda s: full[...], out, buf2, sems2, 1)
    table[:HALF] = avg[...]
    table[HALF:] = got[...]
    copies += write_duals(
        (sol3,), y3, lambda s: table[place_of(sec[s] % BRANCH, quarter)], out, buf3, sems3, 2
    )
    for k in range(sol1.shape[0]):
        base[k] = y1[k].astype(F32) + PENALTY * sol1[k]
    for copy in copies:
        copy.wait()


def last_kernel(
    base, s_own, s_got, eta, duals_row, prior,
    out, first_avg, eta_avg, eta_duals, buf, full, row, one, sems, sems2,
):
    columns = full.shape[1]
    scal = unpacked(s_own[:, columns:]) + unpacked(s_got[:, columns:])
    total, mass = scal[0:1, 0:1], scal[1:2, 0:1]
    full[...] = (s_own[:, :columns].astype(F32) + s_got[:, :columns].astype(F32)) / mass
    level = total / mass
    row[...] = duals_row[...] + PENALTY * (eta[...] - level)
    one[0] = jnp.sum(level)
    copies = [
        pltpu.make_async_copy(full, first_avg, sems2.at[0]),
        pltpu.make_async_copy(row, eta_duals, sems2.at[1]),
        pltpu.make_async_copy(one, eta_avg, sems2.at[2]),
    ]
    for copy in copies:
        copy.start()
    copies += write_duals((base,), None, lambda s: full[...], out, buf, sems, 0)
    for copy in copies:
        copy.wait()


def step(
    unit_costs,
    hour_duals,
    inverse,
    weights,
    section_three,
    prev_first,
    prev_second,
    prev_third,
    eta_mean,
    eta_duals,
):
    scenarios, hours, columns = unit_costs.shape
    length = hours // 3
    nodes = lax.axis_size("node")
    dma = pltpu.SemaphoreType.DMA
    shape = jax.ShapeDtypeStruct
    block = (scenarios, length, columns)
    rows = scenarios * length
    w_row = weights.reshape(1, scenarios)
    duals_row = eta_duals.reshape(1, scenarios)
    costs, duals, matrix = in_hbm(unit_costs), in_hbm(hour_duals), in_hbm(inverse)

    tail = jnp.pad(prev_second, ((0, 0), (0, 0), (0, columns - columns // 4)))
    prev = jnp.concatenate((prev_third, tail))
    y_prev = partner(prev, 2)

    w, sec, y1, c2, y2, c3, y3, inv_v, sol1, a1, mass, pick, cost = call(
        first_kernel,
        32,
        in_specs=[HBM] * 8,
        out_specs=[SMEM, SMEM] + [VMEM] * 11,
        out_shape=[
            pltpu.SMEM((scenarios,), jnp.int32),
            pltpu.SMEM((scenarios,), jnp.int32),
            *[pltpu.VMEM(block, BF16)] * 5,
            pltpu.VMEM(inverse.shape, BF16),
            pltpu.VMEM(block, F32),
            pltpu.VMEM((length, columns), F32),
            pltpu.VMEM((1, LANES), F32),
            pltpu.VMEM((BRANCH * length, rows), BF16),
            pltpu.VMEM((scenarios, length, LANES), F32),
        ],
        scratch_shapes=[
            pltpu.VMEM(block, BF16),
            pltpu.VMEM((length, columns), BF16),
            pltpu.VMEM((1, scenarios), jnp.int32),
            pltpu.VMEM((1, scenarios), jnp.int32),
            pltpu.VMEM((rows, columns), BF16),
            dma((13 + CHUNKS,)),
        ],
    )(
        in_hbm(weights),
        in_hbm(section_three),
        in_hbm(w_row),
        in_hbm(section_three.reshape(1, scenarios)),
        in_hbm(prev_first),
        costs,
        duals,
        matrix,
    )

    y_prev, joined = lax.optimization_barrier((y_prev, (eta_mean, eta_duals)))
    level_row = jnp.concatenate((joined[1], joined[0])).reshape(1, scenarios + 1)
    core_prev, diag_prev = partner((prev, y_prev), 1)
    pieces = (prev, core_prev, y_prev, diag_prev)

    sol3, cost, keep, send = call(
        third_kernel,
        30,
        in_specs=[SMEM] + [VMEM] * 10,
        out_specs=[VMEM] * 4,
        out_shape=[
            pltpu.VMEM(block, F32),
            pltpu.VMEM((scenarios, length, LANES), F32),
            pltpu.VMEM((HALF, length, columns), F32),
            pltpu.VMEM((HALF + 1, length, columns), BF16),
        ],
        scratch_shapes=[pltpu.VMEM((rows, columns), BF16), pltpu.VMEM((BRANCH, length, columns), BF16)],
    )(sec, *pieces, c3, y3, inv_v, pick, cost, a1)

    chip_got = partner(send, 1)
    half_block = (scenarios, length, columns // 2)
    target2, left, a2, cost = call(
        left_kernel,
        30,
        in_specs=[SMEM] + [VMEM] * 8,
        out_specs=[VMEM] * 4,
        out_shape=[
            pltpu.VMEM((rows, columns), BF16),
            pltpu.VMEM(half_block, F32),
            pltpu.VMEM((length, columns // 2), F32),
            pltpu.VMEM((scenarios, length, LANES), F32),
        ],
        scratch_shapes=[pltpu.VMEM((length, columns), BF16)],
    )(w, *pieces, c2, y2, inv_v, cost)
    cut = HALF // 2
    chip_total, chip_send1, chip_send2 = call(
        chip_sum_kernel,
        8,
        in_specs=[VMEM] * 3,
        out_specs=[VMEM] * 3,
        out_shape=[
            pltpu.VMEM((HALF, length, columns), F32),
            pltpu.VMEM((cut + 1, length, columns), BF16),
            pltpu.VMEM((HALF - cut, length, columns), BF16),
        ],
    )(keep, send, chip_got)
    node_got1 = partner(chip_send1, 2)

    right, eta, sums = call(
        right_kernel,
        30,
        in_specs=[SMEM] + [VMEM] * 8,
        out_specs=[VMEM] * 3,
        out_shape=[
            pltpu.VMEM(half_block, F32),
            pltpu.VMEM((1, scenarios), F32),
            pltpu.VMEM((length, 2 * columns + 3 * LANES), BF16),
        ],
        scratch_shapes=[pltpu.VMEM((scenarios, length, LANES), F32)],
    )(w, w_row, level_row, target2, c2, inv_v, cost, a2, mass)

    core_sums = partner(sums, 1)
    scal_chip, a2 = call(
        core_sum_kernel,
        8,
        in_specs=[VMEM] * 2,
        out_specs=[VMEM] * 2,
        out_shape=[pltpu.VMEM((length, 3 * LANES), BF16), pltpu.VMEM((length, columns), F32)],
    )(sums, core_sums)
    y_scal = partner(scal_chip, 2)
    node_got2 = partner(chip_send2, 2)
    a2_got = partner(a2, 2)
    far_shape = pltpu.VMEM((length, columns + 3 * LANES), BF16)
    far, scal = call(
        node_sum_kernel,
        8,
        in_specs=[VMEM] * 4,
        out_specs=[VMEM] * 2,
        out_shape=[far_shape, pltpu.VMEM((length, LANES), F32)],
    )(scal_chip, y_scal, chip_send1, node_got1)
    far_got = partner(far, 4)
    mask = 8
    while mask < nodes:
        far = call(far_sum_kernel, 8, in_specs=[VMEM] * 2, out_specs=VMEM, out_shape=far_shape)(far, far_got)
        far_got = partner(far, mask)
        mask *= 2

    buf = pltpu.VMEM(block, BF16)
    duals_shape = shape(hour_duals.shape, BF16)
    avg = call(
        third_avg_kernel, 8, in_specs=[VMEM] * 4, out_specs=VMEM, out_shape=pltpu.VMEM((HALF, length, columns), F32)
    )(chip_total, node_got1, node_got2, scal)
    avg_got = partner(avg, 1)
    base1, out, second_avg, third_avg = call(
        later_duals_kernel,
        12,
        in_specs=[SMEM] + [VMEM] * 12,
        out_specs=[VMEM] + [HBM] * 3,
        out_shape=[
            pltpu.VMEM(block, F32),
            duals_shape,
            shape((1, length, columns // 4), F32),
            shape((SHARES, length, columns), F32),
        ],
        scratch_shapes=[
            buf,
            buf,
            pltpu.VMEM((length, columns), F32),
            pltpu.VMEM((BRANCH, length, columns), F32),
            dma((4,)),
            dma((4,)),
            dma((2,)),
        ],
    )(sec, left, right, y2, a2, a2_got, scal, sol3, y3, avg, avg_got, sol1, y1)
    out, first_avg, eta_avg, eta_duals_new = call(
        last_kernel,
        8,
        in_specs=[VMEM] * 5 + [HBM],
        out_specs=[HBM] * 4,
        out_shape=[
            duals_shape,
            shape((length, columns), F32),
            shape((1,), F32),
            shape((1, scenarios), F32),
        ],
        scratch_shapes=[
            buf,
            pltpu.VMEM((length, columns), F32),
            pltpu.VMEM((1, scenarios), F32),
            pltpu.SMEM((1,), F32),
            dma((4,)),
            dma((3,)),
        ],
        input_output_aliases={5: 0},
    )(base1, far, far_got, eta, duals_row, out)
    return out, first_avg, second_avg, third_avg, eta_avg, eta_duals_new.reshape(scenarios)


def solution(mesh):
    row = P(("groups", "node"))
    in_specs = (row, row, P(), row, row, P("groups"), row, row, P("groups"), row)
    out_specs = (row, P("groups"), row, row, P("groups"), row)
    return jax.shard_map(step, mesh=mesh, in_specs=in_specs, out_specs=out_specs, check_vma=False)
```
